128 devices in a mesh: rad: 8 (over y_hi, z), ang: 16 (over x, y_lo, core).
Axes of the slice: x: 4, y: 4 (y_hi: 2, y_lo: 2; y = y_hi * 2 + y_lo), z: 4, core: 2. Of those that a mesh axis runs over, the one named last changes fastest.
Arguments:
- coarse_field: float32 [2, 8, 64, 128], P(None, 'rad', 'ang'), may hold values from -6 to 6
- excite_mid: float32 [2, 8, 8, 64, 128], P(None, None, 'rad', 'ang'), may hold values from -6 to 6
- excite_fine: float32 [2, 8, 16, 128, 256], P(None, None, 'rad', 'ang'), may hold values from -6 to 6
- kernels_mid: float32 [16, 8, 27], replicated, may hold values from -0.875 to 0.875
- noise_mid: float32 [16, 8, 8], replicated, may hold values from -1 to 1
- rows_mid: int32 [8], replicated, may hold values from 0 to 15
- kernels_fine: float32 [16, 8, 27], replicated, may hold values from -0.875 to 0.875
- noise_fine: float32 [16, 8, 8], replicated, may hold values from -1 to 1
- rows_fine: int32 [16], replicated, may hold values from 0 to 15
- emission: float32 [32, 256, 512], P('rad', 'ang'), may hold values from 0.3 to 3
- star_bins: int32 [4, 256, 512], P(None, 'ang'), may hold values from 0 to 31
- star_data: float32 [4, 256, 512], P(None, 'ang'), may hold values from -3 to 3
Outputs:
- grad_coarse: float32 [2, 8, 64, 128], P(None, 'rad', 'ang')
- grad_excite_mid: float32 [2, 8, 8, 64, 128], P(None, None, 'rad', 'ang')
- grad_excite_fine: float32 [2, 8, 16, 128, 256], P(None, None, 'rad', 'ang')
- residual: float32 [2, 4, 256, 512], P(None, None, 'ang')
The draws below stay inside these ranges and needn't reach their ends.
All inputs are finite; a program needn't handle non-finite values.
Results may differ from the reference program's by a relative error of at most 0.0003.
Values sent between devices are 32-bit elements; how exact they have to be, the bound alone decides.
A program may use at most 192 MiB of HBM per device.

```python
import math
import jax
import jax.numpy as jnp
from jax import lax

NB0 = 128
NK = 16
NSTAR = 4
SAMPLES = 2
NR0 = 8
NA0 = 64
NR1 = 16
NA1 = 128
NB1 = 256
NRF = 32
NAF = 256
NBF = 512


def with_ends(drawn, stream_key, least, largest):
    index_at = [jax.random.randint(jax.random.fold_in(stream_key, axis), (), 0, length) for axis, length in enumerate(drawn.shape)]
    longest = drawn.shape.index(max(drawn.shape))
    next_to = index_at[:longest] + [(index_at[longest] + 1) % drawn.shape[longest]] + index_at[longest + 1:]
    return drawn.at[tuple(index_at)].set(least).at[tuple(next_to)].set(largest)


def steps_of(stream_key, dims, cuts, smallest, largest):
    level = 1.0
    for axis_at, shards_of in cuts:
        steps = jax.random.uniform(jax.random.fold_in(jax.random.fold_in(stream_key, 6), axis_at), (shards_of,), jnp.float32, smallest / len(cuts), largest / len(cuts))
        level = level * jnp.repeat(jnp.exp(steps), dims[axis_at] // shards_of).reshape((-1,) + (1,) * (len(dims) - 1 - axis_at))
    return level


def centred(rng, shape, deviation, bound, split=(), kind=jnp.bfloat16):
    result = jax.random.normal(rng, shape, jnp.float32) * deviation
    if len(split) > 0:
        result = steps_of(rng, shape, split, -0.22, 0.18) * result
    return jnp.clip(result, min=-bound, max=bound).astype(kind)


def setup_inputs(seed: int = 0) -> dict:
    keys = jax.random.split(jax.random.key(seed), 13)
    coarse_field = centred(keys[0], (SAMPLES, NR0, NA0, NB0), 1.0, 6.0, ((1, 8), (2, 16)), jnp.float32)
    excite_mid = centred(keys[1], (SAMPLES, 8, NR0, NA0, NB0), 1.0, 6.0, ((2, 8), (3, 16)), jnp.float32)
    excite_fine = centred(keys[2], (SAMPLES, 8, NR1, NA1, NB1), 1.0, 6.0, ((2, 8), (3, 16)), jnp.float32)
    kernels_mid = centred(keys[3], (NK, 8, 27), 54 ** -0.5, 0.875, (), jnp.float32)
    noise_mid = centred(keys[4], (NK, 8, 8), 32 ** -0.5, 1.0, (), jnp.float32)
    rows_mid = with_ends(jax.random.randint(keys[5], (NR0,), 0, NK), jax.random.fold_in(keys[5], 1), 0, NK - 1).astype(jnp.int32)
    kernels_fine = centred(keys[6], (NK, 8, 27), 54 ** -0.5, 0.875, (), jnp.float32)
    noise_fine = centred(keys[7], (NK, 8, 8), 32 ** -0.5, 1.0, (), jnp.float32)
    rows_fine = with_ends(jax.random.randint(keys[8], (NR1,), 0, NK), jax.random.fold_in(keys[8], 1), 0, NK - 1).astype(jnp.int32)
    emission = jnp.clip(jnp.exp(math.log(3.0) - 2.3025851 * jax.random.uniform(keys[9], (NRF, NAF, NBF), jnp.float32) ** steps_of(keys[9], (NRF, NAF, NBF), ((0, 8), (1, 16)), -0.2, 0.2)), 0.3, 3.0)
    star_bins = with_ends(jax.random.randint(keys[10], (NSTAR, NAF, NBF), 0, NRF), jax.random.fold_in(keys[10], 1), 0, NRF - 1).astype(jnp.int32)
    star_data = centred(keys[11], (NSTAR, NAF, NBF), 0.5, 3.0, ((1, 16),), jnp.float32)
    return dict(coarse_field=coarse_field, excite_mid=excite_mid, excite_fine=excite_fine, kernels_mid=kernels_mid, noise_mid=noise_mid, rows_mid=rows_mid, kernels_fine=kernels_fine, noise_fine=noise_fine, rows_fine=rows_fine, emission=emission, star_bins=star_bins, star_data=star_data)


HIGH = lax.Precision.HIGHEST


def alternate(children):
    count_s, _, count_r, count_a, count_b = children.shape
    folded = children.reshape(count_s, 2, 2, 2, count_r, count_a, count_b)
    folded = folded.transpose(0, 4, 1, 5, 2, 6, 3)
    return folded.reshape(count_s, 2 * count_r, 2 * count_a, 2 * count_b)


def split_children(fine_grid):
    count_s, twice_r, twice_a, twice_b = fine_grid.shape
    folded = fine_grid.reshape(count_s, twice_r // 2, 2, twice_a // 2, 2, twice_b // 2, 2)
    folded = folded.transpose(0, 2, 4, 6, 1, 3, 5)
    return folded.reshape(count_s, 8, twice_r // 2, twice_a // 2, twice_b // 2)


def refine(parent, excite, kernels, noise_table, table_rows):
    count_s, count_r, count_a, count_b = parent.shape
    kernel_rows = kernels[table_rows]
    noise_rows = noise_table[table_rows]
    padded = jnp.pad(parent, ((0, 0), (1, 1), (1, 1), (1, 1)))
    children = jnp.einsum('rcj,sjrab->scrab', noise_rows, excite, precision=HIGH)
    for step_r in range(3):
        for step_a in range(3):
            for step_b in range(3):
                slot = 9 * step_r + 3 * step_a + step_b
                piece = padded[:, step_r:step_r + count_r, step_a:step_a + count_a, step_b:step_b + count_b]
                children = children + jnp.einsum('rc,srab->scrab', kernel_rows[:, :, slot], piece, precision=HIGH)
    return alternate(children)


def coarseward(gradient, kernels, noise_table, table_rows):
    child_grad = split_children(gradient)
    count_s, _, count_r, count_a, count_b = child_grad.shape
    kernel_rows = kernels[table_rows]
    noise_rows = noise_table[table_rows]
    grad_excite = jnp.einsum('rcj,scrab->sjrab', noise_rows, child_grad, precision=HIGH)
    spread = jnp.zeros((count_s, count_r + 2, count_a + 2, count_b + 2), jnp.float32)
    for step_r in range(3):
        for step_a in range(3):
            for step_b in range(3):
                slot = 9 * step_r + 3 * step_a + step_b
                weighted = jnp.einsum('rc,scrab->srab', kernel_rows[:, :, slot], child_grad, precision=HIGH)
                spread = spread.at[:, step_r:step_r + count_r, step_a:step_a + count_a, step_b:step_b + count_b].add(weighted)
    return spread[:, 1:-1, 1:-1, 1:-1], grad_excite


def reference(coarse_field, excite_mid, excite_fine, kernels_mid, noise_mid, rows_mid, kernels_fine, noise_fine, rows_fine, emission, star_bins, star_data):
    middle = refine(coarse_field, excite_mid, kernels_mid, noise_mid, rows_mid)
    fine_field = refine(middle, excite_fine, kernels_fine, noise_fine, rows_fine)
    density = jnp.exp(fine_field)
    spacing = 1.0 / NRF
    layer = spacing * density
    depth = jnp.cumsum(layer, axis=1)
    transmission = jnp.exp(-(depth - layer))
    column = jnp.cumsum(spacing * emission[None] * transmission, axis=1)
    indices = jnp.broadcast_to(star_bins[None], (SAMPLES, NSTAR, NAF, NBF)).astype(jnp.int32)
    predicted = jnp.take_along_axis(column, indices, axis=1)
    residual = star_data[None] - predicted
    row_ids = jnp.arange(NRF, dtype=jnp.int32)[:, None, None]
    weight = jnp.zeros(fine_field.shape, jnp.float32)
    for star in range(NSTAR):
        below = (row_ids < star_bins[star][None])[None]
        term = residual[:, star][:, None] * (predicted[:, star][:, None] - column)
        weight = weight + jnp.where(below, term, jnp.float32(0.0))
    grad_field = -density * weight
    grad_middle, grad_excite_fine = coarseward(grad_field, kernels_fine, noise_fine, rows_fine)
    grad_coarse, grad_excite_mid = coarseward(grad_middle, kernels_mid, noise_mid, rows_mid)
    return grad_coarse, grad_excite_mid, grad_excite_fine, residual
```

```python
import jax
import jax.numpy as jnp
from jax import lax
from jax.experimental import pallas as pl
from jax.experimental.pallas import tpu as pltpu
from jax.sharding import PartitionSpec as P

F32 = jnp.float32
BF16 = jnp.bfloat16
MESH = pl.DeviceIdType.MESH
ANY = pl.BlockSpec(memory_space=pl.ANY)
SMEM = pl.BlockSpec(memory_space=pltpu.SMEM)

RING2 = [(di, dk) for di in range(-2, 3) for dk in (-1, 0, 1) if (di, dk) != (0, 0)]
MROWS = [(-1, 1), (0, 0), (0, 1), (1, 0)]


def slot_of(di, dk):
    return (di + 2) * 3 + dk + 1


def lane_shift(x, step):
    if step == 1:
        return x
    width = x.shape[1]
    lane = lax.broadcasted_iota(jnp.int32, x.shape, 1)
    if step == 0:
        return jnp.where(lane == 0, F32(0.0), pltpu.roll(x, 1, 1))
    return jnp.where(lane == width - 1, F32(0.0), pltpu.roll(x, width - 1, 1))


def permuted(x, permutation):
    high = x.astype(BF16)
    rest = x - high.astype(F32)
    mid = rest.astype(BF16)
    low = (rest - mid.astype(F32)).astype(BF16)

    def times(part):
        return jnp.dot(part, permutation, preferred_element_type=F32)

    return times(high) + times(mid) + times(low)


SCRATCH = dict(
    slots=pltpu.VMEM((15, 2, 4, 128), F32),
    exm_v=pltpu.VMEM((2, 8, 4, 128), F32),
    exf_v=pltpu.VMEM((2, 8, 2, 8, 256), F32),
    em_v=pltpu.VMEM((4, 64, 128), F32),
    bins_v=pltpu.VMEM((4, 64, 128), jnp.int32),
    data_v=pltpu.VMEM((4, 64, 128), F32),
    spread_m=pltpu.VMEM((256, 256), BF16),
    gather_m=pltpu.VMEM((256, 256), BF16),
    ne=pltpu.VMEM((4, 4, 2, 4, 128), F32),
    ne_edge=pltpu.VMEM((2, 2, 4, 128), F32),
    ne_side=pltpu.VMEM((2, 4, 4, 128), F32),
    nex=pltpu.VMEM((4, 4, 16, 128), F32),
    ce=pltpu.VMEM((5, 2, 8, 128), F32),
    cs=pltpu.VMEM((5, 9, 16, 128), F32),
    xi=pltpu.VMEM((4, 2, 16, 256), F32),
    f16=pltpu.VMEM((2, 4, 2, 16, 128), F32),
    fs=pltpu.VMEM((4, 9, 16, 256), F32),
    esend=pltpu.VMEM((256, 128), F32),
    erecv=pltpu.VMEM((256, 128), F32),
    dsend=pltpu.VMEM((512, 128), F32),
    drecv=pltpu.VMEM((512, 128), F32),
    gsend=pltpu.VMEM((512, 128), F32),
    grecv=pltpu.VMEM((512, 128), F32),
    colv=pltpu.VMEM((512, 128), F32),
    star_x=pltpu.VMEM((2, 8, 8, 512), F32),
    star_y=pltpu.VMEM((2, 4, 8, 128), F32),
    star_z=pltpu.VMEM((2, 2, 32, 128), F32),
    res_x=pltpu.VMEM((2, 32, 128), F32),
    rsend=pltpu.VMEM((64, 128), F32),
    rrecv=pltpu.VMEM((512, 128), F32),
    res_v=pltpu.VMEM((4, 128, 128), F32),
    gf_v=pltpu.VMEM((2, 8, 2, 8, 256), F32),
    ws=pltpu.VMEM((4, 9, 16, 256), F32),
    g16=pltpu.VMEM((2, 4, 2, 16, 128), F32),
    hh=pltpu.VMEM((4, 2, 16, 256), F32),
    h_edge=pltpu.VMEM((2, 4, 4, 128), F32),
    h_rad=pltpu.VMEM((2, 2, 16, 256), F32),
    h_side=pltpu.VMEM((2, 4, 4, 128), F32),
    wq=pltpu.VMEM((5, 9, 16, 128), F32),
    gcx=pltpu.VMEM((5, 16, 128), F32),
    gslots=pltpu.VMEM((15, 16, 128), F32),
    gm_v=pltpu.VMEM((2, 8, 4, 128), F32),
    gc_v=pltpu.VMEM((2, 4, 128), F32),
    local_sem=pltpu.SemaphoreType.DMA((16,)),
    self_sem=pltpu.SemaphoreType.DMA((8,)),
    out_sem=pltpu.SemaphoreType.DMA((8,)),
    cs_send=pltpu.SemaphoreType.DMA((15,)),
    cs_recv=pltpu.SemaphoreType.DMA((15,)),
    ne_send=pltpu.SemaphoreType.DMA((8,)),
    ne_recv=pltpu.SemaphoreType.DMA((8,)),
    e_send=pltpu.SemaphoreType.DMA((8,)),
    e_recv=pltpu.SemaphoreType.DMA((8,)),
    d_send=pltpu.SemaphoreType.DMA((8,)),
    d_recv=pltpu.SemaphoreType.DMA((8,)),
    g_send=pltpu.SemaphoreType.DMA((8,)),
    g_recv=pltpu.SemaphoreType.DMA((8,)),
    r_send=pltpu.SemaphoreType.DMA((8,)),
    r_recv=pltpu.SemaphoreType.DMA((8,)),
    h_send=pltpu.SemaphoreType.DMA((8,)),
    h_recv=pltpu.SemaphoreType.DMA((8,)),
    q_send=pltpu.SemaphoreType.DMA((15,)),
    q_recv=pltpu.SemaphoreType.DMA((15,)),
)
INPUTS = ["cf", "exm", "exf", "km", "nm", "rm", "kf", "nf", "rf", "emi", "bins", "data"]
OUTPUTS = ["gc_o", "gm_o", "gf_o", "res_o"]


class Refs:
    def __init__(self, refs):
        for name, ref in zip(INPUTS + OUTPUTS + list(SCRATCH), refs):
            setattr(self, name, ref)


def kernel(nr, na, *refs):
    v = Refs(refs)
    i = lax.axis_index("rad")
    k = lax.axis_index("ang")
    coarse_a = 4 * na

    def row_at(di):
        return lax.rem(i + (di + nr), nr)

    def block_at(dk):
        return lax.rem(k + (dk + na), na)

    def remote(src, dst, send, recv, di, dk):
        return pltpu.make_async_remote_copy(
            src_ref=src,
            dst_ref=dst,
            send_sem=send,
            recv_sem=recv,
            device_id=(row_at(di), block_at(dk)),
            device_id_type=MESH,
        )

    def part(ref, index, size):
        return ref.at[pl.ds(pl.multiple_of(index * size, size), size)]

    peers = [(d, 0) for d in range(1, nr)] + [(di, dk) for di, dk in RING2 if dk != 0]
    barrier = pltpu.get_barrier_semaphore()
    for di, dk in peers:
        pl.semaphore_signal(
            barrier, inc=1, device_id=(row_at(di), block_at(dk)), device_id_type=MESH
        )

    loads = [
        pltpu.make_async_copy(v.exm.at[:, :, 0], v.exm_v, v.local_sem.at[0]),
        pltpu.make_async_copy(v.cf.at[:, 0], v.slots.at[slot_of(0, 0)], v.local_sem.at[1]),
    ]
    for c in range(4):
        lanes = pl.ds(128 * c, 128)
        for t, (src, dst) in enumerate(
            ((v.emi, v.em_v), (v.bins, v.bins_v), (v.data, v.data_v))
        ):
            loads.append(
                pltpu.make_async_copy(
                    src.at[:, :, lanes],
                    dst.at[c].reshape(4, 16, 128),
                    v.local_sem.at[2 + 4 * t + c],
                )
            )
    loads.append(pltpu.make_async_copy(v.exf, v.exf_v, v.local_sem.at[14]))
    for load in loads:
        load.start()

    row = lax.broadcasted_iota(jnp.int32, (256, 256), 0)
    col = lax.broadcasted_iota(jnp.int32, (256, 256), 1)
    one, none = F32(1.0), F32(0.0)
    v.gather_m[...] = jnp.where(
        row == 2 * lax.bitwise_and(col, 127) + lax.shift_right_logical(col, 7), one, none
    ).astype(BF16)
    v.spread_m[...] = jnp.where(
        col == 2 * lax.bitwise_and(row, 127) + lax.shift_right_logical(row, 7), one, none
    ).astype(BF16)

    loads[0].wait()
    mid_row = v.rm[i]
    for cr in range(2):
        for q in range(4):
            for s in range(2):
                total = v.nm[mid_row, 4 * cr + q, 0] * v.exm_v[s, 0]
                for j in range(1, 8):
                    total = total + v.nm[mid_row, 4 * cr + q, j] * v.exm_v[s, j]
                v.ne[1 + cr, q, s] = total
                ca, cb = q // 2, q % 2
                if ca == 1:
                    v.ne_edge[0, cr, pl.ds(2 * cb + s, 1)] = total[3:4]
                else:
                    v.ne_edge[1, cr, pl.ds(2 * cb + s, 1)] = total[0:1]
    loads[1].wait()

    pl.semaphore_wait(barrier, len(peers))

    halo = [
        remote(
            v.cf.at[:, 0],
            v.slots.at[slot_of(-di, -dk)],
            v.cs_send.at[slot_of(di, dk)],
            v.cs_recv.at[slot_of(-di, -dk)],
            di,
            dk,
        )
        for di, dk in RING2
    ]
    moves = [(v.ne.at[1], v.ne.at[3], -1, 0), (v.ne.at[2], v.ne.at[0], 1, 0)]
    for side, dk in ((0, 1), (1, -1)):
        moves += [
            (v.ne_edge.at[side], v.ne_side.at[side, 1:3], 0, dk),
            (v.ne_edge.at[side, 0], v.ne_side.at[side, 3], -1, dk),
            (v.ne_edge.at[side, 1], v.ne_side.at[side, 0], 1, dk),
        ]
    halo += [
        remote(src, dst, v.ne_send.at[n], v.ne_recv.at[n], di, dk)
        for n, (src, dst, di, dk) in enumerate(moves)
    ]
    for copy in halo:
        copy.start()

    for c in range(12):
        loads[2 + c].wait()
    pieces = [
        jnp.concatenate(
            [v.em_v[2 * h + e, pl.ds(16 * rl + ca, 8, stride=2), :] for e in range(2)], axis=1
        )
        for rl in range(4)
        for ca in range(2)
        for h in range(2)
    ]
    pieces = permuted(jnp.concatenate(pieces, axis=0), v.gather_m[...])
    for rl in range(4):
        for ca in range(2):
            for h in range(2):
                n = (rl * 2 + ca) * 2 + h
                for cb in range(2):
                    at = h * 16 + rl * 4 + ca * 2 + cb
                    v.esend[pl.ds(at, 8, stride=32), :] = pieces[
                        8 * n : 8 * n + 8, 128 * cb : 128 * cb + 128
                    ]

    def scatter(src, dst, send, recv, size):
        return [
            remote(part(src, row_at(d), size), part(dst, i, size), send.at[d], recv.at[d], d, 0)
            for d in range(1, nr)
        ]

    def keep_own(src, dst, size, sem):
        return pltpu.make_async_copy(part(src, i, size), part(dst, i, size), sem)

    sends_e = scatter(v.esend, v.erecv, v.e_send, v.e_recv, 32)
    own_e = keep_own(v.esend, v.erecv, 32, v.self_sem.at[0])
    own_e.start()
    for copy in sends_e:
        copy.start()

    for n in range(4):
        for ca in range(2):
            for c in range(4):
                at = pl.ds(16 * n + ca, 8, stride=2)
                lanes = pl.ds(128 * c, 128)
                v.star_x[0, :, 2 * n + ca, lanes] = v.bins_v[c, at, :].astype(F32)
                v.star_x[1, :, 2 * n + ca, lanes] = v.data_v[c, at, :]
    for kind in range(2):
        x = v.star_x[kind, i]
        y = permuted(jnp.concatenate([x[:, :256], x[:, 256:]], axis=0), v.gather_m[...])
        for h in range(2):
            for cb in range(2):
                v.star_y[kind, 2 * h + cb] = y[8 * h : 8 * h + 8, 128 * cb : 128 * cb + 128]
        for h in range(2):
            for cb in range(2):
                for ca in range(2):
                    rows = v.star_y[kind, 2 * h + cb, pl.ds(ca, 4, stride=2), :]
                    for s in range(2):
                        v.star_z[kind, h, pl.ds(4 * s + 2 * ca + cb, 4, stride=8), :] = rows

    for copy in halo:
        copy.wait()

    sub8 = lax.broadcasted_iota(jnp.int32, (8, 128), 0)
    sub16 = lax.bitwise_and(lax.broadcasted_iota(jnp.int32, (16, 128), 0), 7)

    def inside(local_a, di):
        there = jnp.where((i + di >= 0) & (i + di < nr), coarse_a, 0)
        a = 4 * k + local_a
        return (a >= 0) & (a < there)

    for q in range(5):
        for s in range(2):
            v.ce[q, s, 2:6] = v.slots[slot_of(q - 2, 0), s]
            v.ce[q, s, 0:2] = v.slots[slot_of(q - 2, -1), s, 2:4]
            v.ce[q, s, 6:8] = v.slots[slot_of(q - 2, 1), s, 0:2]
        here = inside(sub8 - 2, q - 2)
        both = [jnp.where(here, v.ce[q, s], none) for s in range(2)]
        for da in range(3):
            if da == 1:
                moved = both
            else:
                moved = [pltpu.roll(x, 1 if da == 0 else 7, 0) for x in both]
            moved = jnp.concatenate(moved, axis=0)
            for db in range(3):
                v.cs[q, 3 * da + db] = lane_shift(moved, db)

    for m in range(4):
        for q in range(4):
            for s in range(2):
                v.nex[m, q, 8 * s + 2 : 8 * s + 6] = v.ne[m, q, s]
                ca, cb = q // 2, q % 2
                if ca == 1:
                    v.nex[m, q, 8 * s + 1 : 8 * s + 2] = v.ne_side[0, m, pl.ds(2 * cb + s, 1)]
                else:
                    v.nex[m, q, 8 * s + 6 : 8 * s + 7] = v.ne_side[1, m, pl.ds(2 * cb + s, 1)]

    table_row = {}
    for di in (-1, 0, 1):
        table_row[di] = v.rm[jnp.clip(i + di, 0, nr - 1)]
    for m, (di, cr) in enumerate(MROWS):
        sums = [v.nex[m, q] for q in range(4)]
        for o in range(27):
            x = v.cs[di + 1 + o // 9, o % 9]
            for q in range(4):
                sums[q] = sums[q] + v.km[table_row[di], 4 * cr + q, o] * x
        used = inside(sub16 - 2, di) & (sub16 >= 1) & (sub16 <= 6)
        for q in range(4):
            lanes = slice(128 * (q % 2), 128 * (q % 2) + 128)
            v.xi[m, q // 2, :, lanes] = jnp.where(used, sums[q], none)
    spread = permuted(v.xi[...].reshape(128, 256), v.spread_m[...])
    for m in range(4):
        for ca in range(2):
            for s in range(2):
                n = (m * 2 + ca) * 16 + 8 * s
                for h in range(2):
                    v.f16[h, m, s, pl.ds(ca, 8, stride=2), :] = spread[
                        n : n + 8, 128 * h : 128 * h + 128
                    ]
    for m in range(4):
        for da in range(3):
            rows = slice(3 + da, 11 + da)
            x = jnp.concatenate(
                [
                    jnp.concatenate([v.f16[h, m, s, rows, :] for h in range(2)], axis=1)
                    for s in range(2)
                ],
                axis=0,
            )
            for db in range(3):
                v.fs[m, 3 * da + db] = lane_shift(x, db)

    loads[14].wait()
    fine_row = [v.rf[2 * i + r] for r in range(2)]
    for r in range(2):
        for half in range(2):
            sums = [None] * 4
            for j in range(8):
                x = jnp.concatenate([v.exf_v[s, j, r] for s in range(2)], axis=0)
                for q in range(4):
                    term = v.nf[fine_row[r], 4 * half + q, j] * x
                    sums[q] = term if j == 0 else sums[q] + term
            for o in range(27):
                x = v.fs[r + o // 9, o % 9]
                for q in range(4):
                    sums[q] = sums[q] + v.kf[fine_row[r], 4 * half + q, o] * x
            for q in range(4):
                density = jnp.exp(sums[q])
                for s in range(2):
                    for h in range(2):
                        at = h * 32 + (2 * r + half) * 8 + 4 * s + q
                        v.dsend[pl.ds(at, 8, stride=64), :] = density[
                            8 * s : 8 * s + 8, 128 * h : 128 * h + 128
                        ]
    sends_d = scatter(v.dsend, v.drecv, v.d_send, v.d_recv, 64)
    own_d = keep_own(v.dsend, v.drecv, 64, v.self_sem.at[1])
    for copy in sends_d:
        copy.start()
    own_d.start()

    for copy in sends_e:
        copy.wait()
    own_e.wait()
    for copy in sends_d:
        copy.wait()
    own_d.wait()

    spacing = F32(1.0 / (4 * nr))
    cells = 4 * nr
    for h in range(2):
        bins = [v.star_z[0, h, 8 * n : 8 * n + 8] for n in range(4)]
        seen = [v.star_z[1, h, 8 * n : 8 * n + 8] for n in range(4)]
        depth = jnp.zeros((8, 128), F32)
        column = jnp.zeros((8, 128), F32)
        picked = [jnp.zeros((8, 128), F32) for _ in range(4)]
        for cell in range(cells):
            at = (cell // 4) * 64 + h * 32 + (cell % 4) * 8
            ea = (cell // 4) * 32 + h * 16 + (cell % 4) * 4
            light = v.erecv[ea : ea + 4]
            light = jnp.concatenate([light, light], axis=0)
            column = column + spacing * light * jnp.exp(-depth)
            depth = depth + spacing * v.drecv[at : at + 8]
            v.colv[at : at + 8] = column
            for n in range(4):
                picked[n] = jnp.where(bins[n] == F32(cell), column, picked[n])
        left = [seen[n] - picked[n] for n in range(4)]
        for n in range(4):
            v.res_x[h, 8 * n : 8 * n + 8] = left[n]
        for cell in range(cells):
            at = (cell // 4) * 64 + h * 32 + (cell % 4) * 8
            column = v.colv[at : at + 8]
            weight = None
            for n in range(4):
                term = jnp.where(
                    bins[n] > F32(cell), left[n] * (picked[n] - column), F32(0.0)
                )
                weight = term if n == 0 else weight + term
            v.gsend[at : at + 8] = -v.drecv[at : at + 8] * weight
    sends_g = scatter(v.gsend, v.grecv, v.g_send, v.g_recv, 64)
    own_g = keep_own(v.gsend, v.grecv, 64, v.self_sem.at[2])
    for copy in sends_g:
        copy.start()
    own_g.start()

    pieces = [
        jnp.concatenate([v.res_x[h, pl.ds(cb, 16, stride=2), :] for cb in range(2)], axis=1)
        for h in range(2)
    ]
    spread = permuted(jnp.concatenate(pieces, axis=0), v.spread_m[...])
    for h in range(2):
        for e in range(2):
            c = 2 * h + e
            v.rsend[16 * c : 16 * c + 16] = spread[
                16 * h : 16 * h + 16, 128 * e : 128 * e + 128
            ]
    sends_r = [
        remote(v.rsend, part(v.rrecv, i, 64), v.r_send.at[d], v.r_recv.at[d], d, 0)
        for d in range(1, nr)
    ]
    own_r = pltpu.make_async_copy(v.rsend, part(v.rrecv, i, 64), v.self_sem.at[3])
    for copy in sends_r:
        copy.start()
    own_r.start()

    for copy in sends_g:
        copy.wait()
    own_g.wait()

    for r in range(2):
        grads = []
        for c in range(8):
            cr, q = c // 4, c % 4
            at = [[h * 32 + (2 * r + cr) * 8 + 4 * s + q for h in range(2)] for s in range(2)]
            grads.append(
                jnp.concatenate(
                    [
                        jnp.concatenate(
                            [v.grecv[pl.ds(at[s][h], 8, stride=64), :] for h in range(2)], axis=1
                        )
                        for s in range(2)
                    ],
                    axis=0,
                )
            )
        for j in range(8):
            total = v.nf[fine_row[r], 0, j] * grads[0]
            for c in range(1, 8):
                total = total + v.nf[fine_row[r], c, j] * grads[c]
            for s in range(2):
                v.gf_v[s, j, r] = total[8 * s : 8 * s + 8]
        for o in range(27):
            total = v.kf[fine_row[r], 0, o] * grads[0]
            for c in range(1, 8):
                total = total + v.kf[fine_row[r], c, o] * grads[c]
            m = r + o // 9
            if r == 1 and m < 3:
                total = total + v.ws[m, o % 9]
            v.ws[m, o % 9] = total
    out_gf = pltpu.make_async_copy(v.gf_v, v.gf_o, v.out_sem.at[0])
    out_gf.start()

    v.g16[...] = jnp.zeros(v.g16.shape, F32)
    for m in range(4):
        for da in range(3):
            total = lane_shift(v.ws[m, 3 * da + 1], 1)
            total = total + lane_shift(v.ws[m, 3 * da], 2)
            total = total + lane_shift(v.ws[m, 3 * da + 2], 0)
            rows = slice(3 + da, 11 + da)
            for h in range(2):
                for s in range(2):
                    v.g16[h, m, s, rows, :] = (
                        v.g16[h, m, s, rows, :]
                        + total[8 * s : 8 * s + 8, 128 * h : 128 * h + 128]
                    )
    pieces = []
    for m in range(4):
        here = inside(sub8 - 2, MROWS[m][0])
        for ca in range(2):
            for s in range(2):
                pieces.append(
                    jnp.concatenate(
                        [
                            jnp.where(here, v.g16[h, m, s, pl.ds(ca, 8, stride=2), :], none)
                            for h in range(2)
                        ],
                        axis=1,
                    )
                )
    v.hh[...] = permuted(jnp.concatenate(pieces, axis=0), v.gather_m[...]).reshape(4, 2, 16, 256)
    for m in range(4):
        for s in range(2):
            for cb in range(2):
                lanes = slice(128 * cb, 128 * cb + 128)
                v.h_edge[0, m, pl.ds(2 * s + cb, 1)] = v.hh[m, 1, 8 * s + 1 : 8 * s + 2, lanes]
                v.h_edge[1, m, pl.ds(2 * s + cb, 1)] = v.hh[m, 0, 8 * s + 6 : 8 * s + 7, lanes]
    moves = [(v.hh.at[0], v.h_rad.at[1], -1, 0), (v.hh.at[3], v.h_rad.at[0], 1, 0)]
    for side, dk in ((0, -1), (1, 1)):
        moves += [
            (v.h_edge.at[side, 1:3], v.h_side.at[side, 0:2], 0, dk),
            (v.h_edge.at[side, 0], v.h_side.at[side, 3], -1, dk),
            (v.h_edge.at[side, 3], v.h_side.at[side, 2], 1, dk),
        ]
    owed = [
        remote(src, dst, v.h_send.at[n], v.h_recv.at[n], di, dk)
        for n, (src, dst, di, dk) in enumerate(moves)
    ]
    for copy in owed:
        copy.start()

    for di in (-1, 0, 1):
        children = []
        for m, (mdi, cr) in enumerate(MROWS):
            if mdi == di:
                for q in range(4):
                    lanes = slice(128 * (q % 2), 128 * (q % 2) + 128)
                    children.append((4 * cr + q, v.hh[m, q // 2, :, lanes]))
        for o in range(27):
            total = None
            for c, x in children:
                term = v.km[table_row[di], c, o] * x
                total = term if total is None else total + term
            row_q = di + 1 + o // 9
            if di > -1 and row_q < di + 3:
                total = total + v.wq[row_q, o % 9]
            v.wq[row_q, o % 9] = total
    for q in range(5):
        pieces = []
        for da in range(3):
            total = v.wq[q, 3 * da + 1]
            total = total + lane_shift(v.wq[q, 3 * da], 2)
            total = total + lane_shift(v.wq[q, 3 * da + 2], 0)
            pieces.append(total)
        here = inside(sub8 - 2, q - 2)
        for s in range(2):
            rows = slice(8 * s, 8 * s + 8)
            total = pieces[1][rows]
            total = total + pltpu.roll(pieces[0][rows], 7, 0)
            total = total + pltpu.roll(pieces[2][rows], 1, 0)
            v.gcx[q, rows] = jnp.where(here, total, none)
    owed_q = [
        remote(
            v.gcx.at[di + 2],
            v.gslots.at[slot_of(-di, -dk)],
            v.q_send.at[slot_of(di, dk)],
            v.q_recv.at[slot_of(-di, -dk)],
            di,
            dk,
        )
        for di, dk in RING2
    ]
    for copy in owed_q:
        copy.start()

    for copy in sends_r:
        copy.wait()
    own_r.wait()
    for c in range(4):
        for n in range(4):
            for s in range(2):
                for ca in range(2):
                    at = 16 * c + n * 4 + s * 2 + ca
                    v.res_v[c, pl.ds((s * 4 + n) * 16 + ca, 8, stride=2), :] = v.rrecv[
                        pl.ds(at, 8, stride=64), :
                    ]
    outs = [
        pltpu.make_async_copy(
            v.res_v.at[c].reshape(2, 4, 16, 128),
            v.res_o.at[:, :, :, pl.ds(128 * c, 128)],
            v.out_sem.at[1 + c],
        )
        for c in range(4)
    ]
    for out in outs:
        out.start()

    for copy in owed:
        copy.wait()
    for s in range(2):
        grads = []
        for cr in range(2):
            for q in range(4):
                ca, cb = q // 2, q % 2
                lanes = slice(128 * cb, 128 * cb + 128)
                rows = slice(8 * s + 2, 8 * s + 6)
                total = v.hh[1 + cr, ca, rows, lanes] + v.h_rad[cr, ca, rows, lanes]
                side, place = (0, 3) if ca == 1 else (1, 0)
                edge = pl.ds(2 * s + cb, 1)
                extra = v.h_side[side, cr, edge] + v.h_side[side, 2 + cr, edge]
                at = lax.broadcasted_iota(jnp.int32, (4, 128), 0)
                grads.append(
                    total + jnp.where(at == place, jnp.broadcast_to(extra, (4, 128)), none)
                )
        for j in range(8):
            total = v.nm[mid_row, 0, j] * grads[0]
            for c in range(1, 8):
                total = total + v.nm[mid_row, c, j] * grads[c]
            v.gm_v[s, j] = total
    out_gm = pltpu.make_async_copy(v.gm_v, v.gm_o.at[:, :, 0], v.out_sem.at[5])
    out_gm.start()

    for copy in owed_q:
        copy.wait()
    for s in range(2):
        total = v.gcx[2, 8 * s + 2 : 8 * s + 6]
        low = jnp.zeros((2, 128), F32)
        high = jnp.zeros((2, 128), F32)
        for di in range(-2, 3):
            if di != 0:
                total = total + v.gslots[slot_of(di, 0), 8 * s + 2 : 8 * s + 6]
            low = low + v.gslots[slot_of(di, -1), 8 * s + 6 : 8 * s + 8]
            high = high + v.gslots[slot_of(di, 1), 8 * s : 8 * s + 2]
        v.gc_v[s] = total + jnp.concatenate([low, high], axis=0)
    out_gc = pltpu.make_async_copy(v.gc_v, v.gc_o.at[:, 0], v.out_sem.at[6])
    out_gc.start()
    for out in [out_gf, *outs, out_gm, out_gc]:
        out.wait()


def per_device(*args):
    import functools

    nr, na = lax.axis_size("rad"), lax.axis_size("ang")
    shapes = [(2, 1, 4, 128), (2, 8, 1, 4, 128), (2, 8, 2, 8, 256), (2, 4, 16, 512)]
    return pl.pallas_call(
        functools.partial(kernel, nr, na),
        out_shape=[jax.ShapeDtypeStruct(shape, F32) for shape in shapes],
        in_specs=[ANY, ANY, ANY] + [SMEM] * 6 + [ANY] * 3,
        out_specs=[ANY] * 4,
        scratch_shapes=list(SCRATCH.values()),
        compiler_params=pltpu.CompilerParams(collective_id=0, has_side_effects=True),
    )(*args)


def solution(mesh):
    placed = (
        P(None, "rad", "ang", None),
        P(None, None, "rad", "ang", None),
        P(None, None, "rad", "ang", None),
        P(),
        P(),
        P(),
        P(),
        P(),
        P(),
        P("rad", "ang", None),
        P(None, "ang", None),
        P(None, "ang", None),
    )
    return jax.shard_map(
        per_device,
        mesh=mesh,
        in_specs=placed,
        out_specs=(
            P(None, "rad", "ang", None),
            P(None, None, "rad", "ang", None),
            P(None, None, "rad", "ang", None),
            P(None, None, "ang", None),
        ),
        check_vma=False,
    )
```

```python
import functools

import jax
import jax.numpy as jnp
from jax import lax
from jax.experimental import pallas as pl
from jax.experimental.pallas import tpu as pltpu
from jax.sharding import PartitionSpec as P

F32 = jnp.float32
BF16 = jnp.bfloat16
MESH = pl.DeviceIdType.MESH
ANY = pl.BlockSpec(memory_space=pl.ANY)
VMEM = pl.BlockSpec(memory_space=pltpu.VMEM)

RING2 = [(di, dk) for di in range(-2, 3) for dk in (-1, 0, 1) if (di, dk) != (0, 0)]
MROWS = [(-1, 1), (0, 0), (0, 1), (1, 0)]


def slot_of(di, dk):
    return (di + 2) * 3 + dk + 1


def lane_shift(x, step):
    if step == 1:
        return x
    width = x.shape[1]
    lane = lax.broadcasted_iota(jnp.int32, x.shape, 1)
    if step == 0:
        return jnp.where(lane == 0, F32(0.0), pltpu.roll(x, 1, 1))
    return jnp.where(lane == width - 1, F32(0.0), pltpu.roll(x, width - 1, 1))


def permuted(x, permutation):
    high = x.astype(BF16)
    rest = x - high.astype(F32)
    mid = rest.astype(BF16)
    low = (rest - mid.astype(F32)).astype(BF16)

    def times(part):
        return jnp.dot(part, permutation, preferred_element_type=F32)

    return times(high) + times(mid) + times(low)


SCRATCH = dict(
    slots=pltpu.VMEM((15, 2, 4, 128), F32),
    exm_v=pltpu.VMEM((2, 8, 4, 128), F32),
    exf_v=pltpu.VMEM((2, 8, 2, 8, 256), F32),
    em_v=pltpu.VMEM((4, 64, 128), F32),
    bins_v=pltpu.VMEM((4, 64, 128), jnp.int32),
    data_v=pltpu.VMEM((4, 64, 128), F32),
    spread_m=pltpu.VMEM((256, 256), BF16),
    gather_m=pltpu.VMEM((256, 256), BF16),
    ne=pltpu.VMEM((4, 4, 2, 4, 128), F32),
    ne_edge=pltpu.VMEM((2, 2, 4, 128), F32),
    ne_side=pltpu.VMEM((2, 4, 4, 128), F32),
    nex=pltpu.VMEM((4, 4, 16, 128), F32),
    ce=pltpu.VMEM((5, 2, 8, 128), F32),
    cs=pltpu.VMEM((5, 9, 16, 128), F32),
    xi=pltpu.VMEM((4, 2, 16, 256), F32),
    f16=pltpu.VMEM((2, 4, 2, 16, 128), F32),
    fs=pltpu.VMEM((4, 9, 16, 256), F32),
    esend=pltpu.VMEM((256, 128), F32),
    erecv=pltpu.VMEM((256, 128), F32),
    dsend=pltpu.VMEM((512, 128), F32),
    drecv=pltpu.VMEM((512, 128), F32),
    gsend=pltpu.VMEM((512, 128), F32),
    grecv=pltpu.VMEM((512, 128), F32),
    colv=pltpu.VMEM((512, 128), F32),
    star_x=pltpu.VMEM((2, 8, 8, 512), F32),
    star_y=pltpu.VMEM((2, 4, 8, 128), F32),
    star_z=pltpu.VMEM((2, 2, 32, 128), F32),
    res_x=pltpu.VMEM((2, 32, 128), F32),
    rsend=pltpu.VMEM((64, 128), F32),
    rrecv=pltpu.VMEM((512, 128), F32),
    ws=pltpu.VMEM((4, 9, 16, 256), F32),
    g16=pltpu.VMEM((2, 4, 2, 16, 128), F32),
    hh=pltpu.VMEM((4, 2, 16, 256), F32),
    h_edge=pltpu.VMEM((2, 4, 4, 128), F32),
    h_rad=pltpu.VMEM((2, 2, 16, 256), F32),
    h_side=pltpu.VMEM((2, 4, 4, 128), F32),
    wq=pltpu.VMEM((5, 9, 16, 128), F32),
    gcx=pltpu.VMEM((5, 16, 128), F32),
    gslots=pltpu.VMEM((15, 16, 128), F32),
    km_s=pltpu.SMEM((16, 8, 27), F32),
    nm_s=pltpu.SMEM((8, 8, 16), F32),
    kf_s=pltpu.SMEM((16, 8, 27), F32),
    nf_s=pltpu.SMEM((8, 8, 16), F32),
    rm_s=pltpu.SMEM((8,), jnp.int32),
    rf_s=pltpu.SMEM((16,), jnp.int32),
    table_sem=pltpu.SemaphoreType.DMA((6,)),
    local_sem=pltpu.SemaphoreType.DMA((16,)),
    self_sem=pltpu.SemaphoreType.DMA((8,)),
    cs_send=pltpu.SemaphoreType.DMA((15,)),
    cs_recv=pltpu.SemaphoreType.DMA((15,)),
    ne_send=pltpu.SemaphoreType.DMA((8,)),
    ne_recv=pltpu.SemaphoreType.DMA((8,)),
    e_send=pltpu.SemaphoreType.DMA((8,)),
    e_recv=pltpu.SemaphoreType.DMA((8,)),
    d_send=pltpu.SemaphoreType.DMA((8,)),
    d_recv=pltpu.SemaphoreType.DMA((8,)),
    g_send=pltpu.SemaphoreType.DMA((8,)),
    g_recv=pltpu.SemaphoreType.DMA((8,)),
    r_send=pltpu.SemaphoreType.DMA((8,)),
    r_recv=pltpu.SemaphoreType.DMA((8,)),
    h_send=pltpu.SemaphoreType.DMA((8,)),
    h_recv=pltpu.SemaphoreType.DMA((8,)),
    q_send=pltpu.SemaphoreType.DMA((15,)),
    q_recv=pltpu.SemaphoreType.DMA((15,)),
)
INPUTS = ["cf", "exm", "exf", "km", "nm", "rm", "kf", "nf", "rf", "emi", "bins", "data"]
OUTPUTS = ["gc_v", "gm_v", "gf_v", "res_v"]


class Refs:
    def __init__(self, refs):
        for name, ref in zip(INPUTS + OUTPUTS + list(SCRATCH), refs):
            setattr(self, name, ref)


def kernel(nr, na, *refs):
    v = Refs(refs)
    i = lax.axis_index("rad")
    k = lax.axis_index("ang")
    coarse_a = 4 * na

    def row_at(di):
        return lax.rem(i + (di + nr), nr)

    def block_at(dk):
        return lax.rem(k + (dk + na), na)

    def remote(src, dst, send, recv, di, dk):
        return pltpu.make_async_remote_copy(
            src_ref=src,
            dst_ref=dst,
            send_sem=send,
            recv_sem=recv,
            device_id=(row_at(di), block_at(dk)),
            device_id_type=MESH,
        )

    def part(ref, index, size):
        return ref.at[pl.ds(pl.multiple_of(index * size, size), size)]

    peers = [(d, 0) for d in range(1, nr)] + [(di, dk) for di, dk in RING2 if dk != 0]
    barrier = pltpu.get_barrier_semaphore()
    for di, dk in peers:
        pl.semaphore_signal(
            barrier, inc=1, device_id=(row_at(di), block_at(dk)), device_id_type=MESH
        )

    loads = [
        pltpu.make_async_copy(v.exm.at[:, :, 0], v.exm_v, v.local_sem.at[0]),
        pltpu.make_async_copy(v.cf.at[:, 0], v.slots.at[slot_of(0, 0)], v.local_sem.at[1]),
    ]
    for c in range(4):
        lanes = pl.ds(128 * c, 128)
        for t, (src, dst) in enumerate(
            ((v.emi, v.em_v), (v.bins, v.bins_v), (v.data, v.data_v))
        ):
            loads.append(
                pltpu.make_async_copy(
                    src.at[:, :, lanes],
                    dst.at[c].reshape(4, 16, 128),
                    v.local_sem.at[2 + 4 * t + c],
                )
            )
    loads.append(pltpu.make_async_copy(v.exf, v.exf_v, v.local_sem.at[14]))
    tables = [
        pltpu.make_async_copy(src, dst, v.table_sem.at[n])
        for n, (src, dst) in enumerate(
            (
                (v.rm, v.rm_s),
                (v.nm, v.nm_s),
                (v.rf, v.rf_s),
                (v.km, v.km_s),
                (v.nf, v.nf_s),
                (v.kf, v.kf_s),
            )
        )
    ]
    for load in loads[:2] + tables + loads[2:]:
        load.start()

    row = lax.broadcasted_iota(jnp.int32, (256, 256), 0)
    col = lax.broadcasted_iota(jnp.int32, (256, 256), 1)
    one, none = F32(1.0), F32(0.0)
    v.gather_m[...] = jnp.where(
        row == 2 * lax.bitwise_and(col, 127) + lax.shift_right_logical(col, 7), one, none
    ).astype(BF16)
    v.spread_m[...] = jnp.where(
        col == 2 * lax.bitwise_and(row, 127) + lax.shift_right_logical(row, 7), one, none
    ).astype(BF16)

    loads[0].wait()
    for table in tables:
        table.wait()
    mid_row = v.rm_s[i]
    for cr in range(2):
        for q in range(4):
            for s in range(2):
                total = v.nm_s[4 * cr + q, 0, mid_row] * v.exm_v[s, 0]
                for j in range(1, 8):
                    total = total + v.nm_s[4 * cr + q, j, mid_row] * v.exm_v[s, j]
                v.ne[1 + cr, q, s] = total
                ca, cb = q // 2, q % 2
                if ca == 1:
                    v.ne_edge[0, cr, pl.ds(2 * cb + s, 1)] = total[3:4]
                else:
                    v.ne_edge[1, cr, pl.ds(2 * cb + s, 1)] = total[0:1]
    loads[1].wait()

    for c in range(12):
        loads[2 + c].wait()
    pieces = [
        jnp.concatenate(
            [v.em_v[2 * h + e, pl.ds(16 * rl + ca, 8, stride=2), :] for e in range(2)], axis=1
        )
        for rl in range(4)
        for ca in range(2)
        for h in range(2)
    ]
    pieces = permuted(jnp.concatenate(pieces, axis=0), v.gather_m[...])
    for rl in range(4):
        for ca in range(2):
            for h in range(2):
                n = (rl * 2 + ca) * 2 + h
                for cb in range(2):
                    at = h * 16 + rl * 4 + ca * 2 + cb
                    v.esend[pl.ds(at, 8, stride=32), :] = pieces[
                        8 * n : 8 * n + 8, 128 * cb : 128 * cb + 128
                    ]

    def scatter(src, dst, send, recv, size):
        return [
            remote(part(src, row_at(d), size), part(dst, i, size), send.at[d], recv.at[d], d, 0)
            for d in range(1, nr)
        ]

    def keep_own(src, dst, size, sem):
        return pltpu.make_async_copy(part(src, i, size), part(dst, i, size), sem)

    for n in range(4):
        for ca in range(2):
            for c in range(4):
                at = pl.ds(16 * n + ca, 8, stride=2)
                lanes = pl.ds(128 * c, 128)
                v.star_x[0, :, 2 * n + ca, lanes] = v.bins_v[c, at, :].astype(F32)
                v.star_x[1, :, 2 * n + ca, lanes] = v.data_v[c, at, :]
    for kind in range(2):
        x = v.star_x[kind, i]
        y = permuted(jnp.concatenate([x[:, :256], x[:, 256:]], axis=0), v.gather_m[...])
        for h in range(2):
            for cb in range(2):
                v.star_y[kind, 2 * h + cb] = y[8 * h : 8 * h + 8, 128 * cb : 128 * cb + 128]
        for h in range(2):
            for cb in range(2):
                for ca in range(2):
                    rows = v.star_y[kind, 2 * h + cb, pl.ds(ca, 4, stride=2), :]
                    for s in range(2):
                        v.star_z[kind, h, pl.ds(4 * s + 2 * ca + cb, 4, stride=8), :] = rows

    pl.semaphore_wait(barrier, len(peers))

    halo = [
        remote(
            v.cf.at[:, 0],
            v.slots.at[slot_of(-di, -dk)],
            v.cs_send.at[slot_of(di, dk)],
            v.cs_recv.at[slot_of(-di, -dk)],
            di,
            dk,
        )
        for di, dk in RING2
    ]
    moves = [(v.ne.at[1], v.ne.at[3], -1, 0), (v.ne.at[2], v.ne.at[0], 1, 0)]
    for side, dk in ((0, 1), (1, -1)):
        moves += [
            (v.ne_edge.at[side], v.ne_side.at[side, 1:3], 0, dk),
            (v.ne_edge.at[side, 0], v.ne_side.at[side, 3], -1, dk),
            (v.ne_edge.at[side, 1], v.ne_side.at[side, 0], 1, dk),
        ]
    halo += [
        remote(src, dst, v.ne_send.at[n], v.ne_recv.at[n], di, dk)
        for n, (src, dst, di, dk) in enumerate(moves)
    ]
    for copy in halo:
        copy.start()

    sends_e = scatter(v.esend, v.erecv, v.e_send, v.e_recv, 32)
    own_e = keep_own(v.esend, v.erecv, 32, v.self_sem.at[0])
    own_e.start()
    for copy in sends_e:
        copy.start()

    for copy in halo:
        copy.wait()

    sub8 = lax.broadcasted_iota(jnp.int32, (8, 128), 0)
    sub16 = lax.bitwise_and(lax.broadcasted_iota(jnp.int32, (16, 128), 0), 7)

    def inside(local_a, di):
        there = jnp.where((i + di >= 0) & (i + di < nr), coarse_a, 0)
        a = 4 * k + local_a
        return (a >= 0) & (a < there)

    for q in range(5):
        for s in range(2):
            v.ce[q, s, 2:6] = v.slots[slot_of(q - 2, 0), s]
            v.ce[q, s, 0:2] = v.slots[slot_of(q - 2, -1), s, 2:4]
            v.ce[q, s, 6:8] = v.slots[slot_of(q - 2, 1), s, 0:2]
        here = inside(sub8 - 2, q - 2)
        both = [jnp.where(here, v.ce[q, s], none) for s in range(2)]
        for da in range(3):
            if da == 1:
                moved = both
            else:
                moved = [pltpu.roll(x, 1 if da == 0 else 7, 0) for x in both]
            moved = jnp.concatenate(moved, axis=0)
            for db in range(3):
                v.cs[q, 3 * da + db] = lane_shift(moved, db)

    for m in range(4):
        for q in range(4):
            for s in range(2):
                v.nex[m, q, 8 * s + 2 : 8 * s + 6] = v.ne[m, q, s]
                ca, cb = q // 2, q % 2
                if ca == 1:
                    v.nex[m, q, 8 * s + 1 : 8 * s + 2] = v.ne_side[0, m, pl.ds(2 * cb + s, 1)]
                else:
                    v.nex[m, q, 8 * s + 6 : 8 * s + 7] = v.ne_side[1, m, pl.ds(2 * cb + s, 1)]

    table_row = {}
    for di in (-1, 0, 1):
        table_row[di] = v.rm_s[jnp.clip(i + di, 0, nr - 1)]
    for m, (di, cr) in enumerate(MROWS):
        sums = [v.nex[m, q] for q in range(4)]
        for o in range(27):
            x = v.cs[di + 1 + o // 9, o % 9]
            for q in range(4):
                sums[q] = sums[q] + v.km_s[table_row[di], 4 * cr + q, o] * x
        used = inside(sub16 - 2, di) & (sub16 >= 1) & (sub16 <= 6)
        for q in range(4):
            lanes = slice(128 * (q % 2), 128 * (q % 2) + 128)
            v.xi[m, q // 2, :, lanes] = jnp.where(used, sums[q], none)
    spread = permuted(v.xi[...].reshape(128, 256), v.spread_m[...])
    for m in range(4):
        for ca in range(2):
            for s in range(2):
                n = (m * 2 + ca) * 16 + 8 * s
                for h in range(2):
                    v.f16[h, m, s, pl.ds(ca, 8, stride=2), :] = spread[
                        n : n + 8, 128 * h : 128 * h + 128
                    ]
    for m in range(4):
        for da in range(3):
            rows = slice(3 + da, 11 + da)
            x = jnp.concatenate(
                [
                    jnp.concatenate([v.f16[h, m, s, rows, :] for h in range(2)], axis=1)
                    for s in range(2)
                ],
                axis=0,
            )
            for db in range(3):
                v.fs[m, 3 * da + db] = lane_shift(x, db)

    loads[14].wait()
    fine_row = [v.rf_s[2 * i + r] for r in range(2)]
    for r in range(2):
        for half in range(2):
            sums = [None] * 4
            for j in range(8):
                x = jnp.concatenate([v.exf_v[s, j, r] for s in range(2)], axis=0)
                for q in range(4):
                    term = v.nf_s[4 * half + q, j, fine_row[r]] * x
                    sums[q] = term if j == 0 else sums[q] + term
            for o in range(27):
                x = v.fs[r + o // 9, o % 9]
                for q in range(4):
                    sums[q] = sums[q] + v.kf_s[fine_row[r], 4 * half + q, o] * x
            for q in range(4):
                density = jnp.exp(sums[q])
                for s in range(2):
                    for h in range(2):
                        at = h * 32 + (2 * r + half) * 8 + 4 * s + q
                        v.dsend[pl.ds(at, 8, stride=64), :] = density[
                            8 * s : 8 * s + 8, 128 * h : 128 * h + 128
                        ]
    sends_d = scatter(v.dsend, v.drecv, v.d_send, v.d_recv, 64)
    own_d = keep_own(v.dsend, v.drecv, 64, v.self_sem.at[1])
    for copy in sends_d:
        copy.start()
    own_d.start()

    for copy in sends_e:
        copy.wait()
    own_e.wait()
    for copy in sends_d:
        copy.wait()
    own_d.wait()

    spacing = F32(1.0 / (4 * nr))
    cells = 4 * nr
    for h in range(2):
        bins = [v.star_z[0, h, 8 * n : 8 * n + 8] for n in range(4)]
        seen = [v.star_z[1, h, 8 * n : 8 * n + 8] for n in range(4)]
        depth = jnp.zeros((8, 128), F32)
        column = jnp.zeros((8, 128), F32)
        picked = [jnp.zeros((8, 128), F32) for _ in range(4)]
        for cell in range(cells):
            at = (cell // 4) * 64 + h * 32 + (cell % 4) * 8
            ea = (cell // 4) * 32 + h * 16 + (cell % 4) * 4
            light = v.erecv[ea : ea + 4]
            light = jnp.concatenate([light, light], axis=0)
            column = column + spacing * light * jnp.exp(-depth)
            depth = depth + spacing * v.drecv[at : at + 8]
            v.colv[at : at + 8] = column
            for n in range(4):
                picked[n] = jnp.where(bins[n] == F32(cell), column, picked[n])
        left = [seen[n] - picked[n] for n in range(4)]
        for n in range(4):
            v.res_x[h, 8 * n : 8 * n + 8] = left[n]
        for cell in range(cells):
            at = (cell // 4) * 64 + h * 32 + (cell % 4) * 8
            column = v.colv[at : at + 8]
            weight = None
            for n in range(4):
                term = jnp.where(
                    bins[n] > F32(cell), left[n] * (picked[n] - column), F32(0.0)
                )
                weight = term if n == 0 else weight + term
            v.gsend[at : at + 8] = -v.drecv[at : at + 8] * weight
    sends_g = scatter(v.gsend, v.grecv, v.g_send, v.g_recv, 64)
    own_g = keep_own(v.gsend, v.grecv, 64, v.self_sem.at[2])
    for copy in sends_g:
        copy.start()
    own_g.start()

    pieces = [
        jnp.concatenate([v.res_x[h, pl.ds(cb, 16, stride=2), :] for cb in range(2)], axis=1)
        for h in range(2)
    ]
    spread = permuted(jnp.concatenate(pieces, axis=0), v.spread_m[...])
    for h in range(2):
        for e in range(2):
            c = 2 * h + e
            v.rsend[16 * c : 16 * c + 16] = spread[
                16 * h : 16 * h + 16, 128 * e : 128 * e + 128
            ]
    sends_r = [
        remote(v.rsend, part(v.rrecv, i, 64), v.r_send.at[d], v.r_recv.at[d], d, 0)
        for d in range(1, nr)
    ]
    own_r = pltpu.make_async_copy(v.rsend, part(v.rrecv, i, 64), v.self_sem.at[3])
    for copy in sends_r:
        copy.start()
    own_r.start()

    for copy in sends_g:
        copy.wait()
    own_g.wait()

    for r in range(2):
        grads = []
        for c in range(8):
            cr, q = c // 4, c % 4
            at = [[h * 32 + (2 * r + cr) * 8 + 4 * s + q for h in range(2)] for s in range(2)]
            grads.append(
                jnp.concatenate(
                    [
                        jnp.concatenate(
                            [v.grecv[pl.ds(at[s][h], 8, stride=64), :] for h in range(2)], axis=1
                        )
                        for s in range(2)
                    ],
                    axis=0,
                )
            )
        for j in range(8):
            total = v.nf_s[0, j, fine_row[r]] * grads[0]
            for c in range(1, 8):
                total = total + v.nf_s[c, j, fine_row[r]] * grads[c]
            for s in range(2):
                v.gf_v[s, j, r] = total[8 * s : 8 * s + 8]
        for o in range(27):
            total = v.kf_s[fine_row[r], 0, o] * grads[0]
            for c in range(1, 8):
                total = total + v.kf_s[fine_row[r], c, o] * grads[c]
            m = r + o // 9
            if r == 1 and m < 3:
                total = total + v.ws[m, o % 9]
            v.ws[m, o % 9] = total
    v.g16[...] = jnp.zeros(v.g16.shape, F32)
    for m in range(4):
        for da in range(3):
            total = lane_shift(v.ws[m, 3 * da + 1], 1)
            total = total + lane_shift(v.ws[m, 3 * da], 2)
            total = total + lane_shift(v.ws[m, 3 * da + 2], 0)
            rows = slice(3 + da, 11 + da)
            for h in range(2):
                for s in range(2):
                    v.g16[h, m, s, rows, :] = (
                        v.g16[h, m, s, rows, :]
                        + total[8 * s : 8 * s + 8, 128 * h : 128 * h + 128]
                    )
    pieces = []
    for m in range(4):
        here = inside(sub8 - 2, MROWS[m][0])
        for ca in range(2):
            for s in range(2):
                pieces.append(
                    jnp.concatenate(
                        [
                            jnp.where(here, v.g16[h, m, s, pl.ds(ca, 8, stride=2), :], none)
                            for h in range(2)
                        ],
                        axis=1,
                    )
                )
    v.hh[...] = permuted(jnp.concatenate(pieces, axis=0), v.gather_m[...]).reshape(4, 2, 16, 256)
    for m in range(4):
        for s in range(2):
            for cb in range(2):
                lanes = slice(128 * cb, 128 * cb + 128)
                v.h_edge[0, m, pl.ds(2 * s + cb, 1)] = v.hh[m, 1, 8 * s + 1 : 8 * s + 2, lanes]
                v.h_edge[1, m, pl.ds(2 * s + cb, 1)] = v.hh[m, 0, 8 * s + 6 : 8 * s + 7, lanes]
    moves = [(v.hh.at[0], v.h_rad.at[1], -1, 0), (v.hh.at[3], v.h_rad.at[0], 1, 0)]
    for side, dk in ((0, -1), (1, 1)):
        moves += [
            (v.h_edge.at[side, 1:3], v.h_side.at[side, 0:2], 0, dk),
            (v.h_edge.at[side, 0], v.h_side.at[side, 3], -1, dk),
            (v.h_edge.at[side, 3], v.h_side.at[side, 2], 1, dk),
        ]
    owed = [
        remote(src, dst, v.h_send.at[n], v.h_recv.at[n], di, dk)
        for n, (src, dst, di, dk) in enumerate(moves)
    ]
    for copy in owed:
        copy.start()

    for di in (-1, 0, 1):
        children = []
        for m, (mdi, cr) in enumerate(MROWS):
            if mdi == di:
                for q in range(4):
                    lanes = slice(128 * (q % 2), 128 * (q % 2) + 128)
                    children.append((4 * cr + q, v.hh[m, q // 2, :, lanes]))
        for o in range(27):
            total = None
            for c, x in children:
                term = v.km_s[table_row[di], c, o] * x
                total = term if total is None else total + term
            row_q = di + 1 + o // 9
            if di > -1 and row_q < di + 3:
                total = total + v.wq[row_q, o % 9]
            v.wq[row_q, o % 9] = total
    for q in range(5):
        pieces = []
        for da in range(3):
            total = v.wq[q, 3 * da + 1]
            total = total + lane_shift(v.wq[q, 3 * da], 2)
            total = total + lane_shift(v.wq[q, 3 * da + 2], 0)
            pieces.append(total)
        here = inside(sub8 - 2, q - 2)
        for s in range(2):
            rows = slice(8 * s, 8 * s + 8)
            total = pieces[1][rows]
            total = total + pltpu.roll(pieces[0][rows], 7, 0)
            total = total + pltpu.roll(pieces[2][rows], 1, 0)
            v.gcx[q, rows] = jnp.where(here, total, none)
    owed_q = [
        remote(
            v.gcx.at[di + 2],
            v.gslots.at[slot_of(-di, -dk)],
            v.q_send.at[slot_of(di, dk)],
            v.q_recv.at[slot_of(-di, -dk)],
            di,
            dk,
        )
        for di, dk in RING2
    ]
    for copy in owed_q:
        copy.start()

    for copy in sends_r:
        copy.wait()
    own_r.wait()
    for c in range(4):
        for n in range(4):
            for s in range(2):
                for ca in range(2):
                    at = 16 * c + n * 4 + s * 2 + ca
                    v.res_v[c, pl.ds((s * 4 + n) * 16 + ca, 8, stride=2), :] = v.rrecv[
                        pl.ds(at, 8, stride=64), :
                    ]
    for copy in owed:
        copy.wait()
    for s in range(2):
        grads = []
        for cr in range(2):
            for q in range(4):
                ca, cb = q // 2, q % 2
                lanes = slice(128 * cb, 128 * cb + 128)
                rows = slice(8 * s + 2, 8 * s + 6)
                total = v.hh[1 + cr, ca, rows, lanes] + v.h_rad[cr, ca, rows, lanes]
                side, place = (0, 3) if ca == 1 else (1, 0)
                edge = pl.ds(2 * s + cb, 1)
                extra = v.h_side[side, cr, edge] + v.h_side[side, 2 + cr, edge]
                at = lax.broadcasted_iota(jnp.int32, (4, 128), 0)
                grads.append(
                    total + jnp.where(at == place, jnp.broadcast_to(extra, (4, 128)), none)
                )
        for j in range(8):
            total = v.nm_s[0, j, mid_row] * grads[0]
            for c in range(1, 8):
                total = total + v.nm_s[c, j, mid_row] * grads[c]
            v.gm_v[s, j] = total
    for copy in owed_q:
        copy.wait()
    for s in range(2):
        total = v.gcx[2, 8 * s + 2 : 8 * s + 6]
        low = jnp.zeros((2, 128), F32)
        high = jnp.zeros((2, 128), F32)
        for di in range(-2, 3):
            if di != 0:
                total = total + v.gslots[slot_of(di, 0), 8 * s + 2 : 8 * s + 6]
            low = low + v.gslots[slot_of(di, -1), 8 * s + 6 : 8 * s + 8]
            high = high + v.gslots[slot_of(di, 1), 8 * s : 8 * s + 2]
        v.gc_v[s] = total + jnp.concatenate([low, high], axis=0)


def hand_out(gc_v, gm_v, gf_v, res_v, gc_o, gm_o, gf_o, res_o, sem):
    outs = [
        pltpu.make_async_copy(gf_v, gf_o, sem.at[0]),
        pltpu.make_async_copy(gm_v, gm_o.at[:, :, 0], sem.at[1]),
        pltpu.make_async_copy(gc_v, gc_o.at[:, 0], sem.at[2]),
    ]
    for c in range(4):
        outs.append(
            pltpu.make_async_copy(
                res_v.at[c].reshape(2, 4, 16, 128),
                res_o.at[:, :, :, pl.ds(128 * c, 128)],
                sem.at[3 + c],
            )
        )
    for out in outs:
        out.start()
    for out in outs:
        out.wait()


def per_device(*args):
    nr, na = lax.axis_size("rad"), lax.axis_size("ang")
    args = list(args)
    for n in (4, 7):
        args[n] = args[n].transpose(1, 2, 0)
    held = [(2, 4, 128), (2, 8, 4, 128), (2, 8, 2, 8, 256), (4, 128, 128)]
    shapes = [(2, 1, 4, 128), (2, 8, 1, 4, 128), (2, 8, 2, 8, 256), (2, 4, 16, 512)]
    results = pl.pallas_call(
        functools.partial(kernel, nr, na),
        out_shape=[pltpu.VMEM(shape, F32) for shape in held],
        in_specs=[ANY] * 12,
        out_specs=[VMEM] * 4,
        scratch_shapes=list(SCRATCH.values()),
        compiler_params=pltpu.CompilerParams(collective_id=0, has_side_effects=True),
    )(*args)
    return pl.pallas_call(
        hand_out,
        out_shape=[jax.ShapeDtypeStruct(shape, F32) for shape in shapes],
        in_specs=[VMEM] * 4,
        out_specs=[ANY] * 4,
        scratch_shapes=[pltpu.SemaphoreType.DMA((7,))],
        compiler_params=pltpu.CompilerParams(vmem_limit_bytes=4 << 20),
    )(*results)


def solution(mesh):
    placed = (
        P(None, "rad", "ang", None),
        P(None, None, "rad", "ang", None),
        P(None, None, "rad", "ang", None),
        P(),
        P(),
        P(),
        P(),
        P(),
        P(),
        P("rad", "ang", None),
        P(None, "ang", None),
        P(None, "ang", None),
    )
    return jax.shard_map(
        per_device,
        mesh=mesh,
        in_specs=placed,
        out_specs=(
            P(None, "rad", "ang", None),
            P(None, None, "rad", "ang", None),
            P(None, None, "rad", "ang", None),
            P(None, None, "ang", None),
        ),
        check_vma=False,
    )
```

```python
import functools

import jax
import jax.numpy as jnp
from jax import lax
from jax.experimental import pallas as pl
from jax.experimental.pallas import tpu as pltpu
from jax.sharding import PartitionSpec as P

F32 = jnp.float32
BF16 = jnp.bfloat16
MESH = pl.DeviceIdType.MESH
ANY = pl.BlockSpec(memory_space=pl.ANY)
VMEM = pl.BlockSpec(memory_space=pltpu.VMEM)


def lane_shift(x, step):
    if step == 1:
        return x
    width = x.shape[1]
    lane = lax.broadcasted_iota(jnp.int32, x.shape, 1)
    if step == 0:
        return jnp.where(lane == 0, F32(0.0), pltpu.roll(x, 1, 1))
    return jnp.where(lane == width - 1, F32(0.0), pltpu.roll(x, width - 1, 1))


def permuted(x, permutation):
    high = x.astype(BF16)
    rest = x - high.astype(F32)
    mid = rest.astype(BF16)
    low = (rest - mid.astype(F32)).astype(BF16)

    def times(part):
        return jnp.dot(part, permutation, preferred_element_type=F32)

    return times(high) + times(mid) + times(low)


SCRATCH = dict(
    cf_v=pltpu.VMEM((2, 4, 128), F32),
    exm_v=pltpu.VMEM((2, 8, 4, 128), F32),
    exf_v=pltpu.VMEM((2, 8, 2, 8, 256), F32),
    em_v=pltpu.VMEM((4, 64, 128), F32),
    bins_v=pltpu.VMEM((4, 64, 128), jnp.int32),
    data_v=pltpu.VMEM((4, 64, 128), F32),
    km_v=pltpu.VMEM((16, 8, 27), F32),
    nm_v=pltpu.VMEM((8, 8, 16), F32),
    kf_v=pltpu.VMEM((16, 8, 27), F32),
    nf_v=pltpu.VMEM((8, 8, 16), F32),
    rm_s=pltpu.SMEM((8,), jnp.int32),
    rf_s=pltpu.SMEM((16,), jnp.int32),
    spread_m=pltpu.VMEM((256, 256), BF16),
    gather_m=pltpu.VMEM((256, 256), BF16),
    table=pltpu.VMEM((3, 64, 128), F32),
    kern=pltpu.VMEM((3, 8, 27, 8, 128), F32),
    noise=pltpu.VMEM((3, 8, 8, 8, 128), F32),
    csend=pltpu.VMEM((8, 128), F32),
    crecv=pltpu.VMEM((3, 64, 128), F32),
    nsend=pltpu.VMEM((64, 128), F32),
    nrecv=pltpu.VMEM((256, 128), F32),
    nside=pltpu.VMEM((128, 128), F32),
    xsend=pltpu.VMEM((512, 128), F32),
    xrecv=pltpu.VMEM((512, 128), F32),
    esend=pltpu.VMEM((256, 128), F32),
    erecv=pltpu.VMEM((256, 128), F32),
    c12=pltpu.VMEM((12, 16, 128), F32),
    emx=pltpu.VMEM((4, 8, 16, 128), F32),
    cs=pltpu.VMEM((4, 9, 16, 128), F32),
    xi=pltpu.VMEM((4, 2, 16, 256), F32),
    m4=pltpu.VMEM((4, 2, 16, 256), F32),
    fs=pltpu.VMEM((4, 9, 16, 256), F32),
    dv=pltpu.VMEM((4, 4, 16, 256), F32),
    star_x=pltpu.VMEM((2, 8, 8, 512), F32),
    star_y=pltpu.VMEM((2, 4, 8, 128), F32),
    star_z=pltpu.VMEM((2, 2, 16, 128), F32),
    res_x=pltpu.VMEM((2, 32, 128), F32),
    rsend=pltpu.VMEM((64, 128), F32),
    rrecv=pltpu.VMEM((512, 128), F32),
    ws=pltpu.VMEM((4, 9, 16, 256), F32),
    h4=pltpu.VMEM((4, 2, 16, 256), F32),
    wq=pltpu.VMEM((4, 9, 16, 128), F32),
    g12=pltpu.VMEM((12, 16, 128), F32),
    gfsend=pltpu.VMEM((512, 128), F32),
    gfrecv=pltpu.VMEM((512, 128), F32),
    hsend=pltpu.VMEM((320, 128), F32),
    hrecv=pltpu.VMEM((320, 128), F32),
    hedge=pltpu.VMEM((2, 64, 128), F32),
    hside=pltpu.VMEM((2, 16, 128), F32),
    gside=pltpu.VMEM((6, 8, 128), F32),
    gm_x=pltpu.VMEM((64, 128), F32),
    table_sem=pltpu.SemaphoreType.DMA((6,)),
    local_sem=pltpu.SemaphoreType.DMA((15,)),
    self_sem=pltpu.SemaphoreType.DMA((7,)),
    c_send=pltpu.SemaphoreType.DMA((13,)),
    c_recv=pltpu.SemaphoreType.DMA((15,)),
    n_send=pltpu.SemaphoreType.DMA((9,)),
    n_recv=pltpu.SemaphoreType.DMA((15,)),
    x_send=pltpu.SemaphoreType.DMA((7,)),
    x_recv=pltpu.SemaphoreType.DMA((7,)),
    e_send=pltpu.SemaphoreType.DMA((7,)),
    e_recv=pltpu.SemaphoreType.DMA((7,)),
    r_send=pltpu.SemaphoreType.DMA((7,)),
    r_recv=pltpu.SemaphoreType.DMA((7,)),
    f_send=pltpu.SemaphoreType.DMA((7,)),
    f_recv=pltpu.SemaphoreType.DMA((7,)),
    h_send=pltpu.SemaphoreType.DMA((7,)),
    h_recv=pltpu.SemaphoreType.DMA((7,)),
    hs_send=pltpu.SemaphoreType.DMA((8,)),
    hs_recv=pltpu.SemaphoreType.DMA((2,)),
    gs_send=pltpu.SemaphoreType.DMA((8,)),
    gs_recv=pltpu.SemaphoreType.DMA((6,)),
)
INPUTS = ["cf", "exm", "exf", "km", "nm", "rm", "kf", "nf", "rf", "emi", "bins", "data"]
OUTPUTS = ["gc_v", "gm_v", "gf_v", "res_v"]


class Refs:
    def __init__(self, refs):
        for name, ref in zip(INPUTS + OUTPUTS + list(SCRATCH), refs):
            setattr(self, name, ref)


def wide(x):
    return jnp.concatenate([x, x], axis=0)


def wide4(x):
    x = jnp.concatenate([x, x], axis=1)
    return jnp.concatenate([x, x], axis=0)


def row_shift(x, step):
    if step == 1:
        return x
    parts = []
    for s in range(2):
        part = x[8 * s : 8 * s + 8]
        sub = lax.broadcasted_iota(jnp.int32, part.shape, 0)
        if step == 0:
            part = jnp.where(sub == 0, F32(0.0), pltpu.roll(part, 1, 0))
        else:
            part = jnp.where(sub == 7, F32(0.0), pltpu.roll(part, 7, 0))
        parts.append(part)
    return jnp.concatenate(parts, axis=0)


def sums_before(x):
    sub = lax.broadcasted_iota(jnp.int32, x.shape, 0)
    total = x
    for step in (1, 2, 4):
        total = total + jnp.where(sub < step, F32(0.0), pltpu.roll(total, step, 0))
    return jnp.where(sub == 0, F32(0.0), pltpu.roll(total, 1, 0))


def row_total(x):
    for step in (4, 2, 1):
        x = x + pltpu.roll(x, step, 0)
    return x


def kernel(nr, na, *refs):
    v = Refs(refs)
    i = lax.axis_index("rad")
    k = lax.axis_index("ang")
    half_up = lax.shift_right_logical(i + 1, 1)
    low = half_up - 1
    first = 1 - lax.bitwise_and(i, 1)
    none = F32(0.0)

    def row_at(d):
        return lax.rem(i + d, nr)

    def block_at(dk):
        return lax.rem(k + (dk + na), na)

    def remote(src, dst, send, recv, row, dk):
        return pltpu.make_async_remote_copy(
            src_ref=src,
            dst_ref=dst,
            send_sem=send,
            recv_sem=recv,
            device_id=(row, block_at(dk)),
            device_id_type=MESH,
        )

    def part(ref, index, size):
        return ref.at[pl.ds(pl.multiple_of(index * size, size), size)]

    def scatter(src, dst, send, recv, size):
        return [
            remote(
                part(src, row_at(d), size),
                part(dst, i, size),
                send.at[d - 1],
                recv.at[d - 1],
                row_at(d),
                0,
            )
            for d in range(1, nr)
        ]

    def keep_own(src, dst, size, sem):
        return pltpu.make_async_copy(part(src, i, size), part(dst, i, size), sem)

    barrier = pltpu.get_barrier_semaphore()
    for d in range(1, nr):
        pl.semaphore_signal(barrier, inc=1, device_id=(row_at(d), k), device_id_type=MESH)
    for dk in (-1, 1):
        for d in range(nr):
            pl.semaphore_signal(
                barrier, inc=1, device_id=(d, block_at(dk)), device_id_type=MESH
            )

    loads = [
        pltpu.make_async_copy(v.exm.at[:, :, 0], v.exm_v, v.local_sem.at[0]),
        pltpu.make_async_copy(v.cf.at[:, 0], v.cf_v, v.local_sem.at[1]),
    ]
    for c in range(4):
        lanes = pl.ds(128 * c, 128)
        for t, (src, dst) in enumerate(
            ((v.emi, v.em_v), (v.bins, v.bins_v), (v.data, v.data_v))
        ):
            loads.append(
                pltpu.make_async_copy(
                    src.at[:, :, lanes],
                    dst.at[c].reshape(4, 16, 128),
                    v.local_sem.at[2 + 4 * t + c],
                )
            )
    loads.append(pltpu.make_async_copy(v.exf, v.exf_v, v.local_sem.at[14]))
    tables = [
        pltpu.make_async_copy(src, dst, v.table_sem.at[n])
        for n, (src, dst) in enumerate(
            (
                (v.rm, v.rm_s),
                (v.rf, v.rf_s),
                (v.km, v.km_v),
                (v.nm, v.nm_v),
                (v.kf, v.kf_v),
                (v.nf, v.nf_v),
            )
        )
    ]
    for load in [loads[14]] + loads[:14] + tables:
        load.start()

    row = lax.broadcasted_iota(jnp.int32, (256, 256), 0)
    col = lax.broadcasted_iota(jnp.int32, (256, 256), 1)
    v.gather_m[...] = jnp.where(
        row == 2 * lax.bitwise_and(col, 127) + lax.shift_right_logical(col, 7), F32(1.0), none
    ).astype(BF16)
    v.spread_m[...] = jnp.where(
        col == 2 * lax.bitwise_and(row, 127) + lax.shift_right_logical(row, 7), F32(1.0), none
    ).astype(BF16)

    for load in loads + tables:
        load.wait()
    for r in range(2):
        for j in range(8):
            for s in range(2):
                for h in range(2):
                    at = ((r * 8 + j) * 2 + s) * 2 + h
                    v.xsend[pl.ds(at, 8, stride=64), :] = v.exf_v[
                        s, j, r, :, 128 * h : 128 * h + 128
                    ]
    for s in range(2):
        v.csend[4 * s : 4 * s + 4] = v.cf_v[s]
        for j in range(8):
            v.nsend[pl.ds(8 * s + j, 4, stride=16), :] = v.exm_v[s, j]
    pieces = [
        jnp.concatenate(
            [v.em_v[2 * h + e, pl.ds(16 * rl + ca, 8, stride=2), :] for e in range(2)], axis=1
        )
        for rl in range(4)
        for ca in range(2)
        for h in range(2)
    ]
    pieces = permuted(jnp.concatenate(pieces, axis=0), v.gather_m[...])
    for rl in range(4):
        for ca in range(2):
            for h in range(2):
                n = (rl * 2 + ca) * 2 + h
                for cb in range(2):
                    at = h * 16 + rl * 4 + ca * 2 + cb
                    v.esend[pl.ds(at, 8, stride=32), :] = pieces[
                        8 * n : 8 * n + 8, 128 * cb : 128 * cb + 128
                    ]

    for n in range(4):
        for ca in range(2):
            for c in range(4):
                at = pl.ds(16 * n + ca, 8, stride=2)
                lanes = pl.ds(128 * c, 128)
                v.star_x[0, :, 2 * n + ca, lanes] = v.bins_v[c, at, :].astype(F32)
                v.star_x[1, :, 2 * n + ca, lanes] = v.data_v[c, at, :]
    for kind in range(2):
        x = v.star_x[kind, i]
        y = permuted(jnp.concatenate([x[:, :256], x[:, 256:]], axis=0), v.gather_m[...])
        for h in range(2):
            for cb in range(2):
                v.star_y[kind, 2 * h + cb] = y[8 * h : 8 * h + 8, 128 * cb : 128 * cb + 128]
        for h in range(2):
            for cb in range(2):
                for ca in range(2):
                    v.star_z[kind, h, pl.ds(2 * ca + cb, 4, stride=4), :] = v.star_y[
                        kind, 2 * h + cb, pl.ds(ca, 4, stride=2), :
                    ]

    entry = lax.broadcasted_iota(jnp.int32, (8, 16), 1)
    place = lax.broadcasted_iota(jnp.int32, (8, 16), 0)
    chosen = []
    for x in range(3):
        index = jnp.zeros((8, 16), jnp.int32)
        for cell in range(8):
            if x == 0:
                number = v.rm_s[cell]
                v.table[x, pl.ds(cell, 8, stride=8), 0:27] = v.km_v[number]
            else:
                number = v.rf_s[2 * cell + x - 1]
                v.table[x, pl.ds(cell, 8, stride=8), 0:27] = v.kf_v[number]
            index = jnp.where(place == cell, number, index)
        chosen.append(jnp.where(index == entry, F32(1.0), none).astype(BF16))
    for x in range(3):
        for c in range(8):
            tile = v.table[x, 8 * c : 8 * c + 8]
            for o in range(27):
                v.kern[x, c, o] = jnp.broadcast_to(tile[:, o : o + 1], (8, 128))
        source = (v.nm_v if x == 0 else v.nf_v)[...].reshape(64, 16)
        high = source.astype(BF16)
        rest = source - high.astype(F32)
        mid = rest.astype(BF16)
        least = (rest - mid.astype(F32)).astype(BF16)
        tile = None
        for piece in (high, mid, least):
            term = lax.dot_general(
                chosen[x], piece, (((1,), (1,)), ((), ())), preferred_element_type=F32
            )
            tile = term if tile is None else tile + term
        for c in range(8):
            for j in range(8):
                at = 8 * c + j
                v.noise[x, c, j] = jnp.broadcast_to(tile[:, at : at + 1], (8, 128))

    pl.semaphore_wait(barrier, 3 * nr - 1)

    sends_c = [
        remote(
            v.csend,
            v.crecv.at[1, pl.ds(pl.multiple_of(i * 8, 8), 8)],
            v.c_send.at[d - 1],
            v.c_recv.at[d - 1],
            row_at(d),
            0,
        )
        for d in range(1, nr)
    ]
    for side, dk, rows in ((0, 1, (0, 1, 2)), (2, -1, (5, 6, 7))):
        for n, to in enumerate(rows):
            sends_c.append(
                remote(
                    v.csend,
                    v.crecv.at[side, pl.ds(pl.multiple_of(i * 8, 8), 8)],
                    v.c_send.at[7 + (0 if side == 0 else 3) + n],
                    v.c_recv.at[7 + i],
                    to,
                    dk,
                )
            )

    def start_of(owner):
        return jnp.clip(lax.shift_right_logical(owner + 1, 1) - 1, 0, 2)

    sends_n = [
        remote(
            v.nsend.at[pl.ds(pl.multiple_of(start_of(row_at(d)) * 16, 16), 32)],
            part(v.nrecv, i, 32),
            v.n_send.at[d - 1],
            v.n_recv.at[d - 1],
            row_at(d),
            0,
        )
        for d in range(1, nr)
    ]
    sends_n.append(
        remote(v.nsend.at[48:64], part(v.nside, i, 16), v.n_send.at[7], v.n_recv.at[7 + i], 0, 1)
    )
    sends_n.append(
        remote(v.nsend.at[0:16], part(v.nside, i, 16), v.n_send.at[8], v.n_recv.at[7 + i], 7, -1)
    )
    sends_x = scatter(v.xsend, v.xrecv, v.x_send, v.x_recv, 64)
    sends_e = scatter(v.esend, v.erecv, v.e_send, v.e_recv, 32)
    own = [
        pltpu.make_async_copy(
            v.csend, v.crecv.at[1, pl.ds(pl.multiple_of(i * 8, 8), 8)], v.self_sem.at[0]
        ),
        pltpu.make_async_copy(
            v.nsend.at[pl.ds(pl.multiple_of(start_of(i) * 16, 16), 32)],
            part(v.nrecv, i, 32),
            v.self_sem.at[1],
        ),
        keep_own(v.xsend, v.xrecv, 64, v.self_sem.at[2]),
        keep_own(v.esend, v.erecv, 32, v.self_sem.at[3]),
    ]
    for copy in sends_c + sends_n + sends_x + sends_e + own:
        copy.start()

    def arrived(dst, sem):
        pltpu.make_async_copy(dst, dst, sem).wait()

    for copy in sends_c[:7] + sends_n[:7]:
        copy.wait_recv()
    own[0].wait()
    own[1].wait()

    @pl.when(i <= 2)
    def _():
        for n in range(nr):
            arrived(v.crecv.at[0, pl.ds(8 * n, 8)], v.c_recv.at[7 + n])

    @pl.when(i >= 5)
    def _():
        for n in range(nr):
            arrived(v.crecv.at[2, pl.ds(8 * n, 8)], v.c_recv.at[7 + n])

    @pl.when((i == 0) | (i == 7))
    def _():
        for n in range(nr):
            arrived(v.nside.at[pl.ds(16 * n, 16)], v.n_recv.at[7 + n])

    for side in range(3):
        for a in range(4):
            x = jnp.concatenate(
                [v.crecv[side, pl.ds(4 * s + a, 8, stride=8), :] for s in range(2)], axis=0
            )
            if side == 0:
                x = jnp.where(k > 0, x, none)
            if side == 2:
                x = jnp.where(k < na - 1, x, none)
            v.c12[4 * side + a] = x
    for t in range(4):
        x = v.c12[half_up + 2 + t]
        for dr in range(3):
            moved = row_shift(x, dr)
            for db in range(3):
                v.cs[t, 3 * dr + db] = lane_shift(moved, db)
    for j in range(8):
        for n in range(2):
            v.emx[1 + n, j] = jnp.concatenate(
                [v.nrecv[pl.ds(16 * n + 8 * s + j, 8, stride=32), :] for s in range(2)], axis=0
            )
        x = jnp.concatenate(
            [v.nside[pl.ds(8 * s + j, 8, stride=16), :] for s in range(2)], axis=0
        )
        v.emx[0, j] = x
        v.emx[3, j] = x
    base = jnp.where(i > 0, 1, 0) + jnp.where(i == nr - 1, 1, 0)

    def parent_inside(u):
        a = 4 * k + low + u
        return (a >= 0) & (a < 4 * na)

    for u in range(2):
        for cr in range(2):
            sums = [None] * 4
            for j in range(8):
                x = v.emx[base + u, j]
                for q in range(4):
                    term = wide(v.noise[0, 4 * cr + q, j]) * x
                    sums[q] = term if j == 0 else sums[q] + term
            for o in range(27):
                dr, da, db = o // 9, o // 3 % 3, o % 3
                x = v.cs[u + da, 3 * dr + db]
                for q in range(4):
                    sums[q] = sums[q] + wide(v.kern[0, 4 * cr + q, o]) * x
            for q in range(4):
                lanes = slice(128 * (q % 2), 128 * (q % 2) + 128)
                v.xi[2 * u + q // 2, cr, :, lanes] = jnp.where(parent_inside(u), sums[q], none)
    v.m4[...] = permuted(v.xi[...].reshape(128, 256), v.spread_m[...]).reshape(4, 2, 16, 256)
    for da in range(3):
        even = v.m4[first + da, 0]
        odd = v.m4[first + da, 1]
        for m, x in enumerate((row_shift(odd, 0), even, odd, row_shift(even, 2))):
            for db in range(3):
                v.fs[m, 3 * da + db] = lane_shift(x, db)

    for copy in sends_x:
        copy.wait_recv()
    own[2].wait()
    for r in range(2):
        for half in range(2):
            sums = [None] * 4
            for j in range(8):
                at = (r * 8 + j) * 4
                x = jnp.concatenate(
                    [
                        jnp.concatenate(
                            [v.xrecv[pl.ds(at + 2 * s + h, 8, stride=64), :] for h in range(2)],
                            axis=1,
                        )
                        for s in range(2)
                    ],
                    axis=0,
                )
                for q in range(4):
                    term = wide4(v.noise[1 + r, 4 * half + q, j]) * x
                    sums[q] = term if j == 0 else sums[q] + term
            for o in range(27):
                x = v.fs[r + o // 9, o % 9]
                for q in range(4):
                    sums[q] = sums[q] + wide4(v.kern[1 + r, 4 * half + q, o]) * x
            for q in range(4):
                v.dv[2 * r + half, q] = jnp.exp(sums[q])

    for copy in sends_e:
        copy.wait_recv()
    own[3].wait()
    spacing = F32(1.0 / (4 * nr))
    cell = 4 * lax.broadcasted_iota(jnp.int32, (8, 256), 0)
    cells = [(cell + j).astype(F32) for j in range(4)]

    def star(kind, n, q):
        at = 4 * n + q
        return jnp.concatenate(
            [
                jnp.broadcast_to(v.star_z[kind, h, at : at + 1, :], (8, 128))
                for h in range(2)
            ],
            axis=1,
        )

    for q in range(4):
        bins = [star(0, n, q) for n in range(4)]
        light = [
            spacing
            * jnp.concatenate(
                [v.erecv[pl.ds(16 * h + 4 * j + q, 8, stride=32), :] for h in range(2)], axis=1
            )
            for j in range(4)
        ]
        for s in range(2):
            rows = slice(8 * s, 8 * s + 8)
            dens = [v.dv[j, q, rows] for j in range(4)]
            layer = [spacing * x for x in dens]
            depth = sums_before((layer[0] + layer[1]) + (layer[2] + layer[3]))
            shine = []
            for j in range(4):
                shine.append(light[j] * jnp.exp(-depth))
                depth = depth + layer[j]
            column = sums_before((shine[0] + shine[1]) + (shine[2] + shine[3]))
            columns = []
            for j in range(4):
                column = column + shine[j]
                columns.append(column)
            weights = [None] * 4
            for n in range(4):
                picked = jnp.where(bins[n] == cells[0], columns[0], none)
                for j in range(1, 4):
                    picked = jnp.where(bins[n] == cells[j], columns[j], picked)
                picked = row_total(picked)
                left = star(1, n, q) - picked
                for h in range(2):
                    at = 8 * n + 4 * s + q
                    v.res_x[h, at : at + 1] = left[0:1, 128 * h : 128 * h + 128]
                for j in range(4):
                    term = jnp.where(bins[n] > cells[j], left * (picked - columns[j]), none)
                    weights[j] = term if n == 0 else weights[j] + term
            for j in range(4):
                v.dv[j, q, rows] = -dens[j] * weights[j]

    pieces = [
        jnp.concatenate([v.res_x[h, pl.ds(cb, 16, stride=2), :] for cb in range(2)], axis=1)
        for h in range(2)
    ]
    spread = permuted(jnp.concatenate(pieces, axis=0), v.spread_m[...])
    for h in range(2):
        for e in range(2):
            c = 2 * h + e
            v.rsend[16 * c : 16 * c + 16] = spread[
                16 * h : 16 * h + 16, 128 * e : 128 * e + 128
            ]
    sends_r = [
        remote(
            v.rsend, part(v.rrecv, i, 64), v.r_send.at[d - 1], v.r_recv.at[d - 1], row_at(d), 0
        )
        for d in range(1, nr)
    ]
    own_r = pltpu.make_async_copy(v.rsend, part(v.rrecv, i, 64), v.self_sem.at[4])
    for copy in sends_r:
        copy.start()
    own_r.start()

    for r in range(2):
        grads = [v.dv[2 * r + c // 4, c % 4] for c in range(8)]
        for j in range(8):
            total = wide4(v.noise[1 + r, 0, j]) * grads[0]
            for c in range(1, 8):
                total = total + wide4(v.noise[1 + r, c, j]) * grads[c]
            for s in range(2):
                for h in range(2):
                    at = ((8 * s + j) * 2 + r) * 2 + h
                    v.gfsend[pl.ds(at, 8, stride=64), :] = total[
                        8 * s : 8 * s + 8, 128 * h : 128 * h + 128
                    ]
        for o in range(27):
            total = wide4(v.kern[1 + r, 0, o]) * grads[0]
            for c in range(1, 8):
                total = total + wide4(v.kern[1 + r, c, o]) * grads[c]
            m = r + o // 9
            if r == 1 and m < 3:
                total = total + v.ws[m, o % 9]
            v.ws[m, o % 9] = total
    sends_f = scatter(v.gfsend, v.gfrecv, v.f_send, v.f_recv, 64)
    own_f = keep_own(v.gfsend, v.gfrecv, 64, v.self_sem.at[5])
    for copy in sends_f:
        copy.start()
    own_f.start()

    pieces = []
    for da in range(3):
        moved = []
        for m in range(4):
            total = v.ws[m, 3 * da + 1]
            total = total + lane_shift(v.ws[m, 3 * da], 2)
            total = total + lane_shift(v.ws[m, 3 * da + 2], 0)
            moved.append(total)
        pieces.append(moved[1] + row_shift(moved[3], 0))
        pieces.append(moved[2] + row_shift(moved[0], 2))
    spread = permuted(jnp.concatenate(pieces, axis=0), v.gather_m[...])
    v.h4[...] = jnp.zeros(v.h4.shape, F32)
    for da in range(3):
        u_inside = 4 * k + low + lax.shift_right_logical(first + da, 1)
        keep = (u_inside >= 0) & (u_inside < 4 * na)
        for cr in range(2):
            n = (2 * da + cr) * 16
            v.h4[first + da, cr] = jnp.where(keep, spread[n : n + 16], none)

    for u in range(2):
        children = []
        for c in range(8):
            lanes = slice(128 * (c % 2), 128 * (c % 2) + 128)
            children.append(v.h4[2 * u + c // 2 % 2, c // 4, :, lanes])
        for j in range(8):
            total = wide(v.noise[0, 0, j]) * children[0]
            for c in range(1, 8):
                total = total + wide(v.noise[0, c, j]) * children[c]
            for s in range(2):
                v.hsend[pl.ds(16 * u + 8 * s + j, 8, stride=40), :] = total[8 * s : 8 * s + 8]
        for o in range(27):
            dr, da, db = o // 9, o // 3 % 3, o % 3
            total = wide(v.kern[0, 0, o]) * children[0]
            for c in range(1, 8):
                total = total + wide(v.kern[0, c, o]) * children[c]
            t = u + da
            if u == 1 and t < 3:
                total = total + v.wq[t, 3 * dr + db]
            v.wq[t, 3 * dr + db] = total
    v.g12[...] = jnp.zeros(v.g12.shape, F32)
    for t in range(4):
        sums = []
        for dr in range(3):
            total = v.wq[t, 3 * dr + 1]
            total = total + lane_shift(v.wq[t, 3 * dr], 2)
            total = total + lane_shift(v.wq[t, 3 * dr + 2], 0)
            sums.append(row_shift(total, 2 - dr))
        v.g12[half_up + 2 + t] = sums[0] + sums[1] + sums[2]
    for a in range(4):
        for s in range(2):
            rows = slice(8 * s, 8 * s + 8)
            v.hsend[pl.ds(32 + 4 * s + a, 8, stride=40), :] = v.g12[4 + a, rows]
            for side in range(2):
                outside = (k > 0) if side == 0 else (k < na - 1)
                v.hedge[side, pl.ds(4 * s + a, 8, stride=8), :] = jnp.where(
                    outside, v.g12[8 * side + a, rows], none
                )
    sends_h = scatter(v.hsend, v.hrecv, v.h_send, v.h_recv, 40)
    own_h = keep_own(v.hsend, v.hrecv, 40, v.self_sem.at[6])
    for copy in sends_h:
        copy.start()
    own_h.start()
    edges = []
    for side, dk in ((0, -1), (1, 1)):
        moves = [
            remote(
                v.hedge.at[side, pl.ds(8 * n, 8)],
                v.gside.at[i if side == 0 else i - 2],
                v.gs_send.at[n],
                v.gs_recv.at[i if side == 0 else i - 2],
                n,
                dk,
            )
            for n in range(nr)
        ]
        edges.append((i <= 2 if side == 0 else i >= 5, moves))
        moves = [
            remote(
                v.hsend.at[pl.ds(40 * n + 16 * side, 16)],
                v.hside.at[side],
                v.hs_send.at[n],
                v.hs_recv.at[side],
                n,
                dk,
            )
            for n in range(nr)
        ]
        edges.append((i == 0 if side == 0 else i == nr - 1, moves))
    for condition, moves in edges:

        @pl.when(condition)
        def _():
            for copy in moves:
                copy.start()

    for copy in sends_r:
        copy.wait_recv()
    own_r.wait()
    for c in range(4):
        for n in range(4):
            for s in range(2):
                for ca in range(2):
                    at = 16 * c + n * 4 + s * 2 + ca
                    v.res_v[c, pl.ds((s * 4 + n) * 16 + ca, 8, stride=2), :] = v.rrecv[
                        pl.ds(at, 8, stride=64), :
                    ]
    for copy in sends_f:
        copy.wait_recv()
    own_f.wait()
    for s in range(2):
        for j in range(8):
            for r in range(2):
                for h in range(2):
                    at = ((8 * s + j) * 2 + r) * 2 + h
                    v.gf_v[s, j, r, :, 128 * h : 128 * h + 128] = v.gfrecv[
                        pl.ds(at, 8, stride=64), :
                    ]
    for copy in sends_h:
        copy.wait_recv()
    own_h.wait()
    for n in range(6):
        arrived(v.gside.at[n], v.gs_recv.at[n])
    for n in range(2):
        arrived(v.hside.at[n], v.hs_recv.at[n])

    def owed(owner, u):
        at = 40 * owner + 16 * u
        return v.hrecv[at : at + 16]

    by_row = [
        owed(1, 0) + owed(2, 0) + owed(0, 1) + v.hside[1],
        owed(3, 0) + owed(4, 0) + owed(1, 1) + owed(2, 1),
        owed(5, 0) + owed(6, 0) + owed(3, 1) + owed(4, 1),
        owed(7, 0) + owed(5, 1) + owed(6, 1) + v.hside[0],
    ]
    for a in range(4):
        v.gm_x[pl.ds(a, 16, stride=4), :] = by_row[a]
    for s in range(2):
        for j in range(8):
            at = 4 * (8 * s + j)
            v.gm_v[s, j] = v.gm_x[at : at + 4]
    total = v.gside[0]
    for n in range(1, 6):
        total = total + v.gside[n]
    for owner in range(nr):
        total = total + v.hrecv[40 * owner + 32 : 40 * owner + 40]
    for s in range(2):
        v.gc_v[s] = total[4 * s : 4 * s + 4]

    for copy in sends_c + sends_n + sends_x + sends_e + sends_r + sends_f + sends_h:
        copy.wait_send()
    for condition, moves in edges:

        @pl.when(condition)
        def _():
            for copy in moves:
                copy.wait_send()


def hand_out(gc_v, gm_v, gf_v, res_v, gc_o, gm_o, gf_o, res_o, sem):
    outs = [
        pltpu.make_async_copy(gf_v, gf_o, sem.at[0]),
        pltpu.make_async_copy(gm_v, gm_o.at[:, :, 0], sem.at[1]),
        pltpu.make_async_copy(gc_v, gc_o.at[:, 0], sem.at[2]),
    ]
    for c in range(4):
        outs.append(
            pltpu.make_async_copy(
                res_v.at[c].reshape(2, 4, 16, 128),
                res_o.at[:, :, :, pl.ds(128 * c, 128)],
                sem.at[3 + c],
            )
        )
    for out in outs:
        out.start()
    for out in outs:
        out.wait()


def per_device(*args):
    nr, na = lax.axis_size("rad"), lax.axis_size("ang")
    args = list(args)
    for n in (4, 7):
        args[n] = args[n].transpose(1, 2, 0)
    held = [(2, 4, 128), (2, 8, 4, 128), (2, 8, 2, 8, 256), (4, 128, 128)]
    shapes = [(2, 1, 4, 128), (2, 8, 1, 4, 128), (2, 8, 2, 8, 256), (2, 4, 16, 512)]
    results = pl.pallas_call(
        functools.partial(kernel, nr, na),
        out_shape=[pltpu.VMEM(shape, F32) for shape in held],
        in_specs=[ANY] * 12,
        out_specs=[VMEM] * 4,
        scratch_shapes=list(SCRATCH.values()),
        compiler_params=pltpu.CompilerParams(collective_id=0, has_side_effects=True),
    )(*args)
    return pl.pallas_call(
        hand_out,
        out_shape=[jax.ShapeDtypeStruct(shape, F32) for shape in shapes],
        in_specs=[VMEM] * 4,
        out_specs=[ANY] * 4,
        scratch_shapes=[pltpu.SemaphoreType.DMA((7,))],
        compiler_params=pltpu.CompilerParams(vmem_limit_bytes=4 << 20),
    )(*results)


def solution(mesh):
    placed = (
        P(None, "rad", "ang", None),
        P(None, None, "rad", "ang", None),
        P(None, None, "rad", "ang", None),
        P(),
        P(),
        P(),
        P(),
        P(),
        P(),
        P("rad", "ang", None),
        P(None, "ang", None),
        P(None, "ang", None),
    )
    return jax.shard_map(
        per_device,
        mesh=mesh,
        in_specs=placed,
        out_specs=(
            P(None, "rad", "ang", None),
            P(None, None, "rad", "ang", None),
            P(None, None, "rad", "ang", None),
            P(None, None, "ang", None),
        ),
        check_vma=False,
    )
```

```python
import functools

import jax
import jax.numpy as jnp
from jax import lax
from jax.experimental import pallas as pl
from jax.experimental.pallas import tpu as pltpu
from jax.sharding import PartitionSpec as P

F32 = jnp.float32
BF16 = jnp.bfloat16
MESH = pl.DeviceIdType.MESH
ANY = pl.BlockSpec(memory_space=pl.ANY)
VMEM = pl.BlockSpec(memory_space=pltpu.VMEM)


def lane_shift(x, step):
    if step == 1:
        return x
    width = x.shape[1]
    lane = lax.broadcasted_iota(jnp.int32, x.shape, 1)
    if step == 0:
        return jnp.where(lane == 0, F32(0.0), pltpu.roll(x, 1, 1))
    return jnp.where(lane == width - 1, F32(0.0), pltpu.roll(x, width - 1, 1))


def permuted(x, permutation):
    high = x.astype(BF16)
    rest = x - high.astype(F32)
    mid = rest.astype(BF16)
    low = (rest - mid.astype(F32)).astype(BF16)

    def times(part):
        return jnp.dot(part, permutation, preferred_element_type=F32)

    return times(high) + times(mid) + times(low)


SCRATCH = dict(
    cf_v=pltpu.VMEM((2, 4, 128), F32),
    exm_v=pltpu.VMEM((2, 8, 4, 128), F32),
    exf_v=pltpu.VMEM((2, 8, 2, 8, 256), F32),
    em_v=pltpu.VMEM((4, 64, 128), F32),
    bins_v=pltpu.VMEM((4, 64, 128), jnp.int32),
    data_v=pltpu.VMEM((4, 64, 128), F32),
    km_v=pltpu.VMEM((16, 8, 27), F32),
    nm_v=pltpu.VMEM((8, 8, 16), F32),
    kf_v=pltpu.VMEM((16, 8, 27), F32),
    nf_v=pltpu.VMEM((8, 8, 16), F32),
    rm_s=pltpu.SMEM((8,), jnp.int32),
    rf_s=pltpu.SMEM((16,), jnp.int32),
    spread_m=pltpu.VMEM((256, 256), BF16),
    gather_m=pltpu.VMEM((256, 256), BF16),
    table=pltpu.VMEM((3, 64, 128), F32),
    kern=pltpu.VMEM((3, 8, 27, 8, 128), F32),
    noise=pltpu.VMEM((3, 8, 8, 8, 128), F32),
    csend=pltpu.VMEM((8, 128), F32),
    crecv=pltpu.VMEM((3, 64, 128), F32),
    nsend=pltpu.VMEM((64, 128), F32),
    nrecv=pltpu.VMEM((256, 128), F32),
    nside=pltpu.VMEM((128, 128), F32),
    xsend=pltpu.VMEM((512, 128), F32),
    xrecv=pltpu.VMEM((512, 128), F32),
    esend=pltpu.VMEM((256, 128), F32),
    erecv=pltpu.VMEM((256, 128), F32),
    c12=pltpu.VMEM((12, 16, 128), F32),
    emx=pltpu.VMEM((4, 8, 16, 128), F32),
    cs=pltpu.VMEM((4, 9, 16, 128), F32),
    xi=pltpu.VMEM((4, 2, 16, 256), F32),
    m4=pltpu.VMEM((4, 2, 16, 256), F32),
    fs=pltpu.VMEM((4, 9, 16, 256), F32),
    dv=pltpu.VMEM((4, 4, 16, 256), F32),
    star_x=pltpu.VMEM((2, 8, 8, 512), F32),
    star_y=pltpu.VMEM((2, 4, 8, 128), F32),
    star_z=pltpu.VMEM((2, 2, 16, 128), F32),
    res_x=pltpu.VMEM((2, 32, 128), F32),
    rsend=pltpu.VMEM((64, 128), F32),
    rrecv=pltpu.VMEM((512, 128), F32),
    ws=pltpu.VMEM((4, 9, 16, 256), F32),
    h4=pltpu.VMEM((4, 2, 16, 256), F32),
    wq=pltpu.VMEM((4, 9, 16, 128), F32),
    g12=pltpu.VMEM((12, 16, 128), F32),
    gfsend=pltpu.VMEM((512, 128), F32),
    gfrecv=pltpu.VMEM((512, 128), F32),
    hsend=pltpu.VMEM((320, 128), F32),
    hrecv=pltpu.VMEM((320, 128), F32),
    hedge=pltpu.VMEM((2, 64, 128), F32),
    hside=pltpu.VMEM((2, 16, 128), F32),
    gside=pltpu.VMEM((6, 8, 128), F32),
    gm_x=pltpu.VMEM((64, 128), F32),
    load_sem=pltpu.SemaphoreType.DMA((12,)),
    send_sem=pltpu.SemaphoreType.DMA((9,)),
    recv_sem=pltpu.SemaphoreType.DMA((12,)),
)
SEND = dict(c=0, n=1, x=2, e=3, r=4, f=5, h=6, gs=7, hs=8)
RECV = dict(c=0, cs=1, n=2, ns=3, x0=4, x1=5, e=6, r=7, f=8, h=9, gs=10, hs=11)
INPUTS = ["cf", "exm", "exf", "km", "nm", "rm", "kf", "nf", "rf", "emi", "bins", "data"]
OUTPUTS = ["gc_v", "gm_v", "gf_v", "res_v"]


class Refs:
    def __init__(self, refs):
        for name, ref in zip(INPUTS + OUTPUTS + list(SCRATCH), refs):
            setattr(self, name, ref)


def wide(x):
    return jnp.concatenate([x, x], axis=0)


def wide4(x):
    x = jnp.concatenate([x, x], axis=1)
    return jnp.concatenate([x, x], axis=0)


def row_shift(x, step):
    if step == 1:
        return x
    parts = []
    for s in range(2):
        part = x[8 * s : 8 * s + 8]
        sub = lax.broadcasted_iota(jnp.int32, part.shape, 0)
        if step == 0:
            part = jnp.where(sub == 0, F32(0.0), pltpu.roll(part, 1, 0))
        else:
            part = jnp.where(sub == 7, F32(0.0), pltpu.roll(part, 7, 0))
        parts.append(part)
    return jnp.concatenate(parts, axis=0)


def sums_before(x):
    sub = lax.broadcasted_iota(jnp.int32, x.shape, 0)
    total = x
    for step in (1, 2, 4):
        total = total + jnp.where(sub < step, F32(0.0), pltpu.roll(total, step, 0))
    return jnp.where(sub == 0, F32(0.0), pltpu.roll(total, 1, 0))


def row_total(x):
    for step in (4, 2, 1):
        x = x + pltpu.roll(x, step, 0)
    return x


def kernel(nr, na, *refs):
    v = Refs(refs)
    i = lax.axis_index("rad")
    k = lax.axis_index("ang")
    half_up = lax.shift_right_logical(i + 1, 1)
    low = half_up - 1
    first = 1 - lax.bitwise_and(i, 1)
    none = F32(0.0)

    def row_at(d):
        return lax.rem(i + d, nr)

    def block_at(dk):
        return lax.rem(k + (dk + na), na)

    def remote(src, dst, group, arrival, row, dk):
        return pltpu.make_async_remote_copy(
            src_ref=src,
            dst_ref=dst,
            send_sem=v.send_sem.at[SEND[group]],
            recv_sem=v.recv_sem.at[RECV[arrival]],
            device_id=(row, block_at(dk)),
            device_id_type=MESH,
        )

    def sent(like, group):
        pltpu.make_async_copy(like, like, v.send_sem.at[SEND[group]]).wait()

    def arrived(like, arrival):
        pltpu.make_async_copy(like, like, v.recv_sem.at[RECV[arrival]]).wait()

    def part(ref, index, size):
        return ref.at[pl.ds(pl.multiple_of(index * size, size), size)]

    def scatter(src, dst, group, size):
        return [
            remote(part(src, row_at(d), size), part(dst, i, size), group, group, row_at(d), 0)
            for d in range(1, nr)
        ]

    def keep_own(src, dst, size):
        own = pl.ds(pl.multiple_of(i * size, size), size)
        dst[own] = src[own]

    loads = [
        [pltpu.make_async_copy(v.exf, v.exf_v, v.load_sem.at[0])],
        [pltpu.make_async_copy(v.exm.at[:, :, 0], v.exm_v, v.load_sem.at[1])],
        [pltpu.make_async_copy(v.cf.at[:, 0], v.cf_v, v.load_sem.at[2])],
    ]
    for n, (src, dst) in enumerate(((v.emi, v.em_v), (v.bins, v.bins_v), (v.data, v.data_v))):
        loads.append(
            [
                pltpu.make_async_copy(
                    src.at[:, :, pl.ds(128 * c, 128)],
                    dst.at[c].reshape(4, 16, 128),
                    v.load_sem.at[3 + n],
                )
                for c in range(4)
            ]
        )
    for n, (src, dst) in enumerate(
        (
            (v.rm, v.rm_s),
            (v.rf, v.rf_s),
            (v.km, v.km_v),
            (v.nm, v.nm_v),
            (v.kf, v.kf_v),
            (v.nf, v.nf_v),
        )
    ):
        loads.append([pltpu.make_async_copy(src, dst, v.load_sem.at[6 + n])])
    for group in loads:
        for load in group:
            load.start()

    barrier = pltpu.get_barrier_semaphore()
    for d in range(1, nr):
        pl.semaphore_signal(barrier, inc=1, device_id=(row_at(d), k), device_id_type=MESH)
    for dk in (-1, 1):
        for d in range(nr):
            pl.semaphore_signal(
                barrier, inc=1, device_id=(d, block_at(dk)), device_id_type=MESH
            )

    for group in loads[:3]:
        group[0].wait()
    for r in range(2):
        for j in range(8):
            for s in range(2):
                for h in range(2):
                    at = ((r * 8 + j) * 2 + s) * 2 + h
                    v.xsend[pl.ds(at, 8, stride=64), :] = v.exf_v[
                        s, j, r, :, 128 * h : 128 * h + 128
                    ]
    for s in range(2):
        v.csend[4 * s : 4 * s + 4] = v.cf_v[s]
        for j in range(8):
            v.nsend[pl.ds(8 * s + j, 4, stride=16), :] = v.exm_v[s, j]

    pl.semaphore_wait(barrier, 3 * nr - 1)

    def start_of(owner):
        return jnp.clip(lax.shift_right_logical(owner + 1, 1) - 1, 0, 2)

    def pair_of(owner):
        return pl.ds(pl.multiple_of(start_of(owner) * 16, 16), 32)

    own8 = pl.ds(pl.multiple_of(i * 8, 8), 8)
    sends = [
        remote(v.csend, v.crecv.at[1, own8], "c", "c", row_at(d), 0) for d in range(1, nr)
    ]
    for side, dk, rows in ((0, 1, (0, 1, 2)), (2, -1, (5, 6, 7))):
        sends += [remote(v.csend, v.crecv.at[side, own8], "c", "cs", to, dk) for to in rows]
    sends += [
        remote(v.nsend.at[pair_of(row_at(d))], part(v.nrecv, i, 32), "n", "n", row_at(d), 0)
        for d in range(1, nr)
    ]
    sends.append(remote(v.nsend.at[48:64], part(v.nside, i, 16), "n", "ns", 0, 1))
    sends.append(remote(v.nsend.at[0:16], part(v.nside, i, 16), "n", "ns", 7, -1))
    for r in range(2):
        for d in range(1, nr):
            src = pl.ds(pl.multiple_of(row_at(d) * 64 + 32 * r, 32), 32)
            dst = pl.ds(pl.multiple_of(i * 64 + 32 * r, 32), 32)
            sends.append(
                remote(v.xsend.at[src], v.xrecv.at[dst], "x", "x0" if r == 0 else "x1", row_at(d), 0)
            )
    for copy in sends:
        copy.start()

    row = lax.broadcasted_iota(jnp.int32, (256, 256), 0)
    col = lax.broadcasted_iota(jnp.int32, (256, 256), 1)
    v.gather_m[...] = jnp.where(
        row == 2 * lax.bitwise_and(col, 127) + lax.shift_right_logical(col, 7), F32(1.0), none
    ).astype(BF16)
    for load in loads[3]:
        load.wait()
    pieces = [
        jnp.concatenate(
            [v.em_v[2 * h + e, pl.ds(16 * rl + ca, 8, stride=2), :] for e in range(2)], axis=1
        )
        for rl in range(4)
        for ca in range(2)
        for h in range(2)
    ]
    pieces = permuted(jnp.concatenate(pieces, axis=0), v.gather_m[...])
    for rl in range(4):
        for ca in range(2):
            for h in range(2):
                n = (rl * 2 + ca) * 2 + h
                for cb in range(2):
                    at = h * 16 + rl * 4 + ca * 2 + cb
                    v.esend[pl.ds(at, 8, stride=32), :] = pieces[
                        8 * n : 8 * n + 8, 128 * cb : 128 * cb + 128
                    ]

    for copy in scatter(v.esend, v.erecv, "e", 32):
        copy.start()

    v.spread_m[...] = jnp.where(
        col == 2 * lax.bitwise_and(row, 127) + lax.shift_right_logical(row, 7), F32(1.0), none
    ).astype(BF16)

    v.crecv[1, own8] = v.csend[...]
    v.nrecv[pl.ds(pl.multiple_of(i * 32, 32), 32)] = v.nsend[pair_of(i)]
    keep_own(v.xsend, v.xrecv, 64)
    keep_own(v.esend, v.erecv, 32)
    for group in loads[4:]:
        for load in group:
            load.wait()

    entry = lax.broadcasted_iota(jnp.int32, (8, 16), 1)
    place = lax.broadcasted_iota(jnp.int32, (8, 16), 0)
    chosen = []
    for x in range(3):
        index = jnp.zeros((8, 16), jnp.int32)
        for cell in range(8):
            if x == 0:
                number = v.rm_s[cell]
                v.table[x, pl.ds(cell, 8, stride=8), 0:27] = v.km_v[number]
            else:
                number = v.rf_s[2 * cell + x - 1]
                v.table[x, pl.ds(cell, 8, stride=8), 0:27] = v.kf_v[number]
            index = jnp.where(place == cell, number, index)
        chosen.append(jnp.where(index == entry, F32(1.0), none).astype(BF16))
    for x in range(3):
        for c in range(8):
            tile = v.table[x, 8 * c : 8 * c + 8]
            for o in range(27):
                v.kern[x, c, o] = jnp.broadcast_to(tile[:, o : o + 1], (8, 128))
        source = (v.nm_v if x == 0 else v.nf_v)[...].reshape(64, 16)
        high = source.astype(BF16)
        rest = source - high.astype(F32)
        mid = rest.astype(BF16)
        least = (rest - mid.astype(F32)).astype(BF16)
        tile = None
        for piece in (high, mid, least):
            term = lax.dot_general(
                chosen[x], piece, (((1,), (1,)), ((), ())), preferred_element_type=F32
            )
            tile = term if tile is None else tile + term
        for c in range(8):
            for j in range(8):
                at = 8 * c + j
                v.noise[x, c, j] = jnp.broadcast_to(tile[:, at : at + 1], (8, 128))

    for n in range(4):
        for ca in range(2):
            for c in range(4):
                at = pl.ds(16 * n + ca, 8, stride=2)
                lanes = pl.ds(128 * c, 128)
                v.star_x[0, :, 2 * n + ca, lanes] = v.bins_v[c, at, :].astype(F32)
                v.star_x[1, :, 2 * n + ca, lanes] = v.data_v[c, at, :]
    for kind in range(2):
        x = v.star_x[kind, i]
        y = permuted(jnp.concatenate([x[:, :256], x[:, 256:]], axis=0), v.gather_m[...])
        for h in range(2):
            for cb in range(2):
                v.star_y[kind, 2 * h + cb] = y[8 * h : 8 * h + 8, 128 * cb : 128 * cb + 128]
        for h in range(2):
            for cb in range(2):
                for ca in range(2):
                    v.star_z[kind, h, pl.ds(2 * ca + cb, 4, stride=4), :] = v.star_y[
                        kind, 2 * h + cb, pl.ds(ca, 4, stride=2), :
                    ]

    arrived(v.crecv.at[1, 0:56], "c")
    arrived(v.nrecv.at[0:224], "n")

    @pl.when((i <= 2) | (i >= 5))
    def _():
        arrived(v.crecv.at[0], "cs")

    @pl.when((i == 0) | (i == nr - 1))
    def _():
        arrived(v.nside, "ns")

    for side in range(3):
        for a in range(4):
            x = jnp.concatenate(
                [v.crecv[side, pl.ds(4 * s + a, 8, stride=8), :] for s in range(2)], axis=0
            )
            if side == 0:
                x = jnp.where(k > 0, x, none)
            if side == 2:
                x = jnp.where(k < na - 1, x, none)
            v.c12[4 * side + a] = x
    for t in range(4):
        x = v.c12[half_up + 2 + t]
        for dr in range(3):
            moved = row_shift(x, dr)
            for db in range(3):
                v.cs[t, 3 * dr + db] = lane_shift(moved, db)
    for j in range(8):
        for n in range(2):
            v.emx[1 + n, j] = jnp.concatenate(
                [v.nrecv[pl.ds(16 * n + 8 * s + j, 8, stride=32), :] for s in range(2)], axis=0
            )
        x = jnp.concatenate(
            [v.nside[pl.ds(8 * s + j, 8, stride=16), :] for s in range(2)], axis=0
        )
        v.emx[0, j] = x
        v.emx[3, j] = x
    base = jnp.where(i > 0, 1, 0) + jnp.where(i == nr - 1, 1, 0)

    def parent_inside(u):
        a = 4 * k + low + u
        return (a >= 0) & (a < 4 * na)

    for u in range(2):
        for cr in range(2):
            sums = [None] * 4
            for j in range(8):
                x = v.emx[base + u, j]
                for q in range(4):
                    term = wide(v.noise[0, 4 * cr + q, j]) * x
                    sums[q] = term if j == 0 else sums[q] + term
            for o in range(27):
                dr, da, db = o // 9, o // 3 % 3, o % 3
                x = v.cs[u + da, 3 * dr + db]
                for q in range(4):
                    sums[q] = sums[q] + wide(v.kern[0, 4 * cr + q, o]) * x
            for q in range(4):
                lanes = slice(128 * (q % 2), 128 * (q % 2) + 128)
                v.xi[2 * u + q // 2, cr, :, lanes] = jnp.where(parent_inside(u), sums[q], none)
    v.m4[...] = permuted(v.xi[...].reshape(128, 256), v.spread_m[...]).reshape(4, 2, 16, 256)
    for da in range(3):
        even = v.m4[first + da, 0]
        odd = v.m4[first + da, 1]
        for m, x in enumerate((row_shift(odd, 0), even, odd, row_shift(even, 2))):
            for db in range(3):
                v.fs[m, 3 * da + db] = lane_shift(x, db)

    for r in range(2):
        arrived(v.xrecv.at[0:224], "x0" if r == 0 else "x1")
        for half in range(2):
            sums = [None] * 4
            for j in range(8):
                at = (r * 8 + j) * 4
                x = jnp.concatenate(
                    [
                        jnp.concatenate(
                            [v.xrecv[pl.ds(at + 2 * s + h, 8, stride=64), :] for h in range(2)],
                            axis=1,
                        )
                        for s in range(2)
                    ],
                    axis=0,
                )
                for q in range(4):
                    term = wide4(v.noise[1 + r, 4 * half + q, j]) * x
                    sums[q] = term if j == 0 else sums[q] + term
            for o in range(27):
                x = v.fs[r + o // 9, o % 9]
                for q in range(4):
                    sums[q] = sums[q] + wide4(v.kern[1 + r, 4 * half + q, o]) * x
            for q in range(4):
                v.dv[2 * r + half, q] = jnp.exp(sums[q])

    arrived(v.erecv.at[0:224], "e")
    spacing = F32(1.0 / (4 * nr))
    cell = 4 * lax.broadcasted_iota(jnp.int32, (8, 256), 0)
    cells = [(cell + j).astype(F32) for j in range(4)]

    def star(kind, n, q):
        at = 4 * n + q
        return jnp.concatenate(
            [
                jnp.broadcast_to(v.star_z[kind, h, at : at + 1, :], (8, 128))
                for h in range(2)
            ],
            axis=1,
        )

    for q in range(4):
        bins = [star(0, n, q) for n in range(4)]
        light = [
            spacing
            * jnp.concatenate(
                [v.erecv[pl.ds(16 * h + 4 * j + q, 8, stride=32), :] for h in range(2)], axis=1
            )
            for j in range(4)
        ]
        for s in range(2):
            rows = slice(8 * s, 8 * s + 8)
            dens = [v.dv[j, q, rows] for j in range(4)]
            layer = [spacing * x for x in dens]
            depth = sums_before((layer[0] + layer[1]) + (layer[2] + layer[3]))
            shine = []
            for j in range(4):
                shine.append(light[j] * jnp.exp(-depth))
                depth = depth + layer[j]
            column = sums_before((shine[0] + shine[1]) + (shine[2] + shine[3]))
            columns = []
            for j in range(4):
                column = column + shine[j]
                columns.append(column)
            weights = [None] * 4
            for n in range(4):
                picked = jnp.where(bins[n] == cells[0], columns[0], none)
                for j in range(1, 4):
                    picked = jnp.where(bins[n] == cells[j], columns[j], picked)
                picked = row_total(picked)
                left = star(1, n, q) - picked
                for h in range(2):
                    at = 8 * n + 4 * s + q
                    v.res_x[h, at : at + 1] = left[0:1, 128 * h : 128 * h + 128]
                for j in range(4):
                    term = jnp.where(bins[n] > cells[j], left * (picked - columns[j]), none)
                    weights[j] = term if n == 0 else weights[j] + term
            for j in range(4):
                v.dv[j, q, rows] = -dens[j] * weights[j]

    pieces = [
        jnp.concatenate([v.res_x[h, pl.ds(cb, 16, stride=2), :] for cb in range(2)], axis=1)
        for h in range(2)
    ]
    spread = permuted(jnp.concatenate(pieces, axis=0), v.spread_m[...])
    for h in range(2):
        for e in range(2):
            c = 2 * h + e
            v.rsend[16 * c : 16 * c + 16] = spread[
                16 * h : 16 * h + 16, 128 * e : 128 * e + 128
            ]
    for d in range(1, nr):
        remote(v.rsend, part(v.rrecv, i, 64), "r", "r", row_at(d), 0).start()
    v.rrecv[pl.ds(pl.multiple_of(i * 64, 64), 64)] = v.rsend[...]

    for r in range(2):
        grads = [v.dv[2 * r + c // 4, c % 4] for c in range(8)]
        for j in range(8):
            total = wide4(v.noise[1 + r, 0, j]) * grads[0]
            for c in range(1, 8):
                total = total + wide4(v.noise[1 + r, c, j]) * grads[c]
            for s in range(2):
                for h in range(2):
                    at = ((8 * s + j) * 2 + r) * 2 + h
                    v.gfsend[pl.ds(at, 8, stride=64), :] = total[
                        8 * s : 8 * s + 8, 128 * h : 128 * h + 128
                    ]
        for o in range(27):
            total = wide4(v.kern[1 + r, 0, o]) * grads[0]
            for c in range(1, 8):
                total = total + wide4(v.kern[1 + r, c, o]) * grads[c]
            m = r + o // 9
            if r == 1 and m < 3:
                total = total + v.ws[m, o % 9]
            v.ws[m, o % 9] = total
    for copy in scatter(v.gfsend, v.gfrecv, "f", 64):
        copy.start()
    keep_own(v.gfsend, v.gfrecv, 64)

    pieces = []
    for da in range(3):
        moved = []
        for m in range(4):
            total = v.ws[m, 3 * da + 1]
            total = total + lane_shift(v.ws[m, 3 * da], 2)
            total = total + lane_shift(v.ws[m, 3 * da + 2], 0)
            moved.append(total)
        pieces.append(moved[1] + row_shift(moved[3], 0))
        pieces.append(moved[2] + row_shift(moved[0], 2))
    spread = permuted(jnp.concatenate(pieces, axis=0), v.gather_m[...])
    v.h4[...] = jnp.zeros(v.h4.shape, F32)
    for da in range(3):
        u_inside = 4 * k + low + lax.shift_right_logical(first + da, 1)
        keep = (u_inside >= 0) & (u_inside < 4 * na)
        for cr in range(2):
            n = (2 * da + cr) * 16
            v.h4[first + da, cr] = jnp.where(keep, spread[n : n + 16], none)

    for u in range(2):
        children = []
        for c in range(8):
            lanes = slice(128 * (c % 2), 128 * (c % 2) + 128)
            children.append(v.h4[2 * u + c // 2 % 2, c // 4, :, lanes])
        for j in range(8):
            total = wide(v.noise[0, 0, j]) * children[0]
            for c in range(1, 8):
                total = total + wide(v.noise[0, c, j]) * children[c]
            for s in range(2):
                v.hsend[pl.ds(16 * u + 8 * s + j, 8, stride=40), :] = total[8 * s : 8 * s + 8]
        for o in range(27):
            dr, da, db = o // 9, o // 3 % 3, o % 3
            total = wide(v.kern[0, 0, o]) * children[0]
            for c in range(1, 8):
                total = total + wide(v.kern[0, c, o]) * children[c]
            t = u + da
            if u == 1 and t < 3:
                total = total + v.wq[t, 3 * dr + db]
            v.wq[t, 3 * dr + db] = total
    v.g12[...] = jnp.zeros(v.g12.shape, F32)
    for t in range(4):
        sums = []
        for dr in range(3):
            total = v.wq[t, 3 * dr + 1]
            total = total + lane_shift(v.wq[t, 3 * dr], 2)
            total = total + lane_shift(v.wq[t, 3 * dr + 2], 0)
            sums.append(row_shift(total, 2 - dr))
        v.g12[half_up + 2 + t] = sums[0] + sums[1] + sums[2]
    for a in range(4):
        for s in range(2):
            rows = slice(8 * s, 8 * s + 8)
            v.hsend[pl.ds(32 + 4 * s + a, 8, stride=40), :] = v.g12[4 + a, rows]
            for side in range(2):
                outside = (k > 0) if side == 0 else (k < na - 1)
                v.hedge[side, pl.ds(4 * s + a, 8, stride=8), :] = jnp.where(
                    outside, v.g12[8 * side + a, rows], none
                )
    for copy in scatter(v.hsend, v.hrecv, "h", 40):
        copy.start()
    keep_own(v.hsend, v.hrecv, 40)
    for side, dk in ((0, -1), (1, 1)):

        @pl.when(i <= 2 if side == 0 else i >= 5)
        def _():
            place = i if side == 0 else i - 2
            for n in range(nr):
                remote(
                    v.hedge.at[side, pl.ds(8 * n, 8)], v.gside.at[place], "gs", "gs", n, dk
                ).start()

        @pl.when(i == 0 if side == 0 else i == nr - 1)
        def _():
            for n in range(nr):
                remote(
                    v.hsend.at[pl.ds(40 * n + 16 * side, 16)], v.hside.at[side], "hs", "hs", n, dk
                ).start()

    arrived(v.rrecv.at[0:448], "r")
    for c in range(4):
        for n in range(4):
            for s in range(2):
                for ca in range(2):
                    at = 16 * c + n * 4 + s * 2 + ca
                    v.res_v[c, pl.ds((s * 4 + n) * 16 + ca, 8, stride=2), :] = v.rrecv[
                        pl.ds(at, 8, stride=64), :
                    ]
    arrived(v.gfrecv.at[0:448], "f")
    for s in range(2):
        for j in range(8):
            for r in range(2):
                for h in range(2):
                    at = ((8 * s + j) * 2 + r) * 2 + h
                    v.gf_v[s, j, r, :, 128 * h : 128 * h + 128] = v.gfrecv[
                        pl.ds(at, 8, stride=64), :
                    ]
    arrived(v.hrecv.at[0:280], "h")
    arrived(v.gside, "gs")
    arrived(v.hside, "hs")

    def owed(owner, u):
        at = 40 * owner + 16 * u
        return v.hrecv[at : at + 16]

    by_row = [
        owed(1, 0) + owed(2, 0) + owed(0, 1) + v.hside[1],
        owed(3, 0) + owed(4, 0) + owed(1, 1) + owed(2, 1),
        owed(5, 0) + owed(6, 0) + owed(3, 1) + owed(4, 1),
        owed(7, 0) + owed(5, 1) + owed(6, 1) + v.hside[0],
    ]
    for a in range(4):
        v.gm_x[pl.ds(a, 16, stride=4), :] = by_row[a]
    for s in range(2):
        for j in range(8):
            at = 4 * (8 * s + j)
            v.gm_v[s, j] = v.gm_x[at : at + 4]
    total = v.gside[0]
    for n in range(1, 6):
        total = total + v.gside[n]
    for owner in range(nr):
        total = total + v.hrecv[40 * owner + 32 : 40 * owner + 40]
    for s in range(2):
        v.gc_v[s] = total[4 * s : 4 * s + 4]

    sent(v.xsend.at[0:104], "c")
    sent(v.xsend.at[0:256], "n")
    sent(v.xsend.at[0:448], "x")
    sent(v.xsend.at[0:224], "e")
    sent(v.xsend.at[0:448], "r")
    sent(v.xsend.at[0:448], "f")
    sent(v.xsend.at[0:280], "h")

    @pl.when((i <= 2) | (i >= 5))
    def _():
        sent(v.xsend.at[0:64], "gs")

    @pl.when((i == 0) | (i == nr - 1))
    def _():
        sent(v.xsend.at[0:128], "hs")


def hand_out(gc_v, gm_v, gf_v, res_v, gc_o, gm_o, gf_o, res_o, sem):
    outs = [
        pltpu.make_async_copy(gf_v, gf_o, sem.at[0]),
        pltpu.make_async_copy(gm_v, gm_o.at[:, :, 0], sem.at[1]),
        pltpu.make_async_copy(gc_v, gc_o.at[:, 0], sem.at[2]),
    ]
    for c in range(4):
        outs.append(
            pltpu.make_async_copy(
                res_v.at[c].reshape(2, 4, 16, 128),
                res_o.at[:, :, :, pl.ds(128 * c, 128)],
                sem.at[3 + c],
            )
        )
    for out in outs:
        out.start()
    for out in outs:
        out.wait()


def per_device(*args):
    nr, na = lax.axis_size("rad"), lax.axis_size("ang")
    args = list(args)
    for n in (4, 7):
        args[n] = args[n].transpose(1, 2, 0)
    held = [(2, 4, 128), (2, 8, 4, 128), (2, 8, 2, 8, 256), (4, 128, 128)]
    shapes = [(2, 1, 4, 128), (2, 8, 1, 4, 128), (2, 8, 2, 8, 256), (2, 4, 16, 512)]
    results = pl.pallas_call(
        functools.partial(kernel, nr, na),
        out_shape=[pltpu.VMEM(shape, F32) for shape in held],
        in_specs=[ANY] * 12,
        out_specs=[VMEM] * 4,
        scratch_shapes=list(SCRATCH.values()),
        compiler_params=pltpu.CompilerParams(collective_id=0, has_side_effects=True),
    )(*args)
    return pl.pallas_call(
        hand_out,
        out_shape=[jax.ShapeDtypeStruct(shape, F32) for shape in shapes],
        in_specs=[VMEM] * 4,
        out_specs=[ANY] * 4,
        scratch_shapes=[pltpu.SemaphoreType.DMA((7,))],
        compiler_params=pltpu.CompilerParams(vmem_limit_bytes=4 << 20),
    )(*results)


def solution(mesh):
    placed = (
        P(None, "rad", "ang", None),
        P(None, None, "rad", "ang", None),
        P(None, None, "rad", "ang", None),
        P(),
        P(),
        P(),
        P(),
        P(),
        P(),
        P("rad", "ang", None),
        P(None, "ang", None),
        P(None, "ang", None),
    )
    return jax.shard_map(
        per_device,
        mesh=mesh,
        in_specs=placed,
        out_specs=(
            P(None, "rad", "ang", None),
            P(None, None, "rad", "ang", None),
            P(None, None, "rad", "ang", None),
            P(None, None, "ang", None),
        ),
        check_vma=False,
    )
```

```python
import functools

import jax
import jax.numpy as jnp
from jax import lax
from jax.experimental import pallas as pl
from jax.experimental.pallas import tpu as pltpu
from jax.sharding import PartitionSpec as P

F32 = jnp.float32
BF16 = jnp.bfloat16
MESH = pl.DeviceIdType.MESH
ANY = pl.BlockSpec(memory_space=pl.ANY)
VMEM = pl.BlockSpec(memory_space=pltpu.VMEM)


def lane_shift(x, step):
    if step == 1:
        return x
    width = x.shape[1]
    lane = lax.broadcasted_iota(jnp.int32, x.shape, 1)
    if step == 0:
        return jnp.where(lane == 0, F32(0.0), pltpu.roll(x, 1, 1))
    return jnp.where(lane == width - 1, F32(0.0), pltpu.roll(x, width - 1, 1))


def permuted(x, permutation):
    high = x.astype(BF16)
    rest = x - high.astype(F32)
    mid = rest.astype(BF16)
    low = (rest - mid.astype(F32)).astype(BF16)

    def times(part):
        return jnp.dot(part, permutation, preferred_element_type=F32)

    return times(high) + times(mid) + times(low)


SCRATCH = dict(
    cf_v=pltpu.VMEM((2, 4, 128), F32),
    exm_v=pltpu.VMEM((2, 8, 4, 128), F32),
    exf_v=pltpu.VMEM((2, 8, 2, 8, 256), F32),
    em_v=pltpu.VMEM((4, 64, 128), F32),
    bins_v=pltpu.VMEM((4, 64, 128), jnp.int32),
    data_v=pltpu.VMEM((4, 64, 128), F32),
    km_v=pltpu.VMEM((16, 8, 27), F32),
    nm_v=pltpu.VMEM((8, 8, 16), F32),
    kf_v=pltpu.VMEM((16, 8, 27), F32),
    nf_v=pltpu.VMEM((8, 8, 16), F32),
    rm_s=pltpu.SMEM((8,), jnp.int32),
    rf_s=pltpu.SMEM((16,), jnp.int32),
    spread_m=pltpu.VMEM((256, 256), BF16),
    gather_m=pltpu.VMEM((256, 256), BF16),
    table=pltpu.VMEM((3, 64, 128), F32),
    kern=pltpu.VMEM((3, 8, 27, 8, 128), F32),
    noise=pltpu.VMEM((3, 8, 8, 8, 128), F32),
    csend=pltpu.VMEM((8, 128), F32),
    crecv=pltpu.VMEM((3, 64, 128), F32),
    nsend=pltpu.VMEM((64, 128), F32),
    nrecv=pltpu.VMEM((256, 128), F32),
    nside=pltpu.VMEM((128, 128), F32),
    xsend=pltpu.VMEM((512, 128), F32),
    xrecv=pltpu.VMEM((512, 128), F32),
    esend=pltpu.VMEM((256, 128), F32),
    erecv=pltpu.VMEM((256, 128), F32),
    c12=pltpu.VMEM((12, 2, 8, 128), F32),
    emx=pltpu.VMEM((4, 8, 8, 128), F32),
    cs=pltpu.VMEM((4, 9, 8, 128), F32),
    xi=pltpu.VMEM((4, 2, 8, 256), F32),
    m4=pltpu.VMEM((4, 2, 8, 256), F32),
    fs=pltpu.VMEM((4, 9, 8, 256), F32),
    dv=pltpu.VMEM((4, 4, 8, 256), F32),
    star_x=pltpu.VMEM((2, 8, 8, 512), F32),
    star_y=pltpu.VMEM((2, 4, 8, 128), F32),
    star_z=pltpu.VMEM((2, 2, 16, 128), F32),
    res_x=pltpu.VMEM((2, 16, 128), F32),
    rsend=pltpu.VMEM((64, 128), F32),
    rrecv=pltpu.VMEM((512, 128), F32),
    ws=pltpu.VMEM((4, 9, 8, 256), F32),
    h4=pltpu.VMEM((4, 2, 8, 256), F32),
    wq=pltpu.VMEM((4, 9, 8, 128), F32),
    g12=pltpu.VMEM((12, 8, 128), F32),
    gfsend=pltpu.VMEM((512, 128), F32),
    gfrecv=pltpu.VMEM((512, 128), F32),
    hsend=pltpu.VMEM((320, 128), F32),
    hrecv=pltpu.VMEM((320, 128), F32),
    hedge=pltpu.VMEM((2, 64, 128), F32),
    hside=pltpu.VMEM((2, 2, 8, 128), F32),
    gside=pltpu.VMEM((6, 8, 128), F32),
    gm_x=pltpu.VMEM((64, 128), F32),
    load_sem=pltpu.SemaphoreType.DMA((12,)),
    send_sem=pltpu.SemaphoreType.DMA((9,)),
    recv_sem=pltpu.SemaphoreType.DMA((17,)),
)
SEND = dict(c=0, n=1, x=2, e=3, r=4, f=5, h=6, gs=7, hs=8)
RECV = {
    name: number
    for number, name in enumerate(
        ["c", "cs", "n0", "n1", "ns0", "ns1", "x0", "x1", "e"]
        + ["r0", "r1", "f0", "f1", "h0", "h1", "gs", "hs"]
    )
}
INPUTS = ["cf", "exm", "exf", "km", "nm", "rm", "kf", "nf", "rf", "emi", "bins", "data"]
OUTPUTS = ["gc_v", "gm_v", "gf_v", "res_v"]


class Refs:
    def __init__(self, refs):
        for name, ref in zip(INPUTS + OUTPUTS + list(SCRATCH), refs):
            setattr(self, name, ref)


def wide(x):
    return jnp.concatenate([x, x], axis=1)


def row_shift(x, step):
    if step == 1:
        return x
    sub = lax.broadcasted_iota(jnp.int32, x.shape, 0)
    if step == 0:
        return jnp.where(sub == 0, F32(0.0), pltpu.roll(x, 1, 0))
    return jnp.where(sub == 7, F32(0.0), pltpu.roll(x, 7, 0))


def weighted(weights, values):
    total = weights[0] * values[0]
    for weight, value in zip(weights[1:], values[1:]):
        total = total + weight * value
    return total


def sums_before(x):
    sub = lax.broadcasted_iota(jnp.int32, x.shape, 0)
    total = x
    for step in (1, 2, 4):
        total = total + jnp.where(sub < step, F32(0.0), pltpu.roll(total, step, 0))
    return jnp.where(sub == 0, F32(0.0), pltpu.roll(total, 1, 0))


def row_total(x):
    for step in (4, 2, 1):
        x = x + pltpu.roll(x, step, 0)
    return x


def kernel(nr, na, *refs):
    v = Refs(refs)
    i = lax.axis_index("rad")
    k = lax.axis_index("ang")
    half_up = lax.shift_right_logical(i + 1, 1)
    low = half_up - 1
    first = 1 - lax.bitwise_and(i, 1)
    none = F32(0.0)

    def row_at(d):
        return lax.rem(i + d, nr)

    def block_at(dk):
        return lax.rem(k + (dk + na), na)

    def remote(src, dst, group, arrival, row, dk):
        return pltpu.make_async_remote_copy(
            src_ref=src,
            dst_ref=dst,
            send_sem=v.send_sem.at[SEND[group]],
            recv_sem=v.recv_sem.at[RECV[arrival]],
            device_id=(row, block_at(dk)),
            device_id_type=MESH,
        )

    def sent(like, group):
        pltpu.make_async_copy(like, like, v.send_sem.at[SEND[group]]).wait()

    def arrived(like, arrival):
        pltpu.make_async_copy(like, like, v.recv_sem.at[RECV[arrival]]).wait()

    def part(ref, index, size):
        return ref.at[pl.ds(pl.multiple_of(index * size, size), size)]

    def rows_of(index, size, offset):
        return pl.ds(pl.multiple_of(index * size + offset, 8), size)

    def scatter(src, dst, group, arrival, size, offset=0):
        for d in range(1, nr):
            remote(
                src.at[rows_of(row_at(d), size, offset)],
                dst.at[rows_of(i, size, offset)],
                group,
                arrival,
                row_at(d),
                0,
            ).start()

    def keep_own(src, dst, size, offset=0):
        own = rows_of(i, size, offset)
        dst[own] = src[own]

    loads = [
        [pltpu.make_async_copy(v.exf, v.exf_v, v.load_sem.at[0])],
        [pltpu.make_async_copy(v.exm.at[:, :, 0], v.exm_v, v.load_sem.at[1])],
        [pltpu.make_async_copy(v.cf.at[:, 0], v.cf_v, v.load_sem.at[2])],
    ]
    for n, (src, dst) in enumerate(((v.emi, v.em_v), (v.bins, v.bins_v), (v.data, v.data_v))):
        loads.append(
            [
                pltpu.make_async_copy(
                    src.at[:, :, pl.ds(128 * c, 128)],
                    dst.at[c].reshape(4, 16, 128),
                    v.load_sem.at[3 + n],
                )
                for c in range(4)
            ]
        )
    for n, (src, dst) in enumerate(
        (
            (v.rm, v.rm_s),
            (v.rf, v.rf_s),
            (v.km, v.km_v),
            (v.nm, v.nm_v),
            (v.kf, v.kf_v),
            (v.nf, v.nf_v),
        )
    ):
        loads.append([pltpu.make_async_copy(src, dst, v.load_sem.at[6 + n])])
    for group in loads:
        for load in group:
            load.start()

    barrier = pltpu.get_barrier_semaphore()
    for d in range(1, nr):
        pl.semaphore_signal(barrier, inc=1, device_id=(row_at(d), k), device_id_type=MESH)
    for dk in (-1, 1):
        for d in range(nr):
            pl.semaphore_signal(
                barrier, inc=1, device_id=(d, block_at(dk)), device_id_type=MESH
            )

    for group in loads[:3]:
        group[0].wait()
    for s in range(2):
        v.csend[4 * s : 4 * s + 4] = v.cf_v[s]
        for j in range(8):
            v.nsend[pl.ds(32 * s + j, 4, stride=8), :] = v.exm_v[s, j]
    for s in range(2):
        for r in range(2):
            for j in range(8):
                for h in range(2):
                    at = 256 * s + (r * 8 + j) * 2 + h
                    v.xsend[pl.ds(at, 8, stride=32), :] = v.exf_v[
                        s, j, r, :, 128 * h : 128 * h + 128
                    ]

    pl.semaphore_wait(barrier, 3 * nr - 1)

    def start_of(owner):
        return jnp.clip(lax.shift_right_logical(owner + 1, 1) - 1, 0, 2)

    def pair_of(owner, s):
        return pl.ds(pl.multiple_of(start_of(owner) * 8 + 32 * s, 8), 16)

    own8 = rows_of(i, 8, 0)
    for d in range(1, nr):
        remote(v.csend, v.crecv.at[1, own8], "c", "c", row_at(d), 0).start()
    for side, dk, rows in ((0, 1, (0, 1, 2)), (2, -1, (5, 6, 7))):
        for to in rows:
            remote(v.csend, v.crecv.at[side, own8], "c", "cs", to, dk).start()

    def send_sample(s):
        for d in range(1, nr):
            remote(
                v.nsend.at[pair_of(row_at(d), s)],
                v.nrecv.at[rows_of(i, 16, 128 * s)],
                "n",
                f"n{s}",
                row_at(d),
                0,
            ).start()
        there = v.nside.at[rows_of(i, 8, 64 * s)]
        remote(v.nsend.at[32 * s + 24 : 32 * s + 32], there, "n", f"ns{s}", 0, 1).start()
        remote(v.nsend.at[32 * s : 32 * s + 8], there, "n", f"ns{s}", 7, -1).start()
        scatter(v.xsend, v.xrecv, "x", f"x{s}", 32, 256 * s)

    send_sample(0)

    row = lax.broadcasted_iota(jnp.int32, (256, 256), 0)
    col = lax.broadcasted_iota(jnp.int32, (256, 256), 1)
    v.gather_m[...] = jnp.where(
        row == 2 * lax.bitwise_and(col, 127) + lax.shift_right_logical(col, 7), F32(1.0), none
    ).astype(BF16)
    for load in loads[3]:
        load.wait()
    pieces = [
        jnp.concatenate(
            [v.em_v[2 * h + e, pl.ds(16 * rl + ca, 8, stride=2), :] for e in range(2)], axis=1
        )
        for rl in range(4)
        for ca in range(2)
        for h in range(2)
    ]
    pieces = permuted(jnp.concatenate(pieces, axis=0), v.gather_m[...])
    for rl in range(4):
        for ca in range(2):
            for h in range(2):
                n = (rl * 2 + ca) * 2 + h
                for cb in range(2):
                    at = h * 16 + rl * 4 + ca * 2 + cb
                    v.esend[pl.ds(at, 8, stride=32), :] = pieces[
                        8 * n : 8 * n + 8, 128 * cb : 128 * cb + 128
                    ]

    scatter(v.esend, v.erecv, "e", "e", 32)
    send_sample(1)

    v.spread_m[...] = jnp.where(
        col == 2 * lax.bitwise_and(row, 127) + lax.shift_right_logical(row, 7), F32(1.0), none
    ).astype(BF16)

    v.crecv[1, own8] = v.csend[...]
    for s in range(2):
        v.nrecv[rows_of(i, 16, 128 * s)] = v.nsend[pair_of(i, s)]
        keep_own(v.xsend, v.xrecv, 32, 256 * s)
    keep_own(v.esend, v.erecv, 32)
    for group in loads[4:]:
        for load in group:
            load.wait()

    entry = lax.broadcasted_iota(jnp.int32, (8, 16), 1)
    place = lax.broadcasted_iota(jnp.int32, (8, 16), 0)
    chosen = []
    for x in range(3):
        index = jnp.zeros((8, 16), jnp.int32)
        for cell in range(8):
            if x == 0:
                number = v.rm_s[cell]
                v.table[x, pl.ds(cell, 8, stride=8), 0:27] = v.km_v[number]
            else:
                number = v.rf_s[2 * cell + x - 1]
                v.table[x, pl.ds(cell, 8, stride=8), 0:27] = v.kf_v[number]
            index = jnp.where(place == cell, number, index)
        chosen.append(jnp.where(index == entry, F32(1.0), none).astype(BF16))
    for x in range(3):
        for c in range(8):
            tile = v.table[x, 8 * c : 8 * c + 8]
            for o in range(27):
                v.kern[x, c, o] = jnp.broadcast_to(tile[:, o : o + 1], (8, 128))
        source = (v.nm_v if x == 0 else v.nf_v)[...].reshape(64, 16)
        high = source.astype(BF16)
        rest = source - high.astype(F32)
        mid = rest.astype(BF16)
        least = (rest - mid.astype(F32)).astype(BF16)
        tile = None
        for piece in (high, mid, least):
            term = lax.dot_general(
                chosen[x], piece, (((1,), (1,)), ((), ())), preferred_element_type=F32
            )
            tile = term if tile is None else tile + term
        for c in range(8):
            for j in range(8):
                at = 8 * c + j
                v.noise[x, c, j] = jnp.broadcast_to(tile[:, at : at + 1], (8, 128))

    for n in range(4):
        for ca in range(2):
            for c in range(4):
                at = pl.ds(16 * n + ca, 8, stride=2)
                lanes = pl.ds(128 * c, 128)
                v.star_x[0, :, 2 * n + ca, lanes] = v.bins_v[c, at, :].astype(F32)
                v.star_x[1, :, 2 * n + ca, lanes] = v.data_v[c, at, :]
    for kind in range(2):
        x = v.star_x[kind, i]
        y = permuted(jnp.concatenate([x[:, :256], x[:, 256:]], axis=0), v.gather_m[...])
        for h in range(2):
            for cb in range(2):
                v.star_y[kind, 2 * h + cb] = y[8 * h : 8 * h + 8, 128 * cb : 128 * cb + 128]
        for h in range(2):
            for cb in range(2):
                for ca in range(2):
                    v.star_z[kind, h, pl.ds(2 * ca + cb, 4, stride=4), :] = v.star_y[
                        kind, 2 * h + cb, pl.ds(ca, 4, stride=2), :
                    ]

    arrived(v.crecv.at[1, 0:56], "c")

    @pl.when((i <= 2) | (i >= 5))
    def _():
        arrived(v.crecv.at[0], "cs")

    for side in range(3):
        for a in range(4):
            for s in range(2):
                x = v.crecv[side, pl.ds(4 * s + a, 8, stride=8), :]
                if side == 0:
                    x = jnp.where(k > 0, x, none)
                if side == 2:
                    x = jnp.where(k < na - 1, x, none)
                v.c12[4 * side + a, s] = x
    base = jnp.where(i > 0, 1, 0) + jnp.where(i == nr - 1, 1, 0)
    spacing = F32(1.0 / (4 * nr))
    cell = 4 * lax.broadcasted_iota(jnp.int32, (8, 256), 0)
    cells = [(cell + j).astype(F32) for j in range(4)]

    def parent_inside(u):
        a = 4 * k + low + u
        return (a >= 0) & (a < 4 * na)

    def star(kind, n, q):
        at = 4 * n + q
        return jnp.concatenate(
            [
                jnp.broadcast_to(v.star_z[kind, h, at : at + 1, :], (8, 128))
                for h in range(2)
            ],
            axis=1,
        )

    def spread_out(sums):
        total = lane_shift(sums[1], 1)
        total = total + lane_shift(sums[0], 2)
        return total + lane_shift(sums[2], 0)

    def forward(s):
        for t in range(4):
            x = v.c12[half_up + 2 + t, s]
            for dr in range(3):
                moved = row_shift(x, dr)
                for db in range(3):
                    v.cs[t, 3 * dr + db] = lane_shift(moved, db)
        arrived(v.nrecv.at[0:112], f"n{s}")

        @pl.when((i == 0) | (i == nr - 1))
        def _():
            arrived(v.nside.at[0:64], f"ns{s}")

        for j in range(8):
            for n in range(2):
                v.emx[1 + n, j] = v.nrecv[pl.ds(128 * s + 8 * n + j, 8, stride=16), :]
            x = v.nside[pl.ds(64 * s + j, 8, stride=8), :]
            v.emx[0, j] = x
            v.emx[3, j] = x
        sums = [[None] * 8, [None] * 8]
        for j in range(8):
            x = [v.emx[base + u, j] for u in range(2)]
            for c in range(8):
                weight = v.noise[0, c, j]
                for u in range(2):
                    term = weight * x[u]
                    sums[u][c] = term if j == 0 else sums[u][c] + term
        for o in range(27):
            dr, da, db = o // 9, o // 3 % 3, o % 3
            x = [v.cs[u + da, 3 * dr + db] for u in range(2)]
            for c in range(8):
                weight = v.kern[0, c, o]
                for u in range(2):
                    sums[u][c] = sums[u][c] + weight * x[u]
        for u in range(2):
            for c in range(8):
                lanes = slice(128 * (c % 2), 128 * (c % 2) + 128)
                v.xi[2 * u + c // 2 % 2, c // 4, :, lanes] = jnp.where(
                    parent_inside(u), sums[u][c], none
                )
        v.m4[...] = permuted(v.xi[...].reshape(64, 256), v.spread_m[...]).reshape(4, 2, 8, 256)
        for da in range(3):
            even = v.m4[first + da, 0]
            odd = v.m4[first + da, 1]
            for m, x in enumerate((row_shift(odd, 0), even, odd, row_shift(even, 2))):
                for db in range(3):
                    v.fs[m, 3 * da + db] = lane_shift(x, db)

        arrived(v.xrecv.at[0:224], f"x{s}")
        for r in range(2):
            sums = [None] * 8
            for j in range(8):
                at = 256 * s + (r * 8 + j) * 2
                x = jnp.concatenate(
                    [v.xrecv[pl.ds(at + h, 8, stride=32), :] for h in range(2)], axis=1
                )
                for c in range(8):
                    term = wide(v.noise[1 + r, c, j]) * x
                    sums[c] = term if j == 0 else sums[c] + term
            for o in range(27):
                x = v.fs[r + o // 9, o % 9]
                for c in range(8):
                    sums[c] = sums[c] + wide(v.kern[1 + r, c, o]) * x
            for c in range(8):
                v.dv[2 * r + c // 4, c % 4] = jnp.exp(sums[c])

    def along(s):
        for q in range(4):
            bins = [star(0, n, q) for n in range(4)]
            light = [
                spacing
                * jnp.concatenate(
                    [v.erecv[pl.ds(16 * h + 4 * j + q, 8, stride=32), :] for h in range(2)], axis=1
                )
                for j in range(4)
            ]
            dens = [v.dv[j, q] for j in range(4)]
            layer = [spacing * x for x in dens]
            depth = sums_before((layer[0] + layer[1]) + (layer[2] + layer[3]))
            shine = []
            for j in range(4):
                shine.append(light[j] * jnp.exp(-depth))
                depth = depth + layer[j]
            column = sums_before((shine[0] + shine[1]) + (shine[2] + shine[3]))
            columns = []
            for j in range(4):
                column = column + shine[j]
                columns.append(column)
            weights = [None] * 4
            for n in range(4):
                picked = jnp.where(bins[n] == cells[0], columns[0], none)
                for j in range(1, 4):
                    picked = jnp.where(bins[n] == cells[j], columns[j], picked)
                picked = row_total(picked)
                left = star(1, n, q) - picked
                for h in range(2):
                    at = 4 * n + q
                    v.res_x[h, at : at + 1] = left[0:1, 128 * h : 128 * h + 128]
                for j in range(4):
                    term = jnp.where(bins[n] > cells[j], left * (picked - columns[j]), none)
                    weights[j] = term if n == 0 else weights[j] + term
            for j in range(4):
                v.dv[j, q] = -dens[j] * weights[j]

        pieces = [
            jnp.concatenate([v.res_x[h, pl.ds(cb, 8, stride=2), :] for cb in range(2)], axis=1)
            for h in range(2)
        ]
        spread = permuted(jnp.concatenate(pieces, axis=0), v.spread_m[...])
        for h in range(2):
            for e in range(2):
                at = 32 * s + 8 * (2 * h + e)
                v.rsend[at : at + 8] = spread[8 * h : 8 * h + 8, 128 * e : 128 * e + 128]
        mine = v.rsend.at[32 * s : 32 * s + 32]
        there = rows_of(i, 32, 256 * s)
        for d in range(1, nr):
            remote(mine, v.rrecv.at[there], "r", f"r{s}", row_at(d), 0).start()
        v.rrecv[there] = mine[...]

    def backward(s):
        for r in range(2):
            grads = [v.dv[2 * r + c // 4, c % 4] for c in range(8)]
            for j in range(8):
                total = weighted([wide(v.noise[1 + r, c, j]) for c in range(8)], grads)
                for h in range(2):
                    at = 256 * s + (2 * j + r) * 2 + h
                    v.gfsend[pl.ds(at, 8, stride=32), :] = total[:, 128 * h : 128 * h + 128]
            for o in range(27):
                total = weighted([wide(v.kern[1 + r, c, o]) for c in range(8)], grads)
                m = r + o // 9
                if r == 1 and m < 3:
                    total = total + v.ws[m, o % 9]
                v.ws[m, o % 9] = total
        scatter(v.gfsend, v.gfrecv, "f", f"f{s}", 32, 256 * s)
        keep_own(v.gfsend, v.gfrecv, 32, 256 * s)

        pieces = []
        for da in range(3):
            moved = [spread_out([v.ws[m, 3 * da + db] for db in range(3)]) for m in range(4)]
            pieces.append(moved[1] + row_shift(moved[3], 0))
            pieces.append(moved[2] + row_shift(moved[0], 2))
        spread = permuted(jnp.concatenate(pieces, axis=0), v.gather_m[...])
        v.h4[...] = jnp.zeros(v.h4.shape, F32)
        for da in range(3):
            keep = parent_inside(lax.shift_right_logical(first + da, 1))
            for cr in range(2):
                n = (2 * da + cr) * 8
                v.h4[first + da, cr] = jnp.where(keep, spread[n : n + 8], none)

        children = []
        for u in range(2):
            children.append([])
            for c in range(8):
                lanes = slice(128 * (c % 2), 128 * (c % 2) + 128)
                children[u].append(v.h4[2 * u + c // 2 % 2, c // 4, :, lanes])
        size = 16 + 8 * s
        for j in range(8):
            weights = [v.noise[0, c, j] for c in range(8)]
            for u in range(2):
                v.hsend[pl.ds(128 * s + 8 * u + j, 8, stride=size), :] = weighted(
                    weights, children[u]
                )
        for dr in range(3):
            for db in range(3):
                sums = [None] * 4
                for da in range(3):
                    o = 9 * dr + 3 * da + db
                    weights = [v.kern[0, c, o] for c in range(8)]
                    for u in range(2):
                        total = weighted(weights, children[u])
                        t = u + da
                        sums[t] = total if sums[t] is None else sums[t] + total
                for t in range(4):
                    v.wq[t, 3 * dr + db] = sums[t]
        v.g12[...] = jnp.zeros(v.g12.shape, F32)
        for t in range(4):
            total = None
            for dr in range(3):
                term = spread_out([v.wq[t, 3 * dr + db] for db in range(3)])
                term = row_shift(term, 2 - dr)
                total = term if total is None else total + term
            v.g12[half_up + 2 + t] = total
        for a in range(4):
            v.hsend[pl.ds(128 + 16 + 4 * s + a, 8, stride=24), :] = v.g12[4 + a]
            for side in range(2):
                outside = (k > 0) if side == 0 else (k < na - 1)
                v.hedge[side, pl.ds(4 * s + a, 8, stride=8), :] = jnp.where(
                    outside, v.g12[8 * side + a], none
                )
        scatter(v.hsend, v.hrecv, "h", f"h{s}", size, 128 * s)
        keep_own(v.hsend, v.hrecv, size, 128 * s)
        for side, dk in ((0, -1), (1, 1)):

            @pl.when(i == 0 if side == 0 else i == nr - 1)
            def _():
                for n in range(nr):
                    at = 128 * s + size * n + 8 * side
                    remote(
                        v.hsend.at[at : at + 8], v.hside.at[side, s], "hs", "hs", n, dk
                    ).start()

    for s in range(2):
        forward(s)
        if s == 0:
            arrived(v.erecv.at[0:224], "e")
        along(s)
        backward(s)
    for side, dk in ((0, -1), (1, 1)):

        @pl.when(i <= 2 if side == 0 else i >= 5)
        def _():
            place = i if side == 0 else i - 2
            for n in range(nr):
                remote(
                    v.hedge.at[side, pl.ds(8 * n, 8)], v.gside.at[place], "gs", "gs", n, dk
                ).start()

    for s in range(2):
        arrived(v.rrecv.at[0:224], f"r{s}")
        for c in range(4):
            for n in range(4):
                for ca in range(2):
                    at = 256 * s + 8 * c + 2 * n + ca
                    v.res_v[c, pl.ds((s * 4 + n) * 16 + ca, 8, stride=2), :] = v.rrecv[
                        pl.ds(at, 8, stride=32), :
                    ]
        arrived(v.gfrecv.at[0:224], f"f{s}")
        for j in range(8):
            for r in range(2):
                for h in range(2):
                    at = 256 * s + (2 * j + r) * 2 + h
                    v.gf_v[s, j, r, :, 128 * h : 128 * h + 128] = v.gfrecv[
                        pl.ds(at, 8, stride=32), :
                    ]
    arrived(v.hrecv.at[0:112], "h0")
    arrived(v.hrecv.at[0:168], "h1")
    arrived(v.gside, "gs")
    arrived(v.hside, "hs")
    for s in range(2):

        def owed(owner, u):
            at = 128 * s + (16 + 8 * s) * owner + 8 * u
            return v.hrecv[at : at + 8]

        by_row = [
            owed(1, 0) + owed(2, 0) + owed(0, 1) + v.hside[1, s],
            owed(3, 0) + owed(4, 0) + owed(1, 1) + owed(2, 1),
            owed(5, 0) + owed(6, 0) + owed(3, 1) + owed(4, 1),
            owed(7, 0) + owed(5, 1) + owed(6, 1) + v.hside[0, s],
        ]
        for a in range(4):
            v.gm_x[pl.ds(32 * s + a, 8, stride=4), :] = by_row[a]
        for j in range(8):
            at = 32 * s + 4 * j
            v.gm_v[s, j] = v.gm_x[at : at + 4]
    total = v.gside[0]
    for n in range(1, 6):
        total = total + v.gside[n]
    for owner in range(nr):
        at = 128 + 24 * owner + 16
        total = total + v.hrecv[at : at + 8]
    for s in range(2):
        v.gc_v[s] = total[4 * s : 4 * s + 4]

    sent(v.xsend.at[0:104], "c")
    sent(v.xsend.at[0:256], "n")
    sent(v.xsend.at[0:448], "x")
    sent(v.xsend.at[0:224], "e")
    sent(v.xsend.at[0:448], "r")
    sent(v.xsend.at[0:448], "f")
    sent(v.xsend.at[0:280], "h")

    @pl.when((i <= 2) | (i >= 5))
    def _():
        sent(v.xsend.at[0:64], "gs")

    @pl.when((i == 0) | (i == nr - 1))
    def _():
        sent(v.xsend.at[0:128], "hs")


def hand_out(gc_v, gm_v, gf_v, res_v, gc_o, gm_o, gf_o, res_o, sem):
    outs = [
        pltpu.make_async_copy(gf_v, gf_o, sem.at[0]),
        pltpu.make_async_copy(gm_v, gm_o.at[:, :, 0], sem.at[1]),
        pltpu.make_async_copy(gc_v, gc_o.at[:, 0], sem.at[2]),
    ]
    for c in range(4):
        outs.append(
            pltpu.make_async_copy(
                res_v.at[c].reshape(2, 4, 16, 128),
                res_o.at[:, :, :, pl.ds(128 * c, 128)],
                sem.at[3 + c],
            )
        )
    for out in outs:
        out.start()
    for out in outs:
        out.wait()


def per_device(*args):
    nr, na = lax.axis_size("rad"), lax.axis_size("ang")
    args = list(args)
    for n in (4, 7):
        args[n] = args[n].transpose(1, 2, 0)
    held = [(2, 4, 128), (2, 8, 4, 128), (2, 8, 2, 8, 256), (4, 128, 128)]
    shapes = [(2, 1, 4, 128), (2, 8, 1, 4, 128), (2, 8, 2, 8, 256), (2, 4, 16, 512)]
    results = pl.pallas_call(
        functools.partial(kernel, nr, na),
        out_shape=[pltpu.VMEM(shape, F32) for shape in held],
        in_specs=[ANY] * 12,
        out_specs=[VMEM] * 4,
        scratch_shapes=list(SCRATCH.values()),
        compiler_params=pltpu.CompilerParams(collective_id=0, has_side_effects=True),
    )(*args)
    return pl.pallas_call(
        hand_out,
        out_shape=[jax.ShapeDtypeStruct(shape, F32) for shape in shapes],
        in_specs=[VMEM] * 4,
        out_specs=[ANY] * 4,
        scratch_shapes=[pltpu.SemaphoreType.DMA((7,))],
        compiler_params=pltpu.CompilerParams(vmem_limit_bytes=4 << 20),
    )(*results)


def solution(mesh):
    placed = (
        P(None, "rad", "ang", None),
        P(None, None, "rad", "ang", None),
        P(None, None, "rad", "ang", None),
        P(),
        P(),
        P(),
        P(),
        P(),
        P(),
        P("rad", "ang", None),
        P(None, "ang", None),
        P(None, "ang", None),
    )
    return jax.shard_map(
        per_device,
        mesh=mesh,
        in_specs=placed,
        out_specs=(
            P(None, "rad", "ang", None),
            P(None, None, "rad", "ang", None),
            P(None, None, "rad", "ang", None),
            P(None, None, "ang", None),
        ),
        check_vma=False,
    )
```

```python
import functools

import jax
import jax.numpy as jnp
from jax import lax
from jax.experimental import pallas as pl
from jax.experimental.pallas import tpu as pltpu
from jax.sharding import PartitionSpec as P

F32 = jnp.float32
BF16 = jnp.bfloat16
MESH = pl.DeviceIdType.MESH
ANY = pl.BlockSpec(memory_space=pl.ANY)
VMEM = pl.BlockSpec(memory_space=pltpu.VMEM)


def lane_shift(x, step):
    if step == 1:
        return x
    width = x.shape[1]
    lane = lax.broadcasted_iota(jnp.int32, x.shape, 1)
    if step == 0:
        return jnp.where(lane == 0, F32(0.0), pltpu.roll(x, 1, 1))
    return jnp.where(lane == width - 1, F32(0.0), pltpu.roll(x, width - 1, 1))


def permuted(x, permutation):
    high = x.astype(BF16)
    rest = x - high.astype(F32)
    mid = rest.astype(BF16)
    low = (rest - mid.astype(F32)).astype(BF16)

    def times(part):
        return jnp.dot(part, permutation, preferred_element_type=F32)

    return times(high) + times(mid) + times(low)


SCRATCH = dict(
    cf_v=pltpu.VMEM((2, 4, 128), F32),
    exm_v=pltpu.VMEM((2, 8, 4, 128), F32),
    exf_v=pltpu.VMEM((2, 8, 2, 8, 256), F32),
    em_v=pltpu.VMEM((4, 64, 128), F32),
    bins_v=pltpu.VMEM((4, 64, 128), jnp.int32),
    data_v=pltpu.VMEM((4, 64, 128), F32),
    km_v=pltpu.VMEM((16, 8, 27), F32),
    nm_v=pltpu.VMEM((8, 8, 16), F32),
    kf_v=pltpu.VMEM((16, 8, 27), F32),
    nf_v=pltpu.VMEM((8, 8, 16), F32),
    rm_s=pltpu.SMEM((8,), jnp.int32),
    rf_s=pltpu.SMEM((16,), jnp.int32),
    spread_m=pltpu.VMEM((256, 256), BF16),
    gather_m=pltpu.VMEM((256, 256), BF16),
    table=pltpu.VMEM((3, 64, 128), F32),
    kern=pltpu.VMEM((3, 8, 27, 8, 128), F32),
    noise=pltpu.VMEM((3, 8, 8, 8, 128), F32),
    csend=pltpu.VMEM((8, 128), F32),
    crecv=pltpu.VMEM((3, 64, 128), F32),
    nsend=pltpu.VMEM((64, 128), F32),
    nrecv=pltpu.VMEM((256, 128), F32),
    nside=pltpu.VMEM((128, 128), F32),
    xsend=pltpu.VMEM((512, 128), F32),
    xrecv=pltpu.VMEM((512, 128), F32),
    esend=pltpu.VMEM((256, 128), F32),
    erecv=pltpu.VMEM((256, 128), F32),
    c12=pltpu.VMEM((12, 2, 8, 128), F32),
    emx=pltpu.VMEM((4, 8, 8, 128), F32),
    cs=pltpu.VMEM((4, 9, 8, 128), F32),
    xi=pltpu.VMEM((4, 2, 8, 256), F32),
    m4=pltpu.VMEM((4, 2, 8, 256), F32),
    fs=pltpu.VMEM((4, 9, 8, 256), F32),
    dv=pltpu.VMEM((4, 4, 8, 256), F32),
    star_x=pltpu.VMEM((2, 8, 8, 512), F32),
    star_y=pltpu.VMEM((2, 4, 8, 128), F32),
    star_z=pltpu.VMEM((2, 2, 16, 128), F32),
    res_x=pltpu.VMEM((2, 16, 128), F32),
    rsend=pltpu.VMEM((64, 128), F32),
    rrecv=pltpu.VMEM((512, 128), F32),
    ws=pltpu.VMEM((4, 9, 8, 256), F32),
    h4=pltpu.VMEM((4, 2, 8, 256), F32),
    wq=pltpu.VMEM((4, 9, 8, 128), F32),
    g12=pltpu.VMEM((12, 8, 128), F32),
    gfsend=pltpu.VMEM((512, 128), F32),
    gfrecv=pltpu.VMEM((512, 128), F32),
    hsend=pltpu.VMEM((320, 128), F32),
    hrecv=pltpu.VMEM((320, 128), F32),
    hedge=pltpu.VMEM((2, 64, 128), F32),
    hside=pltpu.VMEM((2, 2, 8, 128), F32),
    gside=pltpu.VMEM((6, 8, 128), F32),
    gm_x=pltpu.VMEM((64, 128), F32),
    load_sem=pltpu.SemaphoreType.DMA((13,)),
    send_sem=pltpu.SemaphoreType.DMA((9,)),
    recv_sem=pltpu.SemaphoreType.DMA((19,)),
)
SEND = dict(c=0, n=1, x=2, e=3, r=4, f=5, h=6, gs=7, hs=8)
RECV = {
    name: number
    for number, name in enumerate(
        ["c", "cs", "n0", "n1", "ns0", "ns1", "x0", "x1", "e"]
        + ["r0", "r1", "q0", "q1", "f0", "f1", "h0", "h1", "gs", "hs"]
    )
}
INPUTS = ["cf", "exm", "exf", "km", "nm", "rm", "kf", "nf", "rf", "emi", "bins", "data"]
OUTPUTS = ["gc_v", "gm_v", "gf_v", "res_v"]


class Refs:
    def __init__(self, refs):
        for name, ref in zip(INPUTS + OUTPUTS + list(SCRATCH), refs):
            setattr(self, name, ref)


def wide(x):
    return jnp.concatenate([x, x], axis=1)


def row_shift(x, step):
    if step == 1:
        return x
    sub = lax.broadcasted_iota(jnp.int32, x.shape, 0)
    if step == 0:
        return jnp.where(sub == 0, F32(0.0), pltpu.roll(x, 1, 0))
    return jnp.where(sub == 7, F32(0.0), pltpu.roll(x, 7, 0))


def weighted(weights, values):
    total = weights[0] * values[0]
    for weight, value in zip(weights[1:], values[1:]):
        total = total + weight * value
    return total


def sums_before(x):
    sub = lax.broadcasted_iota(jnp.int32, x.shape, 0)
    total = x
    for step in (1, 2, 4):
        total = total + jnp.where(sub < step, F32(0.0), pltpu.roll(total, step, 0))
    return jnp.where(sub == 0, F32(0.0), pltpu.roll(total, 1, 0))


def row_total(x):
    for step in (4, 2, 1):
        x = x + pltpu.roll(x, step, 0)
    return x


def kernel(nr, na, *refs):
    v = Refs(refs)
    i = lax.axis_index("rad")
    k = lax.axis_index("ang")
    half_up = lax.shift_right_logical(i + 1, 1)
    low = half_up - 1
    first = 1 - lax.bitwise_and(i, 1)
    none = F32(0.0)

    def row_at(d):
        return lax.rem(i + d, nr)

    def block_at(dk):
        return lax.rem(k + (dk + na), na)

    def remote(src, dst, group, arrival, row, dk):
        return pltpu.make_async_remote_copy(
            src_ref=src,
            dst_ref=dst,
            send_sem=v.send_sem.at[SEND[group]],
            recv_sem=v.recv_sem.at[RECV[arrival]],
            device_id=(row, block_at(dk)),
            device_id_type=MESH,
        )

    def sent(like, group):
        pltpu.make_async_copy(like, like, v.send_sem.at[SEND[group]]).wait()

    def arrived(like, arrival):
        pltpu.make_async_copy(like, like, v.recv_sem.at[RECV[arrival]]).wait()

    def part(ref, index, size):
        return ref.at[pl.ds(pl.multiple_of(index * size, size), size)]

    def rows_of(index, size, offset):
        return pl.ds(pl.multiple_of(index * size + offset, 8), size)

    def scatter(src, dst, group, arrival, size, offset=0):
        for d in range(1, nr):
            remote(
                src.at[rows_of(row_at(d), size, offset)],
                dst.at[rows_of(i, size, offset)],
                group,
                arrival,
                row_at(d),
                0,
            ).start()

    def keep_own(src, dst, size, offset=0):
        own = rows_of(i, size, offset)
        dst[own] = src[own]

    loads = [
        [pltpu.make_async_copy(v.cf.at[:, 0], v.cf_v, v.load_sem.at[2])],
        [pltpu.make_async_copy(v.exm.at[:, :, 0], v.exm_v, v.load_sem.at[1])],
        [
            pltpu.make_async_copy(v.exf.at[s], v.exf_v.at[s], v.load_sem.at[(0, 12)[s]])
            for s in range(2)
        ],
    ]
    for n, (src, dst) in enumerate(((v.emi, v.em_v), (v.bins, v.bins_v), (v.data, v.data_v))):
        loads.append(
            [
                pltpu.make_async_copy(
                    src.at[:, :, pl.ds(128 * c, 128)],
                    dst.at[c].reshape(4, 16, 128),
                    v.load_sem.at[3 + n],
                )
                for c in range(4)
            ]
        )
    for n, (src, dst) in enumerate(
        (
            (v.rm, v.rm_s),
            (v.rf, v.rf_s),
            (v.km, v.km_v),
            (v.nm, v.nm_v),
            (v.kf, v.kf_v),
            (v.nf, v.nf_v),
        )
    ):
        loads.append([pltpu.make_async_copy(src, dst, v.load_sem.at[6 + n])])
    for group in loads[:3]:
        for load in group:
            load.start()

    barrier = pltpu.get_barrier_semaphore()
    for d in range(1, nr):
        pl.semaphore_signal(barrier, inc=1, device_id=(row_at(d), k), device_id_type=MESH)
    for dk in (-1, 1):
        for d in range(nr):
            pl.semaphore_signal(
                barrier, inc=1, device_id=(d, block_at(dk)), device_id_type=MESH
            )

    for group in loads[3:]:
        for load in group:
            load.start()
    for group in loads[:2]:
        group[0].wait()
    for s in range(2):
        v.csend[4 * s : 4 * s + 4] = v.cf_v[s]
        for j in range(8):
            v.nsend[pl.ds(32 * s + j, 4, stride=8), :] = v.exm_v[s, j]
    pl.semaphore_wait(barrier, 3 * nr - 1)

    def start_of(owner):
        return jnp.clip(lax.shift_right_logical(owner + 1, 1) - 1, 0, 2)

    def pair_of(owner, s):
        return pl.ds(pl.multiple_of(start_of(owner) * 8 + 32 * s, 8), 16)

    own8 = rows_of(i, 8, 0)
    for d in range(1, nr):
        remote(v.csend, v.crecv.at[1, own8], "c", "c", row_at(d), 0).start()
    for side, dk, rows in ((0, 1, (0, 1, 2)), (2, -1, (5, 6, 7))):
        for to in rows:
            remote(v.csend, v.crecv.at[side, own8], "c", "cs", to, dk).start()

    def send_sample(s):
        for d in range(1, nr):
            remote(
                v.nsend.at[pair_of(row_at(d), s)],
                v.nrecv.at[rows_of(i, 16, 128 * s)],
                "n",
                f"n{s}",
                row_at(d),
                0,
            ).start()
        there = v.nside.at[rows_of(i, 8, 64 * s)]
        remote(v.nsend.at[32 * s + 24 : 32 * s + 32], there, "n", f"ns{s}", 0, 1).start()
        remote(v.nsend.at[32 * s : 32 * s + 8], there, "n", f"ns{s}", 7, -1).start()
        loads[2][s].wait()
        for r in range(2):
            for j in range(8):
                for h in range(2):
                    at = 256 * s + (r * 8 + j) * 2 + h
                    v.xsend[pl.ds(at, 8, stride=32), :] = v.exf_v[
                        s, j, r, :, 128 * h : 128 * h + 128
                    ]
        scatter(v.xsend, v.xrecv, "x", f"x{s}", 32, 256 * s)

    send_sample(0)

    row = lax.broadcasted_iota(jnp.int32, (256, 256), 0)
    col = lax.broadcasted_iota(jnp.int32, (256, 256), 1)
    v.gather_m[...] = jnp.where(
        row == 2 * lax.bitwise_and(col, 127) + lax.shift_right_logical(col, 7), F32(1.0), none
    ).astype(BF16)
    for load in loads[3]:
        load.wait()
    pieces = [
        jnp.concatenate(
            [v.em_v[2 * h + e, pl.ds(16 * rl + ca, 8, stride=2), :] for e in range(2)], axis=1
        )
        for rl in range(4)
        for ca in range(2)
        for h in range(2)
    ]
    pieces = permuted(jnp.concatenate(pieces, axis=0), v.gather_m[...])
    for rl in range(4):
        for ca in range(2):
            for h in range(2):
                n = (rl * 2 + ca) * 2 + h
                for cb in range(2):
                    at = h * 16 + rl * 4 + ca * 2 + cb
                    v.esend[pl.ds(at, 8, stride=32), :] = pieces[
                        8 * n : 8 * n + 8, 128 * cb : 128 * cb + 128
                    ]

    scatter(v.esend, v.erecv, "e", "e", 32)
    send_sample(1)

    v.spread_m[...] = jnp.where(
        col == 2 * lax.bitwise_and(row, 127) + lax.shift_right_logical(row, 7), F32(1.0), none
    ).astype(BF16)

    v.crecv[1, own8] = v.csend[...]
    for s in range(2):
        v.nrecv[rows_of(i, 16, 128 * s)] = v.nsend[pair_of(i, s)]
        keep_own(v.xsend, v.xrecv, 32, 256 * s)
    keep_own(v.esend, v.erecv, 32)
    for group in loads[4:]:
        for load in group:
            load.wait()

    entry = lax.broadcasted_iota(jnp.int32, (8, 16), 1)
    place = lax.broadcasted_iota(jnp.int32, (8, 16), 0)
    chosen = []
    for x in range(3):
        index = jnp.zeros((8, 16), jnp.int32)
        for cell in range(8):
            if x == 0:
                number = v.rm_s[cell]
                v.table[x, pl.ds(cell, 8, stride=8), 0:27] = v.km_v[number]
            else:
                number = v.rf_s[2 * cell + x - 1]
                v.table[x, pl.ds(cell, 8, stride=8), 0:27] = v.kf_v[number]
            index = jnp.where(place == cell, number, index)
        chosen.append(jnp.where(index == entry, F32(1.0), none).astype(BF16))
    for x in range(3):
        for c in range(8):
            tile = v.table[x, 8 * c : 8 * c + 8]
            for o in range(27):
                v.kern[x, c, o] = jnp.broadcast_to(tile[:, o : o + 1], (8, 128))
        source = (v.nm_v if x == 0 else v.nf_v)[...].reshape(64, 16)
        high = source.astype(BF16)
        rest = source - high.astype(F32)
        mid = rest.astype(BF16)
        least = (rest - mid.astype(F32)).astype(BF16)
        tile = None
        for piece in (high, mid, least):
            term = lax.dot_general(
                chosen[x], piece, (((1,), (1,)), ((), ())), preferred_element_type=F32
            )
            tile = term if tile is None else tile + term
        for c in range(8):
            for j in range(8):
                at = 8 * c + j
                v.noise[x, c, j] = jnp.broadcast_to(tile[:, at : at + 1], (8, 128))

    for n in range(4):
        for ca in range(2):
            for c in range(4):
                at = pl.ds(16 * n + ca, 8, stride=2)
                lanes = pl.ds(128 * c, 128)
                v.star_x[0, :, 2 * n + ca, lanes] = v.bins_v[c, at, :].astype(F32)
                v.star_x[1, :, 2 * n + ca, lanes] = v.data_v[c, at, :]
    for kind in range(2):
        x = v.star_x[kind, i]
        y = permuted(jnp.concatenate([x[:, :256], x[:, 256:]], axis=0), v.gather_m[...])
        for h in range(2):
            for cb in range(2):
                v.star_y[kind, 2 * h + cb] = y[8 * h : 8 * h + 8, 128 * cb : 128 * cb + 128]
        for h in range(2):
            for cb in range(2):
                for ca in range(2):
                    v.star_z[kind, h, pl.ds(2 * ca + cb, 4, stride=4), :] = v.star_y[
                        kind, 2 * h + cb, pl.ds(ca, 4, stride=2), :
                    ]

    arrived(v.crecv.at[1, 0:56], "c")

    @pl.when((i <= 2) | (i >= 5))
    def _():
        arrived(v.crecv.at[0], "cs")

    for side in range(3):
        for a in range(4):
            for s in range(2):
                x = v.crecv[side, pl.ds(4 * s + a, 8, stride=8), :]
                if side == 0:
                    x = jnp.where(k > 0, x, none)
                if side == 2:
                    x = jnp.where(k < na - 1, x, none)
                v.c12[4 * side + a, s] = x
    base = jnp.where(i > 0, 1, 0) + jnp.where(i == nr - 1, 1, 0)
    spacing = F32(1.0 / (4 * nr))
    cell = 4 * lax.broadcasted_iota(jnp.int32, (8, 256), 0)
    cells = [(cell + j).astype(F32) for j in range(4)]

    def parent_inside(u):
        a = 4 * k + low + u
        return (a >= 0) & (a < 4 * na)

    def star(kind, n, q):
        at = 4 * n + q
        return jnp.concatenate(
            [
                jnp.broadcast_to(v.star_z[kind, h, at : at + 1, :], (8, 128))
                for h in range(2)
            ],
            axis=1,
        )

    def spread_out(sums):
        total = lane_shift(sums[1], 1)
        total = total + lane_shift(sums[0], 2)
        return total + lane_shift(sums[2], 0)

    def forward(s):
        for t in range(4):
            x = v.c12[half_up + 2 + t, s]
            for dr in range(3):
                moved = row_shift(x, dr)
                for db in range(3):
                    v.cs[t, 3 * dr + db] = lane_shift(moved, db)
        arrived(v.nrecv.at[0:112], f"n{s}")

        @pl.when((i == 0) | (i == nr - 1))
        def _():
            arrived(v.nside.at[0:64], f"ns{s}")

        for j in range(8):
            for n in range(2):
                v.emx[1 + n, j] = v.nrecv[pl.ds(128 * s + 8 * n + j, 8, stride=16), :]
            x = v.nside[pl.ds(64 * s + j, 8, stride=8), :]
            v.emx[0, j] = x
            v.emx[3, j] = x
        sums = [[None] * 8, [None] * 8]
        for j in range(8):
            x = [v.emx[base + u, j] for u in range(2)]
            for c in range(8):
                weight = v.noise[0, c, j]
                for u in range(2):
                    term = weight * x[u]
                    sums[u][c] = term if j == 0 else sums[u][c] + term
        for o in range(27):
            dr, da, db = o // 9, o // 3 % 3, o % 3
            x = [v.cs[u + da, 3 * dr + db] for u in range(2)]
            for c in range(8):
                weight = v.kern[0, c, o]
                for u in range(2):
                    sums[u][c] = sums[u][c] + weight * x[u]
        for u in range(2):
            for c in range(8):
                lanes = slice(128 * (c % 2), 128 * (c % 2) + 128)
                v.xi[2 * u + c // 2 % 2, c // 4, :, lanes] = jnp.where(
                    parent_inside(u), sums[u][c], none
                )
        v.m4[...] = permuted(v.xi[...].reshape(64, 256), v.spread_m[...]).reshape(4, 2, 8, 256)
        for da in range(3):
            even = v.m4[first + da, 0]
            odd = v.m4[first + da, 1]
            for m, x in enumerate((row_shift(odd, 0), even, odd, row_shift(even, 2))):
                for db in range(3):
                    v.fs[m, 3 * da + db] = lane_shift(x, db)

        arrived(v.xrecv.at[0:224], f"x{s}")
        for r in range(2):
            sums = [None] * 8
            for j in range(8):
                at = 256 * s + (r * 8 + j) * 2
                x = jnp.concatenate(
                    [v.xrecv[pl.ds(at + h, 8, stride=32), :] for h in range(2)], axis=1
                )
                for c in range(8):
                    term = wide(v.noise[1 + r, c, j]) * x
                    sums[c] = term if j == 0 else sums[c] + term
            for o in range(27):
                x = v.fs[r + o // 9, o % 9]
                for c in range(8):
                    sums[c] = sums[c] + wide(v.kern[1 + r, c, o]) * x
            for c in range(8):
                v.dv[2 * r + c // 4, c % 4] = jnp.exp(sums[c])

    def along(s):
        for q in range(4):
            bins = [star(0, n, q) for n in range(4)]
            light = [
                spacing
                * jnp.concatenate(
                    [v.erecv[pl.ds(16 * h + 4 * j + q, 8, stride=32), :] for h in range(2)], axis=1
                )
                for j in range(4)
            ]
            dens = [v.dv[j, q] for j in range(4)]
            layer = [spacing * x for x in dens]
            depth = sums_before((layer[0] + layer[1]) + (layer[2] + layer[3]))
            shine = []
            for j in range(4):
                shine.append(light[j] * jnp.exp(-depth))
                depth = depth + layer[j]
            column = sums_before((shine[0] + shine[1]) + (shine[2] + shine[3]))
            columns = []
            for j in range(4):
                column = column + shine[j]
                columns.append(column)
            weights = [None] * 4
            for n in range(4):
                picked = jnp.where(bins[n] == cells[0], columns[0], none)
                for j in range(1, 4):
                    picked = jnp.where(bins[n] == cells[j], columns[j], picked)
                picked = row_total(picked)
                left = star(1, n, q) - picked
                for h in range(2):
                    at = 4 * n + q
                    v.res_x[h, at : at + 1] = left[0:1, 128 * h : 128 * h + 128]
                for j in range(4):
                    term = jnp.where(bins[n] > cells[j], left * (picked - columns[j]), none)
                    weights[j] = term if n == 0 else weights[j] + term
            for j in range(4):
                v.dv[j, q] = -dens[j] * weights[j]

        pieces = [
            jnp.concatenate([v.res_x[h, pl.ds(cb, 8, stride=2), :] for cb in range(2)], axis=1)
            for h in range(2)
        ]
        spread = permuted(jnp.concatenate(pieces, axis=0), v.spread_m[...])
        for h in range(2):
            for e in range(2):
                at = 32 * s + 8 * (2 * h + e)
                v.rsend[at : at + 8] = spread[8 * h : 8 * h + 8, 128 * e : 128 * e + 128]
        mine = v.rsend.at[32 * s : 32 * s + 32]
        there = rows_of(i, 32, 256 * s)
        for to in (ring_at(1), ring_at(3), ring_at(2), across):
            remote(mine, v.rrecv.at[there], "r", f"r{s}", to, 0).start()
        v.rrecv[there] = mine[...]

    def backward(s):
        for r in range(2):
            grads = [v.dv[2 * r + c // 4, c % 4] for c in range(8)]
            for j in range(8):
                total = weighted([wide(v.noise[1 + r, c, j]) for c in range(8)], grads)
                for h in range(2):
                    at = 256 * s + (2 * j + r) * 2 + h
                    v.gfsend[pl.ds(at, 8, stride=32), :] = total[:, 128 * h : 128 * h + 128]
            for o in range(27):
                total = weighted([wide(v.kern[1 + r, c, o]) for c in range(8)], grads)
                m = r + o // 9
                if r == 1 and m < 3:
                    total = total + v.ws[m, o % 9]
                v.ws[m, o % 9] = total
        scatter(v.gfsend, v.gfrecv, "f", f"f{s}", 32, 256 * s)
        keep_own(v.gfsend, v.gfrecv, 32, 256 * s)

        pieces = []
        for da in range(3):
            moved = [spread_out([v.ws[m, 3 * da + db] for db in range(3)]) for m in range(4)]
            pieces.append(moved[1] + row_shift(moved[3], 0))
            pieces.append(moved[2] + row_shift(moved[0], 2))
        spread = permuted(jnp.concatenate(pieces, axis=0), v.gather_m[...])
        v.h4[...] = jnp.zeros(v.h4.shape, F32)
        for da in range(3):
            keep = parent_inside(lax.shift_right_logical(first + da, 1))
            for cr in range(2):
                n = (2 * da + cr) * 8
                v.h4[first + da, cr] = jnp.where(keep, spread[n : n + 8], none)

        children = []
        for u in range(2):
            children.append([])
            for c in range(8):
                lanes = slice(128 * (c % 2), 128 * (c % 2) + 128)
                children[u].append(v.h4[2 * u + c // 2 % 2, c // 4, :, lanes])
        size = 16 + 8 * s
        for j in range(8):
            weights = [v.noise[0, c, j] for c in range(8)]
            for u in range(2):
                v.hsend[pl.ds(128 * s + 8 * u + j, 8, stride=size), :] = weighted(
                    weights, children[u]
                )
        for dr in range(3):
            for db in range(3):
                sums = [None] * 4
                for da in range(3):
                    o = 9 * dr + 3 * da + db
                    weights = [v.kern[0, c, o] for c in range(8)]
                    for u in range(2):
                        total = weighted(weights, children[u])
                        t = u + da
                        sums[t] = total if sums[t] is None else sums[t] + total
                for t in range(4):
                    v.wq[t, 3 * dr + db] = sums[t]
        v.g12[...] = jnp.zeros(v.g12.shape, F32)
        for t in range(4):
            total = None
            for dr in range(3):
                term = spread_out([v.wq[t, 3 * dr + db] for db in range(3)])
                term = row_shift(term, 2 - dr)
                total = term if total is None else total + term
            v.g12[half_up + 2 + t] = total
        for a in range(4):
            v.hsend[pl.ds(128 + 16 + 4 * s + a, 8, stride=24), :] = v.g12[4 + a]
            for side in range(2):
                outside = (k > 0) if side == 0 else (k < na - 1)
                v.hedge[side, pl.ds(4 * s + a, 8, stride=8), :] = jnp.where(
                    outside, v.g12[8 * side + a], none
                )
        scatter(v.hsend, v.hrecv, "h", f"h{s}", size, 128 * s)
        keep_own(v.hsend, v.hrecv, size, 128 * s)
        for side, dk in ((0, -1), (1, 1)):

            @pl.when(i == 0 if side == 0 else i == nr - 1)
            def _():
                for n in range(nr):
                    at = 128 * s + size * n + 8 * side
                    remote(
                        v.hsend.at[at : at + 8], v.hside.at[side, s], "hs", "hs", n, dk
                    ).start()

    def ring_at(d):
        return (i & 4) + ((i + d) & 3)

    across = i ^ 4

    def pass_on(s):
        arrived(v.rrecv.at[0:128], f"r{s}")
        opposite = ring_at(2)
        for owner, to in ((across, ring_at(1)), (across, ring_at(3)), (opposite, across)):
            block = v.rrecv.at[rows_of(owner, 32, 256 * s)]
            remote(block, block, "r", f"q{s}", to, 0).start()

    for s in range(2):
        forward(s)
        if s == 0:
            arrived(v.erecv.at[0:224], "e")
        along(s)
        backward(s)
    for side, dk in ((0, -1), (1, 1)):

        @pl.when(i <= 2 if side == 0 else i >= 5)
        def _():
            place = i if side == 0 else i - 2
            for n in range(nr):
                remote(
                    v.hedge.at[side, pl.ds(8 * n, 8)], v.gside.at[place], "gs", "gs", n, dk
                ).start()

    pass_on(0)
    pass_on(1)
    for s in range(2):
        arrived(v.rrecv.at[0:96], f"q{s}")
        for c in range(4):
            for n in range(4):
                for ca in range(2):
                    at = 256 * s + 8 * c + 2 * n + ca
                    v.res_v[c, pl.ds((s * 4 + n) * 16 + ca, 8, stride=2), :] = v.rrecv[
                        pl.ds(at, 8, stride=32), :
                    ]
        arrived(v.gfrecv.at[0:224], f"f{s}")
        for j in range(8):
            for r in range(2):
                for h in range(2):
                    at = 256 * s + (2 * j + r) * 2 + h
                    v.gf_v[s, j, r, :, 128 * h : 128 * h + 128] = v.gfrecv[
                        pl.ds(at, 8, stride=32), :
                    ]
    arrived(v.hrecv.at[0:112], "h0")
    arrived(v.hrecv.at[0:168], "h1")
    arrived(v.gside, "gs")
    arrived(v.hside, "hs")
    for s in range(2):

        def owed(owner, u):
            at = 128 * s + (16 + 8 * s) * owner + 8 * u
            return v.hrecv[at : at + 8]

        by_row = [
            owed(1, 0) + owed(2, 0) + owed(0, 1) + v.hside[1, s],
            owed(3, 0) + owed(4, 0) + owed(1, 1) + owed(2, 1),
            owed(5, 0) + owed(6, 0) + owed(3, 1) + owed(4, 1),
            owed(7, 0) + owed(5, 1) + owed(6, 1) + v.hside[0, s],
        ]
        for a in range(4):
            v.gm_x[pl.ds(32 * s + a, 8, stride=4), :] = by_row[a]
        for j in range(8):
            at = 32 * s + 4 * j
            v.gm_v[s, j] = v.gm_x[at : at + 4]
    total = v.gside[0]
    for n in range(1, 6):
        total = total + v.gside[n]
    for owner in range(nr):
        at = 128 + 24 * owner + 16
        total = total + v.hrecv[at : at + 8]
    for s in range(2):
        v.gc_v[s] = total[4 * s : 4 * s + 4]

    sent(v.xsend.at[0:104], "c")
    sent(v.xsend.at[0:256], "n")
    sent(v.xsend.at[0:448], "x")
    sent(v.xsend.at[0:224], "e")
    sent(v.xsend.at[0:448], "r")
    sent(v.xsend.at[0:448], "f")
    sent(v.xsend.at[0:280], "h")

    @pl.when((i <= 2) | (i >= 5))
    def _():
        sent(v.xsend.at[0:64], "gs")

    @pl.when((i == 0) | (i == nr - 1))
    def _():
        sent(v.xsend.at[0:128], "hs")


def hand_out(gc_v, gm_v, gf_v, res_v, gc_o, gm_o, gf_o, res_o, sem):
    outs = [
        pltpu.make_async_copy(gf_v, gf_o, sem.at[0]),
        pltpu.make_async_copy(gm_v, gm_o.at[:, :, 0], sem.at[1]),
        pltpu.make_async_copy(gc_v, gc_o.at[:, 0], sem.at[2]),
    ]
    for c in range(4):
        outs.append(
            pltpu.make_async_copy(
                res_v.at[c].reshape(2, 4, 16, 128),
                res_o.at[:, :, :, pl.ds(128 * c, 128)],
                sem.at[3 + c],
            )
        )
    for out in outs:
        out.start()
    for out in outs:
        out.wait()


def per_device(*args):
    nr, na = lax.axis_size("rad"), lax.axis_size("ang")
    args = list(args)
    for n in (4, 7):
        args[n] = args[n].transpose(1, 2, 0)
    held = [(2, 4, 128), (2, 8, 4, 128), (2, 8, 2, 8, 256), (4, 128, 128)]
    shapes = [(2, 1, 4, 128), (2, 8, 1, 4, 128), (2, 8, 2, 8, 256), (2, 4, 16, 512)]
    results = pl.pallas_call(
        functools.partial(kernel, nr, na),
        out_shape=[pltpu.VMEM(shape, F32) for shape in held],
        in_specs=[ANY] * 12,
        out_specs=[VMEM] * 4,
        scratch_shapes=list(SCRATCH.values()),
        compiler_params=pltpu.CompilerParams(collective_id=0, has_side_effects=True),
    )(*args)
    return pl.pallas_call(
        hand_out,
        out_shape=[jax.ShapeDtypeStruct(shape, F32) for shape in shapes],
        in_specs=[VMEM] * 4,
        out_specs=[ANY] * 4,
        scratch_shapes=[pltpu.SemaphoreType.DMA((7,))],
        compiler_params=pltpu.CompilerParams(vmem_limit_bytes=4 << 20),
    )(*results)


def solution(mesh):
    placed = (
        P(None, "rad", "ang", None),
        P(None, None, "rad", "ang", None),
        P(None, None, "rad", "ang", None),
        P(),
        P(),
        P(),
        P(),
        P(),
        P(),
        P("rad", "ang", None),
        P(None, "ang", None),
        P(None, "ang", None),
    )
    return jax.shard_map(
        per_device,
        mesh=mesh,
        in_specs=placed,
        out_specs=(
            P(None, "rad", "ang", None),
            P(None, None, "rad", "ang", None),
            P(None, None, "rad", "ang", None),
            P(None, None, "ang", None),
        ),
        check_vma=False,
    )
```

```python
import functools

import jax
import jax.numpy as jnp
from jax import lax
from jax.experimental import pallas as pl
from jax.experimental.pallas import tpu as pltpu
from jax.sharding import PartitionSpec as P

F32 = jnp.float32
BF16 = jnp.bfloat16
MESH = pl.DeviceIdType.MESH
ANY = pl.BlockSpec(memory_space=pl.ANY)
VMEM = pl.BlockSpec(memory_space=pltpu.VMEM)


def lane_shift(x, step):
    if step == 1:
        return x
    width = x.shape[1]
    lane = lax.broadcasted_iota(jnp.int32, x.shape, 1)
    if step == 0:
        return jnp.where(lane == 0, F32(0.0), pltpu.roll(x, 1, 1))
    return jnp.where(lane == width - 1, F32(0.0), pltpu.roll(x, width - 1, 1))


def permuted(x, permutation):
    high = x.astype(BF16)
    rest = x - high.astype(F32)
    mid = rest.astype(BF16)
    low = (rest - mid.astype(F32)).astype(BF16)

    def times(part):
        return jnp.dot(part, permutation, preferred_element_type=F32)

    return times(high) + times(mid) + times(low)


SCRATCH = dict(
    cf_v=pltpu.VMEM((2, 4, 128), F32),
    exm_v=pltpu.VMEM((2, 8, 4, 128), F32),
    exf_v=pltpu.VMEM((2, 8, 2, 8, 256), F32),
    em_v=pltpu.VMEM((4, 64, 128), F32),
    bins_v=pltpu.VMEM((4, 64, 128), jnp.int32),
    data_v=pltpu.VMEM((4, 64, 128), F32),
    km_v=pltpu.VMEM((16, 8, 27), F32),
    nm_v=pltpu.VMEM((8, 8, 16), F32),
    kf_v=pltpu.VMEM((16, 8, 27), F32),
    nf_v=pltpu.VMEM((8, 8, 16), F32),
    rm_s=pltpu.SMEM((8,), jnp.int32),
    rf_s=pltpu.SMEM((16,), jnp.int32),
    spread_m=pltpu.VMEM((256, 256), BF16),
    gather_m=pltpu.VMEM((256, 256), BF16),
    table=pltpu.VMEM((3, 64, 128), F32),
    kern=pltpu.VMEM((3, 8, 27, 8, 128), F32),
    noise=pltpu.VMEM((3, 8, 8, 8, 128), F32),
    csend=pltpu.VMEM((8, 128), F32),
    crecv=pltpu.VMEM((3, 64, 128), F32),
    nsend=pltpu.VMEM((64, 128), F32),
    nrecv=pltpu.VMEM((256, 128), F32),
    nside=pltpu.VMEM((128, 128), F32),
    xsend=pltpu.VMEM((512, 128), F32),
    xrecv=pltpu.VMEM((512, 128), F32),
    esend=pltpu.VMEM((256, 128), F32),
    erecv=pltpu.VMEM((256, 128), F32),
    c12=pltpu.VMEM((12, 2, 8, 128), F32),
    emx=pltpu.VMEM((4, 8, 8, 128), F32),
    cs=pltpu.VMEM((4, 9, 8, 128), F32),
    xi=pltpu.VMEM((4, 2, 8, 256), F32),
    m4=pltpu.VMEM((4, 2, 8, 256), F32),
    fs=pltpu.VMEM((4, 9, 8, 256), F32),
    dv=pltpu.VMEM((4, 4, 8, 256), F32),
    star_x=pltpu.VMEM((2, 8, 8, 512), F32),
    star_y=pltpu.VMEM((2, 4, 8, 128), F32),
    star_z=pltpu.VMEM((2, 2, 16, 128), F32),
    res_x=pltpu.VMEM((2, 16, 128), F32),
    rsend=pltpu.VMEM((64, 128), F32),
    rrecv=pltpu.VMEM((512, 128), F32),
    ws=pltpu.VMEM((4, 9, 8, 256), F32),
    h4=pltpu.VMEM((4, 2, 8, 256), F32),
    wq=pltpu.VMEM((4, 9, 8, 128), F32),
    g12=pltpu.VMEM((12, 8, 128), F32),
    gfsend=pltpu.VMEM((512, 128), F32),
    gfrecv=pltpu.VMEM((512, 128), F32),
    hsend=pltpu.VMEM((320, 128), F32),
    hrecv=pltpu.VMEM((320, 128), F32),
    hedge=pltpu.VMEM((2, 64, 128), F32),
    hside=pltpu.VMEM((2, 2, 8, 128), F32),
    gside=pltpu.VMEM((6, 8, 128), F32),
    gm_x=pltpu.VMEM((64, 128), F32),
    load_sem=pltpu.SemaphoreType.DMA((13,)),
    send_sem=pltpu.SemaphoreType.DMA((9,)),
    recv_sem=pltpu.SemaphoreType.DMA((19,)),
)
SEND = dict(c=0, n=1, x=2, e=3, r=4, f=5, h=6, gs=7, hs=8)
RECV = {
    name: number
    for number, name in enumerate(
        ["c", "cs", "n0", "n1", "ns0", "ns1", "x0", "x1", "e"]
        + ["r0", "r1", "q0", "q1", "f0", "f1", "h0", "h1", "gs", "hs"]
    )
}
INPUTS = ["cf", "exm", "exf", "km", "nm", "rm", "kf", "nf", "rf", "emi", "bins", "data"]
OUTPUTS = ["gc_v", "gm_v", "gf_v", "res_v"]


class Refs:
    def __init__(self, refs):
        for name, ref in zip(INPUTS + OUTPUTS + list(SCRATCH), refs):
            setattr(self, name, ref)


def wide(x):
    return jnp.concatenate([x, x], axis=1)


def row_shift(x, step):
    if step == 1:
        return x
    sub = lax.broadcasted_iota(jnp.int32, x.shape, 0)
    if step == 0:
        return jnp.where(sub == 0, F32(0.0), pltpu.roll(x, 1, 0))
    return jnp.where(sub == 7, F32(0.0), pltpu.roll(x, 7, 0))


def weighted(weights, values):
    total = weights[0] * values[0]
    for weight, value in zip(weights[1:], values[1:]):
        total = total + weight * value
    return total


def sums_before(x):
    sub = lax.broadcasted_iota(jnp.int32, x.shape, 0)
    total = x
    for step in (1, 2, 4):
        total = total + jnp.where(sub < step, F32(0.0), pltpu.roll(total, step, 0))
    return jnp.where(sub == 0, F32(0.0), pltpu.roll(total, 1, 0))


def row_total(x):
    for step in (4, 2, 1):
        x = x + pltpu.roll(x, step, 0)
    return x


def kernel(nr, na, *refs):
    v = Refs(refs)
    i = lax.axis_index("rad")
    k = lax.axis_index("ang")
    half_up = lax.shift_right_logical(i + 1, 1)
    low = half_up - 1
    first = 1 - lax.bitwise_and(i, 1)
    none = F32(0.0)

    def row_at(d):
        return lax.rem(i + d, nr)

    def block_at(dk):
        return lax.rem(k + (dk + na), na)

    def remote(src, dst, group, arrival, row, dk):
        return pltpu.make_async_remote_copy(
            src_ref=src,
            dst_ref=dst,
            send_sem=v.send_sem.at[SEND[group]],
            recv_sem=v.recv_sem.at[RECV[arrival]],
            device_id=(row, block_at(dk)),
            device_id_type=MESH,
        )

    def sent(like, group):
        pltpu.make_async_copy(like, like, v.send_sem.at[SEND[group]]).wait()

    def arrived(like, arrival):
        pltpu.make_async_copy(like, like, v.recv_sem.at[RECV[arrival]]).wait()

    def part(ref, index, size):
        return ref.at[pl.ds(pl.multiple_of(index * size, size), size)]

    def rows_of(index, size, offset):
        return pl.ds(pl.multiple_of(index * size + offset, 8), size)

    def scatter(src, dst, group, arrival, size, offset=0):
        for d in (1, 7, 2, 6, 3, 5, 4):
            remote(
                src.at[rows_of(row_at(d), size, offset)],
                dst.at[rows_of(i, size, offset)],
                group,
                arrival,
                row_at(d),
                0,
            ).start()

    def keep_own(src, dst, size, offset=0):
        own = rows_of(i, size, offset)
        dst[own] = src[own]

    loads = [
        [pltpu.make_async_copy(v.cf.at[:, 0], v.cf_v, v.load_sem.at[2])],
        [pltpu.make_async_copy(v.exm.at[:, :, 0], v.exm_v, v.load_sem.at[1])],
        [
            pltpu.make_async_copy(v.exf.at[s], v.exf_v.at[s], v.load_sem.at[(0, 12)[s]])
            for s in range(2)
        ],
    ]
    for n, (src, dst) in enumerate(((v.emi, v.em_v), (v.bins, v.bins_v), (v.data, v.data_v))):
        loads.append(
            [
                pltpu.make_async_copy(
                    src.at[:, :, pl.ds(128 * c, 128)],
                    dst.at[c].reshape(4, 16, 128),
                    v.load_sem.at[3 + n],
                )
                for c in range(4)
            ]
        )
    for n, (src, dst) in enumerate(
        (
            (v.rm, v.rm_s),
            (v.rf, v.rf_s),
            (v.km, v.km_v),
            (v.nm, v.nm_v),
            (v.kf, v.kf_v),
            (v.nf, v.nf_v),
        )
    ):
        loads.append([pltpu.make_async_copy(src, dst, v.load_sem.at[6 + n])])
    for group in loads[:3]:
        for load in group:
            load.start()

    barrier = pltpu.get_barrier_semaphore()
    for d in range(1, nr):
        pl.semaphore_signal(barrier, inc=1, device_id=(row_at(d), k), device_id_type=MESH)
    for dk in (-1, 1):
        for d in range(nr):
            pl.semaphore_signal(
                barrier, inc=1, device_id=(d, block_at(dk)), device_id_type=MESH
            )

    for group in loads[3:]:
        for load in group:
            load.start()
    for group in loads[:2]:
        group[0].wait()
    for s in range(2):
        v.csend[4 * s : 4 * s + 4] = v.cf_v[s]
        for j in range(8):
            v.nsend[pl.ds(32 * s + j, 4, stride=8), :] = v.exm_v[s, j]
    pl.semaphore_wait(barrier, 3 * nr - 1)

    def start_of(owner):
        return jnp.clip(lax.shift_right_logical(owner + 1, 1) - 1, 0, 2)

    def pair_of(owner, s):
        return pl.ds(pl.multiple_of(start_of(owner) * 8 + 32 * s, 8), 16)

    own8 = rows_of(i, 8, 0)
    for d in (1, 7, 2, 6, 3, 5, 4):
        remote(v.csend, v.crecv.at[1, own8], "c", "c", row_at(d), 0).start()
    for side, dk, rows in ((0, 1, (0, 1, 2)), (2, -1, (5, 6, 7))):
        for to in rows:
            remote(v.csend, v.crecv.at[side, own8], "c", "cs", to, dk).start()

    def send_sample(s):
        for d in (1, 7, 2, 6, 3, 5, 4):
            remote(
                v.nsend.at[pair_of(row_at(d), s)],
                v.nrecv.at[rows_of(i, 16, 128 * s)],
                "n",
                f"n{s}",
                row_at(d),
                0,
            ).start()
        there = v.nside.at[rows_of(i, 8, 64 * s)]
        remote(v.nsend.at[32 * s + 24 : 32 * s + 32], there, "n", f"ns{s}", 0, 1).start()
        remote(v.nsend.at[32 * s : 32 * s + 8], there, "n", f"ns{s}", 7, -1).start()
        loads[2][s].wait()
        for r in range(2):
            for j in range(8):
                for h in range(2):
                    at = 256 * s + (r * 8 + j) * 2 + h
                    v.xsend[pl.ds(at, 8, stride=32), :] = v.exf_v[
                        s, j, r, :, 128 * h : 128 * h + 128
                    ]
        scatter(v.xsend, v.xrecv, "x", f"x{s}", 32, 256 * s)

    send_sample(0)

    row = lax.broadcasted_iota(jnp.int32, (256, 256), 0)
    col = lax.broadcasted_iota(jnp.int32, (256, 256), 1)
    v.gather_m[...] = jnp.where(
        row == 2 * lax.bitwise_and(col, 127) + lax.shift_right_logical(col, 7), F32(1.0), none
    ).astype(BF16)
    for load in loads[3]:
        load.wait()
    pieces = [
        jnp.concatenate(
            [v.em_v[2 * h + e, pl.ds(16 * rl + ca, 8, stride=2), :] for e in range(2)], axis=1
        )
        for rl in range(4)
        for ca in range(2)
        for h in range(2)
    ]
    pieces = permuted(jnp.concatenate(pieces, axis=0), v.gather_m[...])
    for rl in range(4):
        for ca in range(2):
            for h in range(2):
                n = (rl * 2 + ca) * 2 + h
                for cb in range(2):
                    at = h * 16 + rl * 4 + ca * 2 + cb
                    v.esend[pl.ds(at, 8, stride=32), :] = pieces[
                        8 * n : 8 * n + 8, 128 * cb : 128 * cb + 128
                    ]

    scatter(v.esend, v.erecv, "e", "e", 32)
    send_sample(1)

    v.spread_m[...] = jnp.where(
        col == 2 * lax.bitwise_and(row, 127) + lax.shift_right_logical(row, 7), F32(1.0), none
    ).astype(BF16)

    v.crecv[1, own8] = v.csend[...]
    for s in range(2):
        v.nrecv[rows_of(i, 16, 128 * s)] = v.nsend[pair_of(i, s)]
        keep_own(v.xsend, v.xrecv, 32, 256 * s)
    keep_own(v.esend, v.erecv, 32)
    for group in loads[4:]:
        for load in group:
            load.wait()

    entry = lax.broadcasted_iota(jnp.int32, (8, 16), 1)
    place = lax.broadcasted_iota(jnp.int32, (8, 16), 0)
    chosen = []
    for x in range(3):
        index = jnp.zeros((8, 16), jnp.int32)
        for cell in range(8):
            if x == 0:
                number = v.rm_s[cell]
                v.table[x, pl.ds(cell, 8, stride=8), 0:27] = v.km_v[number]
            else:
                number = v.rf_s[2 * cell + x - 1]
                v.table[x, pl.ds(cell, 8, stride=8), 0:27] = v.kf_v[number]
            index = jnp.where(place == cell, number, index)
        chosen.append(jnp.where(index == entry, F32(1.0), none).astype(BF16))
    for x in range(3):
        for c in range(8):
            tile = v.table[x, 8 * c : 8 * c + 8]
            for o in range(27):
                v.kern[x, c, o] = jnp.broadcast_to(tile[:, o : o + 1], (8, 128))
        source = (v.nm_v if x == 0 else v.nf_v)[...].reshape(64, 16)
        high = source.astype(BF16)
        rest = source - high.astype(F32)
        mid = rest.astype(BF16)
        least = (rest - mid.astype(F32)).astype(BF16)
        tile = None
        for piece in (high, mid, least):
            term = lax.dot_general(
                chosen[x], piece, (((1,), (1,)), ((), ())), preferred_element_type=F32
            )
            tile = term if tile is None else tile + term
        for c in range(8):
            for j in range(8):
                at = 8 * c + j
                v.noise[x, c, j] = jnp.broadcast_to(tile[:, at : at + 1], (8, 128))

    for n in range(4):
        for ca in range(2):
            for c in range(4):
                at = pl.ds(16 * n + ca, 8, stride=2)
                lanes = pl.ds(128 * c, 128)
                v.star_x[0, :, 2 * n + ca, lanes] = v.bins_v[c, at, :].astype(F32)
                v.star_x[1, :, 2 * n + ca, lanes] = v.data_v[c, at, :]
    for kind in range(2):
        x = v.star_x[kind, i]
        y = permuted(jnp.concatenate([x[:, :256], x[:, 256:]], axis=0), v.gather_m[...])
        for h in range(2):
            for cb in range(2):
                v.star_y[kind, 2 * h + cb] = y[8 * h : 8 * h + 8, 128 * cb : 128 * cb + 128]
        for h in range(2):
            for cb in range(2):
                for ca in range(2):
                    v.star_z[kind, h, pl.ds(2 * ca + cb, 4, stride=4), :] = v.star_y[
                        kind, 2 * h + cb, pl.ds(ca, 4, stride=2), :
                    ]

    arrived(v.crecv.at[1, 0:56], "c")

    @pl.when((i <= 2) | (i >= 5))
    def _():
        arrived(v.crecv.at[0], "cs")

    for side in range(3):
        for a in range(4):
            for s in range(2):
                x = v.crecv[side, pl.ds(4 * s + a, 8, stride=8), :]
                if side == 0:
                    x = jnp.where(k > 0, x, none)
                if side == 2:
                    x = jnp.where(k < na - 1, x, none)
                v.c12[4 * side + a, s] = x
    base = jnp.where(i > 0, 1, 0) + jnp.where(i == nr - 1, 1, 0)
    spacing = F32(1.0 / (4 * nr))
    cell = 4 * lax.broadcasted_iota(jnp.int32, (8, 256), 0)
    cells = [(cell + j).astype(F32) for j in range(4)]

    def parent_inside(u):
        a = 4 * k + low + u
        return (a >= 0) & (a < 4 * na)

    def star(kind, n, q):
        at = 4 * n + q
        return jnp.concatenate(
            [
                jnp.broadcast_to(v.star_z[kind, h, at : at + 1, :], (8, 128))
                for h in range(2)
            ],
            axis=1,
        )

    def spread_out(sums):
        total = lane_shift(sums[1], 1)
        total = total + lane_shift(sums[0], 2)
        return total + lane_shift(sums[2], 0)

    def forward(s):
        for t in range(4):
            x = v.c12[half_up + 2 + t, s]
            for dr in range(3):
                moved = row_shift(x, dr)
                for db in range(3):
                    v.cs[t, 3 * dr + db] = lane_shift(moved, db)
        arrived(v.nrecv.at[0:112], f"n{s}")

        @pl.when((i == 0) | (i == nr - 1))
        def _():
            arrived(v.nside.at[0:64], f"ns{s}")

        for j in range(8):
            for n in range(2):
                v.emx[1 + n, j] = v.nrecv[pl.ds(128 * s + 8 * n + j, 8, stride=16), :]
            x = v.nside[pl.ds(64 * s + j, 8, stride=8), :]
            v.emx[0, j] = x
            v.emx[3, j] = x
        sums = [[None] * 8, [None] * 8]
        for j in range(8):
            x = [v.emx[base + u, j] for u in range(2)]
            for c in range(8):
                weight = v.noise[0, c, j]
                for u in range(2):
                    term = weight * x[u]
                    sums[u][c] = term if j == 0 else sums[u][c] + term
        for o in range(27):
            dr, da, db = o // 9, o // 3 % 3, o % 3
            x = [v.cs[u + da, 3 * dr + db] for u in range(2)]
            for c in range(8):
                weight = v.kern[0, c, o]
                for u in range(2):
                    sums[u][c] = sums[u][c] + weight * x[u]
        for u in range(2):
            for c in range(8):
                lanes = slice(128 * (c % 2), 128 * (c % 2) + 128)
                v.xi[2 * u + c // 2 % 2, c // 4, :, lanes] = jnp.where(
                    parent_inside(u), sums[u][c], none
                )
        v.m4[...] = permuted(v.xi[...].reshape(64, 256), v.spread_m[...]).reshape(4, 2, 8, 256)
        for da in range(3):
            even = v.m4[first + da, 0]
            odd = v.m4[first + da, 1]
            for m, x in enumerate((row_shift(odd, 0), even, odd, row_shift(even, 2))):
                for db in range(3):
                    v.fs[m, 3 * da + db] = lane_shift(x, db)

        arrived(v.xrecv.at[0:224], f"x{s}")
        for r in range(2):
            sums = [None] * 8
            for j in range(8):
                at = 256 * s + (r * 8 + j) * 2
                x = jnp.concatenate(
                    [v.xrecv[pl.ds(at + h, 8, stride=32), :] for h in range(2)], axis=1
                )
                for c in range(8):
                    term = wide(v.noise[1 + r, c, j]) * x
                    sums[c] = term if j == 0 else sums[c] + term
            for o in range(27):
                x = v.fs[r + o // 9, o % 9]
                for c in range(8):
                    sums[c] = sums[c] + wide(v.kern[1 + r, c, o]) * x
            for c in range(8):
                v.dv[2 * r + c // 4, c % 4] = jnp.exp(sums[c])

    def along(s):
        for q in range(4):
            bins = [star(0, n, q) for n in range(4)]
            light = [
                spacing
                * jnp.concatenate(
                    [v.erecv[pl.ds(16 * h + 4 * j + q, 8, stride=32), :] for h in range(2)], axis=1
                )
                for j in range(4)
            ]
            dens = [v.dv[j, q] for j in range(4)]
            layer = [spacing * x for x in dens]
            depth = sums_before((layer[0] + layer[1]) + (layer[2] + layer[3]))
            shine = []
            for j in range(4):
                shine.append(light[j] * jnp.exp(-depth))
                depth = depth + layer[j]
            column = sums_before((shine[0] + shine[1]) + (shine[2] + shine[3]))
            columns = []
            for j in range(4):
                column = column + shine[j]
                columns.append(column)
            weights = [None] * 4
            for n in range(4):
                picked = jnp.where(bins[n] == cells[0], columns[0], none)
                for j in range(1, 4):
                    picked = jnp.where(bins[n] == cells[j], columns[j], picked)
                picked = row_total(picked)
                left = star(1, n, q) - picked
                for h in range(2):
                    at = 4 * n + q
                    v.res_x[h, at : at + 1] = left[0:1, 128 * h : 128 * h + 128]
                for j in range(4):
                    term = jnp.where(bins[n] > cells[j], left * (picked - columns[j]), none)
                    weights[j] = term if n == 0 else weights[j] + term
            for j in range(4):
                v.dv[j, q] = -dens[j] * weights[j]

        pieces = [
            jnp.concatenate([v.res_x[h, pl.ds(cb, 8, stride=2), :] for cb in range(2)], axis=1)
            for h in range(2)
        ]
        spread = permuted(jnp.concatenate(pieces, axis=0), v.spread_m[...])
        for h in range(2):
            for e in range(2):
                at = 32 * s + 8 * (2 * h + e)
                v.rsend[at : at + 8] = spread[8 * h : 8 * h + 8, 128 * e : 128 * e + 128]
        mine = v.rsend.at[32 * s : 32 * s + 32]
        there = rows_of(i, 32, 256 * s)
        for to in (ring_at(1), ring_at(3), ring_at(2), across):
            remote(mine, v.rrecv.at[there], "r", f"r{s}", to, 0).start()
        v.rrecv[there] = mine[...]

    def backward(s):
        for r in range(2):
            grads = [v.dv[2 * r + c // 4, c % 4] for c in range(8)]
            for j in range(8):
                total = weighted([wide(v.noise[1 + r, c, j]) for c in range(8)], grads)
                for h in range(2):
                    at = 256 * s + (2 * j + r) * 2 + h
                    v.gfsend[pl.ds(at, 8, stride=32), :] = total[:, 128 * h : 128 * h + 128]
            for o in range(27):
                total = weighted([wide(v.kern[1 + r, c, o]) for c in range(8)], grads)
                m = r + o // 9
                if r == 1 and m < 3:
                    total = total + v.ws[m, o % 9]
                v.ws[m, o % 9] = total
        scatter(v.gfsend, v.gfrecv, "f", f"f{s}", 32, 256 * s)
        keep_own(v.gfsend, v.gfrecv, 32, 256 * s)

        pieces = []
        for da in range(3):
            moved = [spread_out([v.ws[m, 3 * da + db] for db in range(3)]) for m in range(4)]
            pieces.append(moved[1] + row_shift(moved[3], 0))
            pieces.append(moved[2] + row_shift(moved[0], 2))
        spread = permuted(jnp.concatenate(pieces, axis=0), v.gather_m[...])
        v.h4[...] = jnp.zeros(v.h4.shape, F32)
        for da in range(3):
            keep = parent_inside(lax.shift_right_logical(first + da, 1))
            for cr in range(2):
                n = (2 * da + cr) * 8
                v.h4[first + da, cr] = jnp.where(keep, spread[n : n + 8], none)

        children = []
        for u in range(2):
            children.append([])
            for c in range(8):
                lanes = slice(128 * (c % 2), 128 * (c % 2) + 128)
                children[u].append(v.h4[2 * u + c // 2 % 2, c // 4, :, lanes])
        size = 16 + 8 * s
        for j in range(8):
            weights = [v.noise[0, c, j] for c in range(8)]
            for u in range(2):
                v.hsend[pl.ds(128 * s + 8 * u + j, 8, stride=size), :] = weighted(
                    weights, children[u]
                )
        for dr in range(3):
            for db in range(3):
                sums = [None] * 4
                for da in range(3):
                    o = 9 * dr + 3 * da + db
                    weights = [v.kern[0, c, o] for c in range(8)]
                    for u in range(2):
                        total = weighted(weights, children[u])
                        t = u + da
                        sums[t] = total if sums[t] is None else sums[t] + total
                for t in range(4):
                    v.wq[t, 3 * dr + db] = sums[t]
        v.g12[...] = jnp.zeros(v.g12.shape, F32)
        for t in range(4):
            total = None
            for dr in range(3):
                term = spread_out([v.wq[t, 3 * dr + db] for db in range(3)])
                term = row_shift(term, 2 - dr)
                total = term if total is None else total + term
            v.g12[half_up + 2 + t] = total
        for a in range(4):
            v.hsend[pl.ds(128 + 16 + 4 * s + a, 8, stride=24), :] = v.g12[4 + a]
            for side in range(2):
                outside = (k > 0) if side == 0 else (k < na - 1)
                v.hedge[side, pl.ds(4 * s + a, 8, stride=8), :] = jnp.where(
                    outside, v.g12[8 * side + a], none
                )
        scatter(v.hsend, v.hrecv, "h", f"h{s}", size, 128 * s)
        keep_own(v.hsend, v.hrecv, size, 128 * s)
        for side, dk in ((0, -1), (1, 1)):

            @pl.when(i == 0 if side == 0 else i == nr - 1)
            def _():
                for n in range(nr):
                    at = 128 * s + size * n + 8 * side
                    remote(
                        v.hsend.at[at : at + 8], v.hside.at[side, s], "hs", "hs", n, dk
                    ).start()

    def ring_at(d):
        return (i & 4) + ((i + d) & 3)

    across = i ^ 4

    def pass_on(s):
        arrived(v.rrecv.at[0:128], f"r{s}")
        opposite = ring_at(2)
        for owner, to in ((across, ring_at(1)), (across, ring_at(3)), (opposite, across)):
            block = v.rrecv.at[rows_of(owner, 32, 256 * s)]
            remote(block, block, "r", f"q{s}", to, 0).start()

    for s in range(2):
        forward(s)
        if s == 0:
            arrived(v.erecv.at[0:224], "e")
        along(s)
        backward(s)
    for side, dk in ((0, -1), (1, 1)):

        @pl.when(i <= 2 if side == 0 else i >= 5)
        def _():
            place = i if side == 0 else i - 2
            for n in range(nr):
                remote(
                    v.hedge.at[side, pl.ds(8 * n, 8)], v.gside.at[place], "gs", "gs", n, dk
                ).start()

    pass_on(0)
    pass_on(1)
    for s in range(2):
        arrived(v.rrecv.at[0:96], f"q{s}")
        for c in range(4):
            for n in range(4):
                for ca in range(2):
                    at = 256 * s + 8 * c + 2 * n + ca
                    v.res_v[c, pl.ds((s * 4 + n) * 16 + ca, 8, stride=2), :] = v.rrecv[
                        pl.ds(at, 8, stride=32), :
                    ]
        arrived(v.gfrecv.at[0:224], f"f{s}")
        for j in range(8):
            for r in range(2):
                for h in range(2):
                    at = 256 * s + (2 * j + r) * 2 + h
                    v.gf_v[s, j, r, :, 128 * h : 128 * h + 128] = v.gfrecv[
                        pl.ds(at, 8, stride=32), :
                    ]
    arrived(v.hrecv.at[0:112], "h0")
    arrived(v.hrecv.at[0:168], "h1")
    arrived(v.gside, "gs")
    arrived(v.hside, "hs")
    for s in range(2):

        def owed(owner, u):
            at = 128 * s + (16 + 8 * s) * owner + 8 * u
            return v.hrecv[at : at + 8]

        by_row = [
            owed(1, 0) + owed(2, 0) + owed(0, 1) + v.hside[1, s],
            owed(3, 0) + owed(4, 0) + owed(1, 1) + owed(2, 1),
            owed(5, 0) + owed(6, 0) + owed(3, 1) + owed(4, 1),
            owed(7, 0) + owed(5, 1) + owed(6, 1) + v.hside[0, s],
        ]
        for a in range(4):
            v.gm_x[pl.ds(32 * s + a, 8, stride=4), :] = by_row[a]
        for j in range(8):
            at = 32 * s + 4 * j
            v.gm_v[s, j] = v.gm_x[at : at + 4]
    total = v.gside[0]
    for n in range(1, 6):
        total = total + v.gside[n]
    for owner in range(nr):
        at = 128 + 24 * owner + 16
        total = total + v.hrecv[at : at + 8]
    for s in range(2):
        v.gc_v[s] = total[4 * s : 4 * s + 4]

    sent(v.xsend.at[0:104], "c")
    sent(v.xsend.at[0:256], "n")
    sent(v.xsend.at[0:448], "x")
    sent(v.xsend.at[0:224], "e")
    sent(v.xsend.at[0:448], "r")
    sent(v.xsend.at[0:448], "f")
    sent(v.xsend.at[0:280], "h")

    @pl.when((i <= 2) | (i >= 5))
    def _():
        sent(v.xsend.at[0:64], "gs")

    @pl.when((i == 0) | (i == nr - 1))
    def _():
        sent(v.xsend.at[0:128], "hs")


def hand_out(gc_v, gm_v, gf_v, res_v, gc_o, gm_o, gf_o, res_o, sem):
    outs = [
        pltpu.make_async_copy(gf_v, gf_o, sem.at[0]),
        pltpu.make_async_copy(gm_v, gm_o.at[:, :, 0], sem.at[1]),
        pltpu.make_async_copy(gc_v, gc_o.at[:, 0], sem.at[2]),
    ]
    for c in range(4):
        outs.append(
            pltpu.make_async_copy(
                res_v.at[c].reshape(2, 4, 16, 128),
                res_o.at[:, :, :, pl.ds(128 * c, 128)],
                sem.at[3 + c],
            )
        )
    for out in outs:
        out.start()
    for out in outs:
        out.wait()


def per_device(*args):
    nr, na = lax.axis_size("rad"), lax.axis_size("ang")
    args = list(args)
    for n in (4, 7):
        args[n] = args[n].transpose(1, 2, 0)
    held = [(2, 4, 128), (2, 8, 4, 128), (2, 8, 2, 8, 256), (4, 128, 128)]
    shapes = [(2, 1, 4, 128), (2, 8, 1, 4, 128), (2, 8, 2, 8, 256), (2, 4, 16, 512)]
    results = pl.pallas_call(
        functools.partial(kernel, nr, na),
        out_shape=[pltpu.VMEM(shape, F32) for shape in held],
        in_specs=[ANY] * 12,
        out_specs=[VMEM] * 4,
        scratch_shapes=list(SCRATCH.values()),
        compiler_params=pltpu.CompilerParams(collective_id=0, has_side_effects=True),
    )(*args)
    return pl.pallas_call(
        hand_out,
        out_shape=[jax.ShapeDtypeStruct(shape, F32) for shape in shapes],
        in_specs=[VMEM] * 4,
        out_specs=[ANY] * 4,
        scratch_shapes=[pltpu.SemaphoreType.DMA((7,))],
        compiler_params=pltpu.CompilerParams(vmem_limit_bytes=4 << 20),
    )(*results)


def solution(mesh):
    placed = (
        P(None, "rad", "ang", None),
        P(None, None, "rad", "ang", None),
        P(None, None, "rad", "ang", None),
        P(),
        P(),
        P(),
        P(),
        P(),
        P(),
        P("rad", "ang", None),
        P(None, "ang", None),
        P(None, "ang", None),
    )
    return jax.shard_map(
        per_device,
        mesh=mesh,
        in_specs=placed,
        out_specs=(
            P(None, "rad", "ang", None),
            P(None, None, "rad", "ang", None),
            P(None, None, "rad", "ang", None),
            P(None, None, "ang", None),
        ),
        check_vma=False,
    )
```
